32 devices in a mesh: seq: 8 (over z, x), dp: 4 (over y, core).
Axes of the slice: x: 2, y: 2, z: 4, core: 2. Of those that a mesh axis runs over, the one named last changes fastest.
Arguments:
- inputs: bfloat16 [4, 1024, 8192], P('dp', 'seq'), may hold values from -8 to 8
- adapter_down_weight: bfloat16 [8192, 128], replicated, may hold values from -0.0625 to 0.0625
- adapter_up_weight: bfloat16 [384, 128], replicated, may hold values from -0.3125 to 0.3125
- query: bfloat16 [4, 1024, 128], P('dp', 'seq'), may hold values from -6 to 6
- key: bfloat16 [4, 1024, 128], P('dp', 'seq'), may hold values from -6 to 6
- value: bfloat16 [4, 1024, 128], P('dp', 'seq'), may hold values from -6 to 6
- output_gradient: bfloat16 [4, 1024, 128], P('dp', 'seq'), may hold values from -6 to 6
Outputs:
- query_grad: bfloat16 [4, 1024, 128], P('dp', 'seq')
- key_grad: bfloat16 [4, 1024, 128], P('dp', 'seq')
- value_grad: bfloat16 [4, 1024, 128], P('dp', 'seq')
- down_grad: float32 [8192, 128], P('dp')
- up_grad: float32 [384, 128], P('dp')
The draws below stay inside these ranges and needn't reach their ends.
All inputs are finite; a program needn't handle non-finite values.
Results may differ from the reference program's by a relative error of at most 0.0058.
Values sent between devices are 32-bit elements; how exact they have to be, the bound alone decides.
A program may use at most 64 MiB of HBM per device.

```python
import math
import jax
import jax.numpy as jnp
from jax import lax

MODEL_DIM = 8192
HEAD_SIZE = 128
LOCAL_HEADS = 1
ADAPTER_RANK = 128
TOK_DEV = 128
L = 1024
BATCH = 4


def spiked(result, stream_key, source, target, blocks, factor):
    def block_of(dim):
        return (jnp.arange(result.shape[dim]) // (result.shape[dim] // blocks)).reshape((-1,) + (1,) * (result.ndim - 1 - dim))

    first = jax.random.permutation(stream_key, blocks)[block_of(target)]
    other_side = (block_of(target) + blocks // 2) % blocks
    return jnp.where((block_of(source) == first) | (block_of(source) == other_side), factor * result, result)


def levels(key, extent, cuts, low, top_value):
    def one(axis_at, blocks):
        steps = jax.random.uniform(jax.random.fold_in(jax.random.fold_in(key, 6), axis_at), (blocks,), jnp.float32, low / len(cuts), top_value / len(cuts))
        return jnp.repeat(jnp.exp(steps), extent[axis_at] // blocks).reshape((-1,) + (1,) * (len(extent) - axis_at - 1))

    gain = one(*cuts[0])
    for cut in cuts[1:]:
        gain = gain * one(*cut)
    return gain


def bell_draw(key, dims, spread, limit, shards=(), kind=jnp.bfloat16):
    drawn = spread * jax.random.normal(key, dims, jnp.float32)
    if shards:
        drawn = drawn * levels(key, dims, shards, -0.22, 0.18)
    return jnp.clip(drawn, -limit, limit).astype(kind)


def heavy_noise(own_key, extent, spread, most, cuts, heavy, held_as=jnp.bfloat16):
    values = spread * jax.random.normal(own_key, extent, jnp.float32)
    if cuts:
        values = values * levels(own_key, extent, cuts, -0.22, 0.18)
    return jnp.clip(spiked(values, jax.random.fold_in(own_key, 3), *heavy), -most, most).astype(held_as)


def setup_inputs(seed: int = 0) -> dict:
    arg_keys = jax.random.split(jax.random.key(seed), 8)
    inputs = heavy_noise(arg_keys[0], (BATCH, L, MODEL_DIM), 1.0, 8.0, ((0, 4), (1, 8)), (0, 2, 4, 2.0))
    adapter_down_weight = bell_draw(arg_keys[1], (MODEL_DIM, ADAPTER_RANK), MODEL_DIM ** -0.5, 0.0625)
    adapter_up_weight = bell_draw(arg_keys[2], (3 * LOCAL_HEADS * HEAD_SIZE, ADAPTER_RANK), (3 * LOCAL_HEADS * HEAD_SIZE) ** -0.5, 0.3125)
    query = bell_draw(arg_keys[3], (BATCH, L, LOCAL_HEADS * HEAD_SIZE), 1.0, 6.0, ((0, 4), (1, 8)))
    key = bell_draw(arg_keys[4], (BATCH, L, LOCAL_HEADS * HEAD_SIZE), 1.0, 6.0, ((0, 4), (1, 8)))
    value = bell_draw(arg_keys[5], (BATCH, L, LOCAL_HEADS * HEAD_SIZE), 1.0, 6.0, ((0, 4), (1, 8)))
    output_gradient = bell_draw(arg_keys[6], (BATCH, L, LOCAL_HEADS * HEAD_SIZE), 1.0, 6.0, ((0, 4), (1, 8)))
    return {"inputs": inputs, "adapter_down_weight": adapter_down_weight, "adapter_up_weight": adapter_up_weight, "query": query, "key": key, "value": value, "output_gradient": output_gradient}


def hold(array):
    return lax.optimization_barrier(array.astype(jnp.bfloat16)).astype(jnp.float32)

def head_grads(query, key, value, output_gradient):
    blocks = L // TOK_DEV
    factor = 1.0 / math.sqrt(HEAD_SIZE * L)

    def split(array):
        return array.reshape(blocks, TOK_DEV, LOCAL_HEADS, HEAD_SIZE).astype(jnp.float32)
    queries = split(query)
    keys = split(key)
    values = split(value)
    grads_out = split(output_gradient)
    kv_state = jnp.einsum('nthi,nthj->nhij', keys, values)
    qg_state = jnp.einsum('nthi,nthj->nhij', queries, grads_out)
    zero_state = jnp.zeros((1, LOCAL_HEADS, HEAD_SIZE, HEAD_SIZE), jnp.float32)
    prefix = jnp.concatenate([zero_state, jnp.cumsum(kv_state, axis=0)[:-1]], axis=0)
    suffix = jnp.concatenate([jnp.cumsum(qg_state[::-1], axis=0)[:-1][::-1], zero_state], axis=0)
    prefix = hold(prefix)
    suffix = hold(suffix)
    rows_idx = lax.broadcasted_iota(jnp.int32, (TOK_DEV, TOK_DEV), 0)
    cols_idx = lax.broadcasted_iota(jnp.int32, (TOK_DEV, TOK_DEV), 1)
    causal = rows_idx >= cols_idx
    grad_scores = hold(jnp.where(causal, jnp.einsum('nthj,nshj->nhts', grads_out, values), 0.0))
    scores = hold(jnp.where(causal, jnp.einsum('nthi,nshi->nhts', queries, keys), 0.0))
    query_grad = jnp.einsum('nhts,nshi->nthi', grad_scores, keys) + jnp.einsum('nthj,nhij->nthi', grads_out, prefix)
    key_grad = jnp.einsum('nhts,nthi->nshi', grad_scores, queries) + jnp.einsum('nshj,nhij->nshi', values, suffix)
    value_grad = jnp.einsum('nhts,nthj->nshj', scores, grads_out) + jnp.einsum('nshi,nhij->nshj', keys, suffix)

    def finish(array):
        return (factor * array).reshape(L, LOCAL_HEADS * HEAD_SIZE).astype(jnp.bfloat16)
    return (finish(query_grad), finish(key_grad), finish(value_grad))

def reference(inputs, adapter_down_weight, adapter_up_weight, query, key, value, output_gradient):
    inverse = 1.0 / math.sqrt(BATCH * L)
    contract = (((0,), (0,)), ((), ()))

    def one_row(carry, items):
        input_rows, row_query, row_key, row_value, row_grad = items
        query_grad, key_grad, value_grad = head_grads(row_query, row_key, row_value, row_grad)
        gradient_list = jnp.concatenate([query_grad, key_grad, value_grad], axis=1)
        low_rank_state = jnp.dot(input_rows, adapter_down_weight, preferred_element_type=jnp.float32).astype(jnp.bfloat16)
        low_rank_gradient = jnp.dot(gradient_list, adapter_up_weight, preferred_element_type=jnp.float32).astype(jnp.bfloat16)
        down_sum = carry[0] + lax.dot_general(input_rows, low_rank_gradient, contract, preferred_element_type=jnp.float32)
        up_sum = carry[1] + lax.dot_general(gradient_list, low_rank_state, contract, preferred_element_type=jnp.float32)
        return ((down_sum, up_sum), (query_grad, key_grad, value_grad))
    start = (jnp.zeros((MODEL_DIM, ADAPTER_RANK), jnp.float32), jnp.zeros((3 * LOCAL_HEADS * HEAD_SIZE, ADAPTER_RANK), jnp.float32))
    sums, grads = lax.scan(one_row, start, (inputs, query, key, value, output_gradient))
    return (grads[0], grads[1], grads[2], sums[0] * inverse, sums[1] * inverse)
```

```python
import functools
import math

import jax
import jax.numpy as jnp
from jax import lax
from jax.experimental import pallas as pl
from jax.experimental.pallas import tpu as pltpu
from jax.sharding import PartitionSpec as P

HEAD_SIZE = 128
LOCAL_HEADS = 1


def entering(part, axis, combine, identity, reverse):
    count = lax.axis_size(axis)
    place = lax.axis_index(axis)
    ahead = count - 1 - place if reverse else place
    gathered = lax.all_gather(part, axis)
    state = jnp.zeros_like(part) + jnp.asarray(identity, part.dtype)

    def one(turn, state):
        source = count - 1 - turn if reverse else turn
        return combine(state, lax.dynamic_index_in_dim(gathered, source, 0, False))

    return lax.fori_loop(0, ahead, one, state)


def add_states(earlier, later):
    return earlier + later


def rounded_values(array):
    return array.astype(jnp.bfloat16)


def local(inputs, adapter_down_weight, adapter_up_weight, query, key, value, output_gradient):
    rows = query.shape[1]
    width = query.shape[2]
    seq_count = lax.axis_size("seq")
    dp_count = lax.axis_size("dp")
    length = rows * seq_count
    factor = 1.0 / math.sqrt(HEAD_SIZE * length)
    queries = query.reshape(rows, LOCAL_HEADS, HEAD_SIZE)
    keys = key.reshape(rows, LOCAL_HEADS, HEAD_SIZE)
    values = value.reshape(rows, LOCAL_HEADS, HEAD_SIZE)
    grads_out = output_gradient.reshape(rows, LOCAL_HEADS, HEAD_SIZE)
    kv_state = jnp.einsum("thi,thj->hij", keys, values, preferred_element_type=jnp.float32)
    qg_state = jnp.einsum("thi,thj->hij", queries, grads_out, preferred_element_type=jnp.float32)
    zeros = jnp.zeros_like(kv_state)
    prefix = entering(kv_state, "seq", add_states, zeros, False)
    suffix = entering(qg_state, "seq", add_states, zeros, True)
    prefix = rounded_values(prefix)
    suffix = rounded_values(suffix)
    rows_idx = lax.broadcasted_iota(jnp.int32, (rows, rows), 0)
    cols_idx = lax.broadcasted_iota(jnp.int32, (rows, rows), 1)
    causal = rows_idx >= cols_idx
    grad_scores = rounded_values(
        jnp.where(
            causal,
            jnp.einsum("thj,shj->hts", grads_out, values, preferred_element_type=jnp.float32),
            0.0,
        )
    )
    scores = rounded_values(
        jnp.where(
            causal,
            jnp.einsum("thi,shi->hts", queries, keys, preferred_element_type=jnp.float32),
            0.0,
        )
    )
    query_grad = jnp.einsum(
        "hts,shi->thi", grad_scores, keys, preferred_element_type=jnp.float32
    ) + jnp.einsum("thj,hij->thi", grads_out, prefix, preferred_element_type=jnp.float32)
    key_grad = jnp.einsum(
        "hts,thi->shi", grad_scores, queries, preferred_element_type=jnp.float32
    ) + jnp.einsum("shj,hij->shi", values, suffix, preferred_element_type=jnp.float32)
    value_grad = jnp.einsum(
        "hts,thj->shj", scores, grads_out, preferred_element_type=jnp.float32
    ) + jnp.einsum("shi,hij->shj", keys, suffix, preferred_element_type=jnp.float32)
    query_grad = rounded_values(factor * query_grad).reshape(rows, width)
    key_grad = rounded_values(factor * key_grad).reshape(rows, width)
    value_grad = rounded_values(factor * value_grad).reshape(rows, width)
    flattened = inputs.reshape(rows, inputs.shape[2])
    gradient_list = jnp.concatenate([query_grad, key_grad, value_grad], axis=1)
    low_rank_state = rounded_values(
        jnp.dot(flattened, adapter_down_weight, preferred_element_type=jnp.float32)
    )
    low_rank_gradient = rounded_values(
        jnp.dot(gradient_list, adapter_up_weight, preferred_element_type=jnp.float32)
    )
    inverse = 1.0 / math.sqrt(length * dp_count)
    contract = (((0,), (0,)), ((), ()))
    down_part = lax.psum_scatter(
        lax.dot_general(flattened, low_rank_gradient, contract, preferred_element_type=jnp.float32)
        * inverse,
        "dp",
        scatter_dimension=0,
        tiled=True,
    )
    up_term = (
        lax.dot_general(gradient_list, low_rank_state, contract, preferred_element_type=jnp.float32)
        * inverse
    )
    up_part = lax.psum_scatter(up_term, "dp", scatter_dimension=0, tiled=True)
    down_grad, up_grad = lax.psum((down_part, up_part), "seq")
    return (
        query_grad.reshape(1, rows, width),
        key_grad.reshape(1, rows, width),
        value_grad.reshape(1, rows, width),
        down_grad,
        up_grad,
    )


MESH = pl.DeviceIdType.MESH
CORES = 2
LINE = 4
KINDS = 8
Y, X, ZI, ZM, ZF, ZO, B, F = range(KINDS)
ROLES = ("outer", "inner")
PIECES = 16
UP_AT = 8
X_FIRST = (0, 1, 2, 3)
RELAYED = (2, 2, 2, 2, 2, 2, 2, 1, 1, 1, 1, 1, 1, 0, 3, 3, 3)
RATE, HOP, MORE = 92.0, 1.75, 0.75
DEEP_Y, DEEP_X = 2.0, 1.0
COST = {"y_send": 0.17, "x_send": 0.18, "x_first": 0.32}


def cut(shard, ushard):
    size = shard // PIECES
    spans = [(i * size, size) for i in range(PIECES)]
    spans.insert(UP_AT, (shard, ushard))
    return [(off, n, i in X_FIRST, RELAYED[i]) for i, (off, n) in enumerate(spans)]


def landing(pieces):
    slots = {}
    for i, (_, _, _, mode) in enumerate(pieces):
        for kind in (Y, X, ZI, ZM):
            slots[kind, i] = len(slots)
        if mode in (0, 2):
            slots[ZO, i] = slots[ZI, i]
        if mode == 1:
            slots[B, i] = len(slots)
        if mode == 2:
            slots[B, i] = slots[ZM, i]
        if mode == 3:
            slots[ZF, i] = len(slots)
    return slots


def plan(pieces):
    free, links, arrive = {}, {}, {}
    out = {role: [] for role in ROLES}
    todo = {role: [] for role in ROLES}
    starts = {role: {"y_send": [], "x_first": []} for role in ROLES}
    for i, (_, _, first_x, mode) in enumerate(pieces):
        landed = Y if first_x else X
        for role in ROLES:
            starts[role]["x_first" if first_x else "y_send"].append(i)
            todo[role].append(("y_second", i, (X,)) if first_x else ("x_send", i, (Y,)))
        todo["outer"].append(("z_in", i, (landed,)))
        if mode == 3:
            todo["inner"] += [("z_own", i, (landed,)), ("z_out", i, (ZI, ZM, ZF))]
        else:
            todo["inner"] += [("z_mid", i, (landed, ZI)), ("z_out", i, (ZM,))]
        if mode in (0, 2):
            todo["outer"].append(("relay", i, (ZO,)))
        if mode in (1, 2):
            todo["inner" if mode == 1 else "outer"].append(("forward", i, (B,)))

    def move(role, link, rows, now, to, kind, i, then=None):
        begin = max(now, links.get((role, link), 0.0))
        done = begin + rows / RATE
        links[role, link] = done
        if then:
            begin = max(begin + MORE, links.get(then, 0.0))
            done = max(begin + rows / RATE, done + MORE)
            links[then] = done
        arrive[to, kind, i] = max(done + HOP, arrive.get((to, kind, i), 0.0))

    def carry(role, op, i, now):
        _, n, first_x, mode = pieces[i]
        h = n // 2
        if op == "y_send":
            move(role, Y, n, now, role, Y, i)
        elif op == "x_send":
            move(role, X, h, now, role, X, i)
        elif op == "x_first":
            move(role, X, n, now, role, X, i)
        elif op == "y_second":
            move(role, Y, h, now, role, Y, i)
        elif op == "z_in":
            move(role, ZI, h, now, "inner", ZI, i)
            if mode == 3:
                move(role, ZI, h, now, "inner", ZF, i, ("inner", ZM))
        elif op in ("z_mid", "z_own"):
            move(role, ZM, h, now, role, ZM, i)
        elif op == "z_out":
            if mode == 3:
                move(role, X, h, now, "outer", F, i, (role, ZO))
            if mode != 2:
                move(role, X, h, now, role, B, i)
            move(role, ZO, h, now, "outer", ZO, i)
        elif op == "relay":
            move(role, X, h, now, role, B, i)
        elif op == "forward":
            to = "outer" if role == "inner" else "inner"
            move(role, ZO if role == "inner" else ZI, h, now, to, F, i)

    while True:
        options = []
        for role in ROLES:
            clock = free.get(role, 0.0)
            for op, i, kinds in todo[role]:
                if all((role, kind, i) in arrive for kind in kinds):
                    ready = max(arrive[role, kind, i] for kind in kinds)
                    options.append((max(clock, ready), ready, role, op, i, kinds))
            for op, link, deep in (("y_send", Y, DEEP_Y), ("x_first", X, DEEP_X)):
                if starts[role][op]:
                    ready = links.get((role, link), 0.0) - deep
                    options.append((max(clock, ready), ready, role, op, starts[role][op][0], None))
        if not options:
            return out
        now, _, role, op, i, kinds = min(options, key=lambda option: option[:2])
        if kinds is None:
            starts[role][op].pop(0)
        else:
            todo[role].remove((op, i, kinds))
        out[role].append((now, op, i))
        now += COST.get(op, 0.03)
        free[role] = now
        carry(role, op, i, now)
        out["end"] = max(arrive.values())
        out["links"] = links


def fits(seq_count, dp_count):
    return dp_count == 2 * CORES and seq_count == 2 * LINE


def dot(a, b, da, db):
    return lax.dot_general(a, b, (((da,), (db,)), ((), ())), preferred_element_type=jnp.float32)


def fused_kernel(
    depth, factor, inverse,
    x_hbm, w_hbm, u_ref, q_ref, k_ref, v_ref, g_ref,
    qo_ref, ko_ref, vo_ref, down_ref, up_ref,
    x_ref, w_ref, xs_ref, xr_ref, xt_ref,
    st_ref, pair_ref, kvr_ref, qgr_ref, ox_ref, sxs_ref, sxr_ref,
    ls_ref, lr_ref, ups_ref, upr_ref, fg_ref,
    ys_ref, yr_ref, acc_ref, xrs_ref, zs_ref, zr_ref, zm_ref, zf_ref,
    load_sem, core_s, core_r, kv_s, kv_r, qg_s, qg_r, sx_s, sx_r,
    send_s, hop_r,
):
    seq = lax.axis_index("seq")
    dp = lax.axis_index("dp")
    z, x = seq // 2, seq % 2
    y, c = dp // CORES, dp % CORES
    mate = {"seq": seq, "dp": y * CORES + (1 - c)}
    across = {"seq": seq, "dp": (1 - y) * CORES + c}
    beside = {"seq": z * 2 + (1 - x), "dp": dp}

    near = jnp.where(z % 3 == 0, z + 1 - 2 * (z // 3), 3 * (z // 2))
    diagonal = {"seq": near * 2 + (1 - x), "dp": dp}

    def along(other):
        return {"seq": other * 2 + x, "dp": dp}

    load_x = pltpu.make_async_copy(x_hbm, x_ref, load_sem.at[0])
    load_w = pltpu.make_async_copy(w_hbm, w_ref, load_sem.at[1])
    load_x.start()
    load_w.start()

    barrier = pltpu.get_barrier_semaphore()
    friends = [mate, across, beside, diagonal] + [along(lax.rem(z + d, depth)) for d in range(1, depth)]
    for friend in friends:
        pl.semaphore_signal(barrier, inc=1, device_id=friend, device_id_type=MESH)

    rows = q_ref.shape[0]
    shard = down_ref.shape[0]
    ushard = up_ref.shape[0]
    width = q_ref.shape[1]
    q, k, v, g = q_ref[...], k_ref[...], v_ref[...], g_ref[...]
    st_ref[0] = dot(k, v, 0, 0)
    st_ref[1] = dot(q, g, 0, 0)
    pl.semaphore_wait(barrier, len(friends))

    def remote(src, dst, ssem, rsem, where):
        return pltpu.make_async_remote_copy(
            src_ref=src, dst_ref=dst, send_sem=ssem, recv_sem=rsem, device_id=where, device_id_type=MESH
        )

    lead = width // 2
    first, second = slice(0, lead), slice(lead, width)
    other = remote(st_ref.at[:, second, :], ox_ref, sx_s.at[1], sx_r.at[1], beside)
    other.start()

    def scan(source, part, at):
        ups, downs = [], []
        for d in range(1, depth):
            slot = at * (depth - 1) + d - 1
            ups.append(remote(source.at[0, part, :], kvr_ref.at[d - 1, part, :], kv_s.at[slot], kv_r.at[slot], along(lax.rem(z + d, depth))))
            downs.append(remote(source.at[1, part, :], qgr_ref.at[d - 1, part, :], qg_s.at[slot], qg_r.at[slot], along(lax.rem(z - d + depth, depth))))
        for d in range(1, depth):
            pl.when(z + d < depth)(ups[d - 1].start)
            pl.when(z >= d)(downs[d - 1].start)
        return ups, downs

    def collect(ups, downs, part):
        sxs_ref[:, part, :] = jnp.zeros((2, lead, width), jnp.float32)
        for d in range(1, depth):
            @pl.when(z >= d)
            def _(d=d):
                ups[d - 1].wait_recv()
                sxs_ref[0, part, :] += kvr_ref[d - 1, part, :]

            @pl.when(z + d < depth)
            def _(d=d):
                downs[d - 1].wait_recv()
                sxs_ref[1, part, :] += qgr_ref[d - 1, part, :]

    scan_a = scan(st_ref, first, 0)

    load_x.wait()
    core_copies = []
    for part in range(2):
        cols = pl.ds(pl.multiple_of((part * CORES + 1 - c) * shard, 128), shard)
        xs_ref[part] = x_ref[:, cols].astype(jnp.float32)
        copy = remote(xs_ref.at[part], xr_ref.at[part], core_s.at[part], core_r.at[part], mate)
        copy.start()
        core_copies.append(copy)

    other.wait_recv()
    pair_ref[:, second, :] = st_ref[:, second, :] + ox_ref[...]
    scan_b = scan(pair_ref, second, 1)

    r_idx = lax.broadcasted_iota(jnp.int32, (rows, rows), 0)
    c_idx = lax.broadcasted_iota(jnp.int32, (rows, rows), 1)
    causal = r_idx >= c_idx
    gs = jnp.where(causal, dot(g, v, 1, 1), 0.0).astype(jnp.bfloat16)
    sc = jnp.where(causal, dot(q, k, 1, 1), 0.0).astype(jnp.bfloat16)
    q_in = dot(gs, k, 1, 0)
    k_in = dot(gs, q, 0, 0)
    v_in = dot(sc, g, 0, 0)

    for part in range(2):
        cols = pl.ds(pl.multiple_of((part * CORES + c) * shard, 128), shard)
        xt_ref[part, :, 0:rows] = x_ref[:, cols].T

    load_w.wait()
    low = jnp.dot(x_ref[...], w_ref[...], preferred_element_type=jnp.float32).astype(jnp.bfloat16)

    collect(*scan_a, first)
    lead_sum = sxs_ref[:, first, :]

    @pl.when(x == 0)
    def _():
        sxs_ref[0, first, :] += st_ref[0, first, :]

    @pl.when(x == 1)
    def _():
        sxs_ref[1, first, :] += st_ref[1, first, :]

    swap = remote(sxs_ref.at[:, first, :], sxr_ref, sx_s.at[0], sx_r.at[0], beside)
    swap.start()

    for part in range(2):
        core_copies[part].wait_recv()
        xt_ref[part, :, rows:] = xr_ref[part].astype(jnp.bfloat16).T

    collect(*scan_b, second)

    @pl.when(x == 1)
    def _():
        sxs_ref[0, second, :] += ox_ref[0]

    @pl.when(x == 0)
    def _():
        sxs_ref[1, second, :] += ox_ref[1]

    swap.wait_recv()
    states = jnp.concatenate([lead_sum + sxr_ref[...], sxs_ref[:, second, :]], axis=1).astype(jnp.bfloat16)
    prefix, suffix = states[0], states[1]
    q_grad = (factor * (q_in + dot(g, prefix, 1, 1))).astype(jnp.bfloat16)
    k_grad = (factor * (k_in + dot(v, suffix, 1, 1))).astype(jnp.bfloat16)
    v_grad = (factor * (v_in + dot(k, suffix, 1, 0))).astype(jnp.bfloat16)
    fg = jnp.concatenate([q_grad, k_grad, v_grad], axis=1)
    low_grad = dot(fg, u_ref[...], 1, 0).astype(jnp.bfloat16)
    ls_ref[...] = low_grad.astype(jnp.float32)
    low_copy = remote(ls_ref, lr_ref, core_s.at[2], core_r.at[2], mate)
    low_copy.start()
    qo_ref[...] = q_grad
    ko_ref[...] = k_grad
    vo_ref[...] = v_grad

    low_copy.wait_recv()
    both = jnp.concatenate([low_grad, lr_ref[...].astype(jnp.bfloat16)], axis=0)

    pieces = cut(shard, ushard)
    count = len(pieces)
    outer = (z == 0) | (z == depth - 1)
    inner = jnp.logical_not(outer)
    mid = jnp.where(z < depth // 2, depth // 2 - 1, depth // 2)
    end = jnp.where(z < depth // 2, 0, depth - 1)
    inward, outward, opposite = along(mid), along(end), along(depth - 1 - z)
    further = along(depth - 1 - mid)
    corner = {"seq": end * 2 + (1 - x), "dp": dp}
    slots = landing(pieces)
    sent = {}

    def send(role, kind, i, src, dst, where):
        rows = src.shape[0]
        sent[kind] = sent.get(kind, 0) + rows
        at = slots.get((kind, i), len(slots))
        remote(src, dst, send_s.at[kind], hop_r.at[at], where).start()

    def arrived(kind, i, like):
        remote(like, like, send_s.at[kind], hop_r.at[slots[kind, i]], mate).wait_recv()

    def partial(i, part):
        off, n = pieces[i][:2]
        if off < shard:
            return jnp.dot(xt_ref[part, off : off + n, :], both, preferred_element_type=jnp.float32)
        mine = pl.ds(pl.multiple_of((part * CORES + c) * ushard, 8), ushard)
        return fg_ref[mine, :] + upr_ref[part]

    def half(i, which):
        off, n = pieces[i][:2]
        return pl.ds(pl.multiple_of(off + which * (n // 2), 8), n // 2)

    def short(i):
        off, n = pieces[i][:2]
        return slice(off // 2, off // 2 + n // 2)

    def place(i, which):
        off, n = pieces[i][:2]
        ref, base = (down_ref, off) if off < shard else (up_ref, 0)
        return ref.at[pl.ds(pl.multiple_of(base + which * (n // 2), 8), n // 2), :]

    def perform(role, op, i):
        off, n, first_x, mode = pieces[i]
        h = n // 2
        whole, low_half, high_half = slice(off, off + n), slice(off, off + h), slice(off + h, off + n)
        small = short(i)
        landed = Y if first_x else X
        if op == "y_send":
            if off >= shard:
                up_copy.wait_recv()
            ys_ref[whole, :] = partial(i, 1 - y)
            send(role, Y, i, ys_ref.at[whole, :], yr_ref.at[whole, :], across)
        elif op == "x_send":
            own = partial(i, y)
            arrived(Y, i, yr_ref.at[whole, :])
            acc_ref[whole, :] = own + yr_ref[whole, :]
            send(role, X, i, acc_ref.at[half(i, 1 - x), :], xrs_ref.at[small, :], beside)
        elif op == "x_first":
            ys_ref[whole, :] = partial(i, 1 - y)
            send(role, X, i, ys_ref.at[half(i, 1 - x), :], yr_ref.at[high_half, :], beside)
            acc_ref[whole, :] = partial(i, y)
            send(role, X, i, acc_ref.at[half(i, 1 - x), :], yr_ref.at[low_half, :], beside)
        elif op == "y_second":
            arrived(X, i, yr_ref.at[whole, :])
            ys_ref[half(i, x), :] += yr_ref[high_half, :]
            send(role, Y, i, ys_ref.at[half(i, x), :], xrs_ref.at[small, :], across)
            acc_ref[half(i, x), :] += yr_ref[low_half, :]
        elif op == "z_in":
            arrived(landed, i, xrs_ref.at[small, :])
            zs_ref[small, :] = acc_ref[half(i, x), :] + xrs_ref[small, :]
            send(role, ZI, i, zs_ref.at[small, :], zr_ref.at[small, :], inward)
            if mode == 3:
                send(role, ZF, i, zs_ref.at[small, :], zf_ref.at[small, :], further)
        elif op == "z_own":
            arrived(landed, i, xrs_ref.at[small, :])
            zs_ref[small, :] = acc_ref[half(i, x), :] + xrs_ref[small, :]
            send(role, ZM, i, zs_ref.at[small, :], zm_ref.at[small, :], opposite)
        elif op == "z_mid":
            arrived(landed, i, xrs_ref.at[small, :])
            own = acc_ref[half(i, x), :] + xrs_ref[small, :]
            arrived(ZI, i, zr_ref.at[small, :])
            zs_ref[small, :] = own + zr_ref[small, :]
            send(role, ZM, i, zs_ref.at[small, :], zm_ref.at[small, :], opposite)
        elif op == "z_out":
            own = zs_ref[small, :]
            if mode == 3:
                arrived(ZI, i, zr_ref.at[small, :])
                own = own + zr_ref[small, :]
            arrived(ZM, i, zm_ref.at[small, :])
            own = own + zm_ref[small, :]
            if mode == 3:
                arrived(ZF, i, zf_ref.at[small, :])
                own = own + zf_ref[small, :]
            spot = place(i, x)
            spot[...] = own * inverse
            if mode == 3:
                send(role, F, i, spot, spot, corner)
            if mode in (0, 1, 3):
                send(role, B, i, spot, spot, beside)
            send(role, ZO, i, spot, spot, outward)
        elif op == "relay":
            spot = place(i, x)
            arrived(ZO, i, spot)
            send(role, B, i, spot, spot, beside)
        elif op == "forward":
            spot = place(i, 1 - x)
            arrived(B, i, spot)
            send(role, F, i, spot, spot, outward if role == "inner" else inward)

    up_all = dot(fg, low, 0, 0)
    fg_ref[...] = up_all
    for part in range(2):
        rng = pl.ds(pl.multiple_of((part * CORES + 1 - c) * ushard, 8), ushard)
        ups_ref[part] = fg_ref[rng, :]
    up_copy = remote(ups_ref, upr_ref, core_s.at[3], core_r.at[3], mate)
    up_copy.start()

    for role, here in (("outer", outer), ("inner", inner)):
        @pl.when(here)
        def _(role=role):
            sent.clear()
            for _, op, i in plan(pieces)[role]:
                perform(role, op, i)
            late = sum(n // 2 for _, n, _, mode in pieces if mode in (1, 3) and role == "outer") + sum(
                n // 2 for _, n, _, mode in pieces if (role, mode) not in (("outer", 2), ("inner", 1)))
            like = ys_ref.at[0:late, :]
            remote(like, like, send_s.at[0], hop_r.at[len(slots)], mate).wait_recv()
            for kind, rows in sent.items():
                like = ys_ref.at[0:rows, :]
                remote(like, like, send_s.at[kind], hop_r.at[len(slots)], mate).wait_send()

    for ups, downs in (scan_a, scan_b):
        for d in range(1, depth):
            pl.when(z + d < depth)(ups[d - 1].wait_send)
            pl.when(z >= d)(downs[d - 1].wait_send)
    for copy in core_copies + [other, swap, low_copy, up_copy]:
        copy.wait_send()


def write_out(*refs):
    copies = [pltpu.make_async_copy(refs[i], refs[5 + i], refs[10].at[i]) for i in range(5)]
    for copy in copies:
        copy.start()
    for copy in copies:
        copy.wait()


def fast(inputs, adapter_down_weight, adapter_up_weight, query, key, value, output_gradient):
    rows, width = query.shape[1:]
    model = inputs.shape[2]
    rank = adapter_down_weight.shape[1]
    features = adapter_up_weight.shape[0]
    seq_count = lax.axis_size("seq")
    dp_count = lax.axis_size("dp")
    length = rows * seq_count
    factor = 1.0 / math.sqrt(HEAD_SIZE * length)
    inverse = 1.0 / math.sqrt(length * dp_count)
    depth = seq_count // 2
    shard, ushard = model // dp_count, features // dp_count
    total = shard + ushard
    f32, bf16 = jnp.float32, jnp.bfloat16
    dma = pltpu.SemaphoreType.DMA
    vmem = pl.BlockSpec(memory_space=pltpu.VMEM)
    hbm = pl.BlockSpec(memory_space=pl.ANY)
    shapes = [jax.ShapeDtypeStruct((rows, width), bf16)] * 3 + [
        jax.ShapeDtypeStruct((shard, rank), f32),
        jax.ShapeDtypeStruct((ushard, rank), f32),
    ]
    out = pl.pallas_call(
        functools.partial(fused_kernel, depth, factor, inverse),
        out_shape=[pltpu.VMEM(part.shape, part.dtype) for part in shapes],
        in_specs=[hbm, hbm] + [vmem] * 5,
        out_specs=[vmem] * 5,
        scratch_shapes=[
            pltpu.VMEM((rows, model), bf16),
            pltpu.VMEM((model, rank), bf16),
            pltpu.VMEM((2, rows, shard), f32),
            pltpu.VMEM((2, rows, shard), f32),
            pltpu.VMEM((2, shard, 2 * rows), bf16),
            pltpu.VMEM((2, width, width), f32),
            pltpu.VMEM((2, width, width), f32),
            pltpu.VMEM((depth - 1, width, width), f32),
            pltpu.VMEM((depth - 1, width, width), f32),
            pltpu.VMEM((2, width // 2, width), f32),
            pltpu.VMEM((2, width, width), f32),
            pltpu.VMEM((2, width // 2, width), f32),
            pltpu.VMEM((rows, rank), f32),
            pltpu.VMEM((rows, rank), f32),
            pltpu.VMEM((2, ushard, rank), f32),
            pltpu.VMEM((2, ushard, rank), f32),
            pltpu.VMEM((features, rank), f32),
            pltpu.VMEM((total, rank), f32),
            pltpu.VMEM((total, rank), f32),
            pltpu.VMEM((total, rank), f32),
            pltpu.VMEM((total // 2, rank), f32),
            pltpu.VMEM((total // 2, rank), f32),
            pltpu.VMEM((total // 2, rank), f32),
            pltpu.VMEM((total // 2, rank), f32),
            pltpu.VMEM((total // 2, rank), f32),
            dma((2,)), dma((4,)), dma((4,)),
            dma((2 * depth - 2,)), dma((2 * depth - 2,)), dma((2 * depth - 2,)), dma((2 * depth - 2,)),
            dma((2,)), dma((2,)),
            dma((KINDS,)), dma((len(landing(cut(shard, ushard))) + 1,)),
        ],
        compiler_params=pltpu.CompilerParams(
            collective_id=0, has_side_effects=True
        ),
    )(
        inputs.reshape(rows, model), adapter_down_weight, adapter_up_weight,
        query.reshape(rows, width), key.reshape(rows, width),
        value.reshape(rows, width), output_gradient.reshape(rows, width),
    )
    out = pl.pallas_call(
        write_out,
        out_shape=shapes,
        in_specs=[vmem] * 5,
        out_specs=[hbm] * 5,
        scratch_shapes=[dma((5,))],
    )(*[pltpu.with_memory_space_constraint(part, pltpu.VMEM) for part in out])
    return tuple(part.reshape(1, rows, width) for part in out[:3]) + tuple(out[3:])


def solution(mesh):
    fused = fits(mesh.shape["seq"], mesh.shape["dp"])
    chosen = fast if fused else local
    return jax.shard_map(
        chosen,
        mesh=mesh,
        in_specs=(
            P("dp", "seq", None),
            P(),
            P(),
            P("dp", "seq", None),
            P("dp", "seq", None),
            P("dp", "seq", None),
            P("dp", "seq", None),
        ),
        out_specs=(
            P("dp", "seq", None),
            P("dp", "seq", None),
            P("dp", "seq", None),
            P("dp", None),
            P("dp", None),
        ),
        check_vma=False,
    )
```

```python
import functools
import math

import jax
import jax.numpy as jnp
from jax import lax
from jax.experimental import pallas as pl
from jax.experimental.pallas import tpu as pltpu
from jax.sharding import PartitionSpec as P

HEAD_SIZE = 128
LOCAL_HEADS = 1


def entering(part, axis, combine, identity, reverse):
    count = lax.axis_size(axis)
    place = lax.axis_index(axis)
    ahead = count - 1 - place if reverse else place
    gathered = lax.all_gather(part, axis)
    state = jnp.zeros_like(part) + jnp.asarray(identity, part.dtype)

    def one(turn, state):
        source = count - 1 - turn if reverse else turn
        return combine(state, lax.dynamic_index_in_dim(gathered, source, 0, False))

    return lax.fori_loop(0, ahead, one, state)


def add_states(earlier, later):
    return earlier + later


def rounded_values(array):
    return array.astype(jnp.bfloat16)


def local(inputs, adapter_down_weight, adapter_up_weight, query, key, value, output_gradient):
    rows = query.shape[1]
    width = query.shape[2]
    seq_count = lax.axis_size("seq")
    dp_count = lax.axis_size("dp")
    length = rows * seq_count
    factor = 1.0 / math.sqrt(HEAD_SIZE * length)
    queries = query.reshape(rows, LOCAL_HEADS, HEAD_SIZE)
    keys = key.reshape(rows, LOCAL_HEADS, HEAD_SIZE)
    values = value.reshape(rows, LOCAL_HEADS, HEAD_SIZE)
    grads_out = output_gradient.reshape(rows, LOCAL_HEADS, HEAD_SIZE)
    kv_state = jnp.einsum("thi,thj->hij", keys, values, preferred_element_type=jnp.float32)
    qg_state = jnp.einsum("thi,thj->hij", queries, grads_out, preferred_element_type=jnp.float32)
    zeros = jnp.zeros_like(kv_state)
    prefix = entering(kv_state, "seq", add_states, zeros, False)
    suffix = entering(qg_state, "seq", add_states, zeros, True)
    prefix = rounded_values(prefix)
    suffix = rounded_values(suffix)
    rows_idx = lax.broadcasted_iota(jnp.int32, (rows, rows), 0)
    cols_idx = lax.broadcasted_iota(jnp.int32, (rows, rows), 1)
    causal = rows_idx >= cols_idx
    grad_scores = rounded_values(
        jnp.where(
            causal,
            jnp.einsum("thj,shj->hts", grads_out, values, preferred_element_type=jnp.float32),
            0.0,
        )
    )
    scores = rounded_values(
        jnp.where(
            causal,
            jnp.einsum("thi,shi->hts", queries, keys, preferred_element_type=jnp.float32),
            0.0,
        )
    )
    query_grad = jnp.einsum(
        "hts,shi->thi", grad_scores, keys, preferred_element_type=jnp.float32
    ) + jnp.einsum("thj,hij->thi", grads_out, prefix, preferred_element_type=jnp.float32)
    key_grad = jnp.einsum(
        "hts,thi->shi", grad_scores, queries, preferred_element_type=jnp.float32
    ) + jnp.einsum("shj,hij->shi", values, suffix, preferred_element_type=jnp.float32)
    value_grad = jnp.einsum(
        "hts,thj->shj", scores, grads_out, preferred_element_type=jnp.float32
    ) + jnp.einsum("shi,hij->shj", keys, suffix, preferred_element_type=jnp.float32)
    query_grad = rounded_values(factor * query_grad).reshape(rows, width)
    key_grad = rounded_values(factor * key_grad).reshape(rows, width)
    value_grad = rounded_values(factor * value_grad).reshape(rows, width)
    flattened = inputs.reshape(rows, inputs.shape[2])
    gradient_list = jnp.concatenate([query_grad, key_grad, value_grad], axis=1)
    low_rank_state = rounded_values(
        jnp.dot(flattened, adapter_down_weight, preferred_element_type=jnp.float32)
    )
    low_rank_gradient = rounded_values(
        jnp.dot(gradient_list, adapter_up_weight, preferred_element_type=jnp.float32)
    )
    inverse = 1.0 / math.sqrt(length * dp_count)
    contract = (((0,), (0,)), ((), ()))
    down_part = lax.psum_scatter(
        lax.dot_general(flattened, low_rank_gradient, contract, preferred_element_type=jnp.float32)
        * inverse,
        "dp",
        scatter_dimension=0,
        tiled=True,
    )
    up_term = (
        lax.dot_general(gradient_list, low_rank_state, contract, preferred_element_type=jnp.float32)
        * inverse
    )
    up_part = lax.psum_scatter(up_term, "dp", scatter_dimension=0, tiled=True)
    down_grad, up_grad = lax.psum((down_part, up_part), "seq")
    return (
        query_grad.reshape(1, rows, width),
        key_grad.reshape(1, rows, width),
        value_grad.reshape(1, rows, width),
        down_grad,
        up_grad,
    )


MESH = pl.DeviceIdType.MESH
CORES = 2
LINE = 4
KINDS = 9
Y, X, ZI, ZM, ZF, ZO, B, F, ZL = range(KINDS)
ROLES = ("outer", "inner")
CUTS = (
    (14, 1, 2), (14, 1, 0), (16, 0, 0), (7, 1, 2), (5, 1, 0), (2, 0, 2), (12, 0, 2), (11, 0, 2),
    (6, 0, 0), (7, 0, 2), (6, 1, 0), (4, 0, 1), (6, 1, 1), (7, 1, 0), (2, 1, 1), (2, 1, 1),
    (0, 0, 0), (5, 1, 3), (2, 0, 0),
)
RATE, HOP, MORE, EARLY = 92.0, 1.75, 0.75, 4.3
DEEP = (2.5, 0.3, 1.0)
COST = {"y_send": 0.17, "x_send": 0.18, "x_first": 0.32, "z_first": 0.32, "z_join": 0.34, "p_send": 0.25}


def cut(shard, ushard):
    unit = shard // sum(parts for parts, _, _ in CUTS)
    places, off = {}, 0
    for i in sorted(range(len(CUTS)), key=lambda i: CUTS[i][1] != 2):
        places[i] = off
        off += CUTS[i][0] * unit
    return [
        (places[i], parts * unit, color, mode) if parts else (shard, ushard, color, mode)
        for i, (parts, color, mode) in enumerate(CUTS)
    ]


def fetched(pieces):
    return sum(n for _, n, color, _ in pieces if color == 2)


def working(color):
    return {3: ("inner",), 5: ("inner",), 4: ("outer",), 6: ("outer",)}.get(color, ROLES)


def direct(color, mode):
    return mode == 3 and color < 3


def landing(pieces):
    slots = {}
    for i, (_, _, color, mode) in enumerate(pieces):
        for kind in (Y, X, ZI, ZM):
            slots[kind, i] = len(slots)
        if color >= 3:
            slots[ZL, i] = len(slots)
        if mode in (0, 2):
            slots[ZO, i] = slots[ZI, i]
        if mode == 1:
            slots[B, i] = len(slots)
        if mode == 2:
            slots[B, i] = slots[ZM, i]
        if direct(color, mode):
            slots[ZF, i] = len(slots)
    return slots


def plan(pieces):
    free, links, arrive = {}, {}, {}
    out = {role: [] for role in ROLES}
    todo = {role: [] for role in ROLES}
    starts = {role: {"y_send": [], "x_first": [], "z_first": []} for role in ROLES}
    early = any(color == 2 for _, _, color, _ in pieces)
    for i, (_, _, color, mode) in enumerate(pieces):
        first_x = color in (1, 5, 6)
        landed = Y if first_x else X
        for role in working(color):
            if color == 2:
                arrive[role, "P", i] = EARLY
                todo[role].append(("p_send", i, ("P",)))
                continue
            if color >= 3:
                todo[role].append(("z_join", i, (ZL,)))
                starts["outer" if role == "inner" else "inner"]["z_first"].append(i)
            else:
                starts[role]["x_first" if first_x else "y_send"].append(i)
            todo[role].append(("y_second", i, (X,)) if first_x else ("x_send", i, (Y,)))
        if "outer" in working(color):
            todo["outer"].append(("z_in", i, (landed,)))
        needs = (landed,) * ("inner" in working(color)) + (ZI,) * ("outer" in working(color))
        if direct(color, mode):
            todo["inner"] += [("z_own", i, (landed,)), ("z_out", i, (ZI, ZM, ZF))]
        else:
            todo["inner"] += [("z_mid", i, needs), ("z_out", i, (ZM,))]
        if mode in (0, 2):
            todo["outer"].append(("relay", i, (ZO,)))
        if mode in (1, 2):
            todo["inner" if mode == 1 else "outer"].append(("forward", i, (B,)))
    if early:
        for role in ROLES:
            links[role, Y] = 128 / RATE
            arrive[role, "L", 0] = EARLY - 1.1
            arrive[role, "G", 0] = EARLY - 0.1
            todo[role] += [("p_low", 0, ("L",)), ("p_get", 0, ("G",))]

    def move(role, link, rows, now, to, kind, i, then=None):
        begin = max(now, links.get((role, link), 0.0))
        done = begin + rows / RATE
        links[role, link] = done
        if then:
            begin = max(begin + MORE, links.get(then, 0.0))
            done = max(begin + rows / RATE, done + MORE)
            links[then] = done
        arrive[to, kind, i] = max(done + HOP, arrive.get((to, kind, i), 0.0))

    def carry(role, op, i, now):
        _, n, color, mode = pieces[i]
        h = n // 2
        first_x = color in (1, 5, 6)
        if op == "z_first":
            move(role, ZI if role == "outer" else ZO, 2 * n, now, "inner" if role == "outer" else "outer", ZL, i)
        elif op == "y_send" or (op == "z_join" and not first_x):
            move(role, Y, n, now, role, Y, i)
        elif op in ("x_send", "p_send"):
            move(role, X, h, now, role, X, i)
        elif op == "x_first" or op == "z_join":
            move(role, X, n, now, role, X, i)
        elif op == "y_second":
            move(role, Y, h, now, role, Y, i)
        elif op == "z_in":
            move(role, ZI, h, now, "inner", ZI, i)
            if direct(color, mode):
                move(role, ZI, h, now, "inner", ZF, i, ("inner", ZM))
        elif op in ("z_mid", "z_own"):
            move(role, ZM, h, now, role, ZM, i)
        elif op == "z_out":
            if mode == 3:
                move(role, X, h, now, "outer", F, i, (role, ZO))
            if mode != 2:
                move(role, X, h, now, role, B, i)
            move(role, ZO, h, now, "outer", ZO, i)
        elif op == "relay":
            move(role, X, h, now, role, B, i)
        elif op == "forward":
            to = "outer" if role == "inner" else "inner"
            move(role, ZO if role == "inner" else ZI, h, now, to, F, i)

    while True:
        options = []
        for role in ROLES:
            clock = free.get(role, 0.0)
            for op, i, kinds in todo[role]:
                if all((role, kind, i) in arrive for kind in kinds):
                    ready = max(arrive[role, kind, i] for kind in kinds)
                    options.append((max(clock, ready), ready, role, op, i, kinds))
            side = ZI if role == "outer" else ZO
            for op, link, deep in (("y_send", Y, DEEP[0]), ("x_first", X, DEEP[1]), ("z_first", side, DEEP[2])):
                if starts[role][op]:
                    ready = links.get((role, link), 0.0) - deep
                    options.append((max(clock, ready), ready, role, op, starts[role][op][0], None))
        if not options:
            return out
        now, _, role, op, i, kinds = min(options, key=lambda option: option[:2])
        if kinds is None:
            starts[role][op].pop(0)
        else:
            todo[role].remove((op, i, kinds))
        out[role].append((now, op, i))
        now += COST.get(op, 0.03)
        free[role] = now
        carry(role, op, i, now)
        out["end"] = max(arrive.values())
        out["links"] = links


def fits(seq_count, dp_count):
    return dp_count == 2 * CORES and seq_count == 2 * LINE


def dot(a, b, da, db):
    return lax.dot_general(a, b, (((da,), (db,)), ((), ())), preferred_element_type=jnp.float32)


def fused_kernel(
    depth, factor, inverse,
    x_hbm, w_hbm, u_hbm, q_hbm, k_hbm, v_hbm, g_hbm,
    qo_ref, ko_ref, vo_ref, down_ref, up_ref,
    x_ref, w_ref, u_ref, four_ref, xs_ref, xr_ref, xt_ref,
    st_ref, pair_ref, kvr_ref, qgr_ref, ox_ref, sxs_ref, sxr_ref,
    ls_ref, lr_ref, ups_ref, upr_ref, fg_ref,
    ys_ref, yr_ref, acc_ref, xrs_ref, zs_ref, zr_ref, zm_ref, zf_ref, zl_ref,
    ps_ref, pr_ref, pt_ref, lo_ref, them_ref, pre_s, pre_r,
    load_sem, core_s, core_r, scan_s, scan_r, sx_s, sx_r,
    send_s, hop_r,
):
    seq = lax.axis_index("seq")
    dp = lax.axis_index("dp")
    z, x = seq // 2, seq % 2
    y, c = dp // CORES, dp % CORES
    mate = {"seq": seq, "dp": y * CORES + (1 - c)}
    across = {"seq": seq, "dp": (1 - y) * CORES + c}
    apart = {"seq": seq, "dp": (1 - y) * CORES + (1 - c)}
    beside = {"seq": z * 2 + (1 - x), "dp": dp}

    near = jnp.where(z % 3 == 0, z + 1 - 2 * (z // 3), 3 * (z // 2))
    diagonal = {"seq": near * 2 + (1 - x), "dp": dp}

    def along(other):
        return {"seq": other * 2 + x, "dp": dp}

    for i, part in enumerate((q_hbm, k_hbm, v_hbm, g_hbm)):
        pltpu.make_async_copy(part, four_ref.at[i], load_sem.at[2]).start()
    load_u = pltpu.make_async_copy(u_hbm, u_ref, load_sem.at[3])
    load_x = pltpu.make_async_copy(x_hbm, x_ref, load_sem.at[0])
    load_w = pltpu.make_async_copy(w_hbm, w_ref, load_sem.at[1])
    load_u.start()
    load_x.start()
    load_w.start()

    barrier = pltpu.get_barrier_semaphore()
    friends = [mate, across, apart, beside, diagonal] + [along(lax.rem(z + d, depth)) for d in range(1, depth)]
    for friend in friends:
        pl.semaphore_signal(barrier, inc=1, device_id=friend, device_id_type=MESH)

    rows, width = qo_ref.shape
    shard = down_ref.shape[0]
    ushard = up_ref.shape[0]
    pieces = cut(shard, ushard)
    early = fetched(pieces)
    pltpu.make_async_copy(four_ref, four_ref, load_sem.at[2]).wait()
    q, k, v, g = four_ref[0], four_ref[1], four_ref[2], four_ref[3]
    st_ref[0] = dot(k, v, 0, 0)
    st_ref[1] = dot(q, g, 0, 0)
    pl.semaphore_wait(barrier, len(friends))

    def remote(src, dst, ssem, rsem, where):
        return pltpu.make_async_remote_copy(
            src_ref=src, dst_ref=dst, send_sem=ssem, recv_sem=rsem, device_id=where, device_id_type=MESH
        )

    lead = width // 2
    first, second = slice(0, lead), slice(lead, width)
    other = remote(st_ref.at[:, second, :], ox_ref, sx_s.at[1], sx_r.at[1], beside)
    other.start()

    def scan(source, part, at):
        ups, downs = [], []
        for d in range(1, depth):
            slot = at * (depth - 1) + d - 1
            back = at * (depth - 1) + depth - d - 1
            ups.append(remote(source.at[0, part, :], kvr_ref.at[d - 1, part, :], scan_s.at[0], scan_r.at[slot], along(lax.rem(z + d, depth))))
            downs.append(remote(source.at[1, part, :], qgr_ref.at[d - 1, part, :], scan_s.at[0], scan_r.at[back], along(lax.rem(z - d + depth, depth))))
        for d in range(1, depth):
            pl.when(z + d < depth)(ups[d - 1].start)
            pl.when(z >= d)(downs[d - 1].start)
        return ups, downs

    def collect(ups, downs, part):
        sxs_ref[:, part, :] = jnp.zeros((2, lead, width), jnp.float32)
        for d in range(1, depth):
            @pl.when(z >= d)
            def _(d=d):
                ups[d - 1].wait_recv()
                sxs_ref[0, part, :] += kvr_ref[d - 1, part, :]

            @pl.when(z + d < depth)
            def _(d=d):
                downs[d - 1].wait_recv()
                sxs_ref[1, part, :] += qgr_ref[d - 1, part, :]

    scan_a = scan(st_ref, first, 0)

    load_x.wait()
    core_copies, extra = [], []
    if early:
        for at, where, core in ((0, across, c), (1, apart, 1 - c)):
            cols = pl.ds(pl.multiple_of(((1 - y) * CORES + core) * shard, 128), early)
            ps_ref[at] = x_ref[:, cols].astype(jnp.float32)
            copy = remote(ps_ref.at[at], pr_ref.at[at], pre_s.at[at], pre_r.at[at], where)
            copy.start()
            extra.append(copy)
    for part in range(2):
        cols = pl.ds(pl.multiple_of((part * CORES + 1 - c) * shard, 128), shard)
        xs_ref[part] = x_ref[:, cols].astype(jnp.float32)
        copy = remote(xs_ref.at[part], xr_ref.at[part], core_s.at[part], core_r.at[part], mate)
        copy.start()
        core_copies.append(copy)

    other.wait_recv()
    pair_ref[:, second, :] = st_ref[:, second, :] + ox_ref[...]
    scan_b = scan(pair_ref, second, 1)

    r_idx = lax.broadcasted_iota(jnp.int32, (rows, rows), 0)
    c_idx = lax.broadcasted_iota(jnp.int32, (rows, rows), 1)
    causal = r_idx >= c_idx
    gs = jnp.where(causal, dot(g, v, 1, 1), 0.0).astype(jnp.bfloat16)
    sc = jnp.where(causal, dot(q, k, 1, 1), 0.0).astype(jnp.bfloat16)
    q_in = dot(gs, k, 1, 0)
    k_in = dot(gs, q, 0, 0)
    v_in = dot(sc, g, 0, 0)

    for part in range(2):
        cols = pl.ds(pl.multiple_of((part * CORES + c) * shard, 128), shard)
        xt_ref[part, :, 0:rows] = x_ref[:, cols].T

    load_w.wait()
    low = jnp.dot(x_ref[...], w_ref[...], preferred_element_type=jnp.float32).astype(jnp.bfloat16)

    collect(*scan_a, first)
    lead_sum = sxs_ref[:, first, :]

    @pl.when(x == 0)
    def _():
        sxs_ref[0, first, :] += st_ref[0, first, :]

    @pl.when(x == 1)
    def _():
        sxs_ref[1, first, :] += st_ref[1, first, :]

    swap = remote(sxs_ref.at[:, first, :], sxr_ref, sx_s.at[0], sx_r.at[0], beside)
    swap.start()

    for part in range(2):
        core_copies[part].wait_recv()
        xt_ref[part, :, rows:] = xr_ref[part].astype(jnp.bfloat16).T

    collect(*scan_b, second)

    @pl.when(x == 1)
    def _():
        sxs_ref[0, second, :] += ox_ref[0]

    @pl.when(x == 0)
    def _():
        sxs_ref[1, second, :] += ox_ref[1]

    swap.wait_recv()
    states = jnp.concatenate([lead_sum + sxr_ref[...], sxs_ref[:, second, :]], axis=1).astype(jnp.bfloat16)
    prefix, suffix = states[0], states[1]
    q_grad = (factor * (q_in + dot(g, prefix, 1, 1))).astype(jnp.bfloat16)
    k_grad = (factor * (k_in + dot(v, suffix, 1, 1))).astype(jnp.bfloat16)
    v_grad = (factor * (v_in + dot(k, suffix, 1, 0))).astype(jnp.bfloat16)
    fg = jnp.concatenate([q_grad, k_grad, v_grad], axis=1)
    load_u.wait()
    low_grad = dot(fg, u_ref[...], 1, 0).astype(jnp.bfloat16)
    ls_ref[...] = low_grad.astype(jnp.float32)
    low_copy = remote(ls_ref, lr_ref, core_s.at[2], core_r.at[2], mate)
    low_copy.start()
    if early:
        low_across = remote(ls_ref, lo_ref.at[0], pre_s.at[2], pre_r.at[2], across)
        low_across.start()
        low_apart = remote(lo_ref.at[0], lo_ref.at[1], pre_s.at[3], pre_r.at[3], mate)
        extra.extend([low_across, low_apart])
    qo_ref[...] = q_grad
    ko_ref[...] = k_grad
    vo_ref[...] = v_grad

    low_copy.wait_recv()
    both = jnp.concatenate([low_grad, lr_ref[...].astype(jnp.bfloat16)], axis=0)

    outer = (z == 0) | (z == depth - 1)
    inner = jnp.logical_not(outer)
    mid = jnp.where(z < depth // 2, depth // 2 - 1, depth // 2)
    end = jnp.where(z < depth // 2, 0, depth - 1)
    inward, outward, opposite = along(mid), along(end), along(depth - 1 - z)
    further = along(depth - 1 - mid)
    corner = {"seq": end * 2 + (1 - x), "dp": dp}
    slots = landing(pieces)
    sent = {}

    def send(role, kind, i, src, dst, where):
        sent[kind] = sent.get(kind, 0) + src.shape[0]
        at = slots.get((kind, i), len(slots))
        remote(src, dst, send_s.at[kind], hop_r.at[at], where).start()

    def arrived(kind, i, like):
        remote(like, like, send_s.at[kind], hop_r.at[slots[kind, i]], mate).wait_recv()

    def partial(i, part):
        off, n = pieces[i][:2]
        if off < shard:
            return jnp.dot(xt_ref[part, off : off + n, :], both, preferred_element_type=jnp.float32)
        mine = pl.ds(pl.multiple_of((part * CORES + c) * ushard, 8), ushard)
        return fg_ref[mine, :] + upr_ref[part]

    def half(i, which):
        off, n = pieces[i][:2]
        return pl.ds(pl.multiple_of(off + which * (n // 2), 8), n // 2)

    def short(i):
        off, n = pieces[i][:2]
        return slice(off // 2, off // 2 + n // 2)

    def place(i, which):
        off, n = pieces[i][:2]
        ref, base = (down_ref, off) if off < shard else (up_ref, 0)
        return ref.at[pl.ds(pl.multiple_of(base + which * (n // 2), 8), n // 2), :]

    def perform(role, op, i):
        off, n, color, mode = pieces[i]
        h = n // 2
        first_x = color in (1, 5, 6)
        workers = working(color)
        whole, low_half, high_half = slice(off, off + n), slice(off, off + h), slice(off + h, off + n)
        small = short(i)
        landed = Y if first_x else X
        if op == "y_send":
            if off >= shard:
                up_copy.wait_recv()
            ys_ref[whole, :] = partial(i, 1 - y)
            send(role, Y, i, ys_ref.at[whole, :], yr_ref.at[whole, :], across)
        elif op == "z_first":
            where = inward if role == "outer" else outward
            ys_ref[whole, :] = partial(i, 1 - y)
            send(role, ZL, i, ys_ref.at[whole, :], zl_ref.at[0, whole, :], where)
            acc_ref[whole, :] = partial(i, y)
            send(role, ZL, i, acc_ref.at[whole, :], zl_ref.at[1, whole, :], where)
        elif op == "z_join":
            arrived(ZL, i, zl_ref.at[:, whole, :])
            ys_ref[whole, :] = partial(i, 1 - y) + zl_ref[0, whole, :]
            if first_x:
                send(role, X, i, ys_ref.at[half(i, 1 - x), :], yr_ref.at[high_half, :], beside)
                acc_ref[whole, :] = partial(i, y) + zl_ref[1, whole, :]
                send(role, X, i, acc_ref.at[half(i, 1 - x), :], yr_ref.at[low_half, :], beside)
            else:
                send(role, Y, i, ys_ref.at[whole, :], yr_ref.at[whole, :], across)
        elif op == "p_low":
            low_across.wait_recv()
            low_apart.start()
        elif op == "p_get":
            low_apart.wait_recv()
            for at in range(2):
                extra[at].wait_recv()
                pt_ref[:, at * rows : (at + 1) * rows] = pr_ref[at].astype(jnp.bfloat16).T
                them_ref[at * rows : (at + 1) * rows, :] = lo_ref[at].astype(jnp.bfloat16)
        elif op == "p_send":
            acc_ref[whole, :] = partial(i, y) + jnp.dot(
                pt_ref[whole, :], them_ref[...], preferred_element_type=jnp.float32
            )
            send(role, X, i, acc_ref.at[half(i, 1 - x), :], xrs_ref.at[small, :], beside)
        elif op == "x_send":
            own = partial(i, y)
            if color >= 3:
                own = own + zl_ref[1, whole, :]
            arrived(Y, i, yr_ref.at[whole, :])
            acc_ref[whole, :] = own + yr_ref[whole, :]
            send(role, X, i, acc_ref.at[half(i, 1 - x), :], xrs_ref.at[small, :], beside)
        elif op == "x_first":
            ys_ref[whole, :] = partial(i, 1 - y)
            send(role, X, i, ys_ref.at[half(i, 1 - x), :], yr_ref.at[high_half, :], beside)
            acc_ref[whole, :] = partial(i, y)
            send(role, X, i, acc_ref.at[half(i, 1 - x), :], yr_ref.at[low_half, :], beside)
        elif op == "y_second":
            arrived(X, i, yr_ref.at[whole, :])
            ys_ref[half(i, x), :] += yr_ref[high_half, :]
            send(role, Y, i, ys_ref.at[half(i, x), :], xrs_ref.at[small, :], across)
            acc_ref[half(i, x), :] += yr_ref[low_half, :]
        elif op == "z_in":
            arrived(landed, i, xrs_ref.at[small, :])
            zs_ref[small, :] = acc_ref[half(i, x), :] + xrs_ref[small, :]
            send(role, ZI, i, zs_ref.at[small, :], zr_ref.at[small, :], inward)
            if direct(color, mode):
                send(role, ZF, i, zs_ref.at[small, :], zf_ref.at[small, :], further)
        elif op == "z_own":
            arrived(landed, i, xrs_ref.at[small, :])
            zs_ref[small, :] = acc_ref[half(i, x), :] + xrs_ref[small, :]
            send(role, ZM, i, zs_ref.at[small, :], zm_ref.at[small, :], opposite)
        elif op == "z_mid":
            if "inner" in workers:
                arrived(landed, i, xrs_ref.at[small, :])
                own = acc_ref[half(i, x), :] + xrs_ref[small, :]
            if "outer" in workers:
                arrived(ZI, i, zr_ref.at[small, :])
                own = own + zr_ref[small, :] if "inner" in workers else zr_ref[small, :]
            zs_ref[small, :] = own
            send(role, ZM, i, zs_ref.at[small, :], zm_ref.at[small, :], opposite)
        elif op == "z_out":
            own = zs_ref[small, :]
            if direct(color, mode):
                arrived(ZI, i, zr_ref.at[small, :])
                own = own + zr_ref[small, :]
            arrived(ZM, i, zm_ref.at[small, :])
            own = own + zm_ref[small, :]
            if direct(color, mode):
                arrived(ZF, i, zf_ref.at[small, :])
                own = own + zf_ref[small, :]
            spot = place(i, x)
            spot[...] = own * inverse
            if mode == 3:
                send(role, F, i, spot, spot, corner)
            if mode in (0, 1, 3):
                send(role, B, i, spot, spot, beside)
            send(role, ZO, i, spot, spot, outward)
        elif op == "relay":
            spot = place(i, x)
            arrived(ZO, i, spot)
            send(role, B, i, spot, spot, beside)
        elif op == "forward":
            spot = place(i, 1 - x)
            arrived(B, i, spot)
            send(role, F, i, spot, spot, outward if role == "inner" else inward)

    up_all = dot(fg, low, 0, 0)
    fg_ref[...] = up_all
    for part in range(2):
        rng = pl.ds(pl.multiple_of((part * CORES + 1 - c) * ushard, 8), ushard)
        ups_ref[part] = fg_ref[rng, :]
    up_copy = remote(ups_ref, upr_ref, core_s.at[3], core_r.at[3], mate)
    up_copy.start()

    for role, here in (("outer", outer), ("inner", inner)):
        @pl.when(here)
        def _(role=role):
            sent.clear()
            for _, op, i in plan(pieces)[role]:
                perform(role, op, i)
            late = sum(n // 2 for _, n, _, mode in pieces if mode in (1, 3) and role == "outer") + sum(
                n // 2 for _, n, _, mode in pieces if (role, mode) not in (("outer", 2), ("inner", 1)))
            like = ys_ref.at[0:late, :]
            remote(like, like, send_s.at[0], hop_r.at[len(slots)], mate).wait_recv()
            for kind, rows in list(sent.items()):
                like = zl_ref.at[:, 0 : rows // 2, :] if kind == ZL else ys_ref.at[0:rows, :]
                remote(like, like, send_s.at[kind], hop_r.at[len(slots)], mate).wait_send()

    remote(kvr_ref, kvr_ref, scan_s.at[0], scan_r.at[0], mate).wait_send()
    for copy in core_copies + [other, swap, low_copy, up_copy] + extra:
        copy.wait_send()


def write_out(*refs):
    copies = [pltpu.make_async_copy(refs[i], refs[5 + i], refs[10].at[i]) for i in range(5)]
    for copy in copies:
        copy.start()
    for copy in copies:
        copy.wait()


def fast(inputs, adapter_down_weight, adapter_up_weight, query, key, value, output_gradient):
    rows, width = query.shape[1:]
    model = inputs.shape[2]
    rank = adapter_down_weight.shape[1]
    features = adapter_up_weight.shape[0]
    seq_count = lax.axis_size("seq")
    dp_count = lax.axis_size("dp")
    length = rows * seq_count
    factor = 1.0 / math.sqrt(HEAD_SIZE * length)
    inverse = 1.0 / math.sqrt(length * dp_count)
    depth = seq_count // 2
    shard, ushard = model // dp_count, features // dp_count
    total = shard + ushard
    pieces = cut(shard, ushard)
    early = max(fetched(pieces), rows)
    f32, bf16 = jnp.float32, jnp.bfloat16
    dma = pltpu.SemaphoreType.DMA
    vmem = pl.BlockSpec(memory_space=pltpu.VMEM)
    hbm = pl.BlockSpec(memory_space=pl.ANY)
    shapes = [jax.ShapeDtypeStruct((rows, width), bf16)] * 3 + [
        jax.ShapeDtypeStruct((shard, rank), f32),
        jax.ShapeDtypeStruct((ushard, rank), f32),
    ]
    out = pl.pallas_call(
        functools.partial(fused_kernel, depth, factor, inverse),
        out_shape=[pltpu.VMEM(part.shape, part.dtype) for part in shapes],
        in_specs=[hbm] * 7,
        out_specs=[vmem] * 5,
        scratch_shapes=[
            pltpu.VMEM((rows, model), bf16),
            pltpu.VMEM((model, rank), bf16),
            pltpu.VMEM((features, rank), bf16),
            pltpu.VMEM((4, rows, width), bf16),
            pltpu.VMEM((2, rows, shard), f32),
            pltpu.VMEM((2, rows, shard), f32),
            pltpu.VMEM((2, shard, 2 * rows), bf16),
            pltpu.VMEM((2, width, width), f32),
            pltpu.VMEM((2, width, width), f32),
            pltpu.VMEM((depth - 1, width, width), f32),
            pltpu.VMEM((depth - 1, width, width), f32),
            pltpu.VMEM((2, width // 2, width), f32),
            pltpu.VMEM((2, width, width), f32),
            pltpu.VMEM((2, width // 2, width), f32),
            pltpu.VMEM((rows, rank), f32),
            pltpu.VMEM((rows, rank), f32),
            pltpu.VMEM((2, ushard, rank), f32),
            pltpu.VMEM((2, ushard, rank), f32),
            pltpu.VMEM((features, rank), f32),
            pltpu.VMEM((total, rank), f32),
            pltpu.VMEM((total, rank), f32),
            pltpu.VMEM((total, rank), f32),
            pltpu.VMEM((total // 2, rank), f32),
            pltpu.VMEM((total // 2, rank), f32),
            pltpu.VMEM((total // 2, rank), f32),
            pltpu.VMEM((total // 2, rank), f32),
            pltpu.VMEM((total // 2, rank), f32),
            pltpu.VMEM((2, total, rank), f32),
            pltpu.VMEM((2, rows, early), f32),
            pltpu.VMEM((2, rows, early), f32),
            pltpu.VMEM((early, 2 * rows), bf16),
            pltpu.VMEM((2, rows, rank), f32),
            pltpu.VMEM((2 * rows, rank), bf16),
            dma((4,)), dma((4,)),
            dma((4,)), dma((4,)), dma((4,)),
            dma((1,)), dma((2 * depth - 2,)),
            dma((2,)), dma((2,)),
            dma((KINDS,)), dma((len(landing(pieces)) + 1,)),
        ],
        compiler_params=pltpu.CompilerParams(
            collective_id=0, has_side_effects=True
        ),
    )(
        inputs.reshape(rows, model), adapter_down_weight, adapter_up_weight,
        query.reshape(rows, width), key.reshape(rows, width),
        value.reshape(rows, width), output_gradient.reshape(rows, width),
    )
    out = pl.pallas_call(
        write_out,
        out_shape=shapes,
        in_specs=[vmem] * 5,
        out_specs=[hbm] * 5,
        scratch_shapes=[dma((5,))],
    )(*[pltpu.with_memory_space_constraint(part, pltpu.VMEM) for part in out])
    return tuple(part.reshape(1, rows, width) for part in out[:3]) + tuple(out[3:])


def solution(mesh):
    fused = fits(mesh.shape["seq"], mesh.shape["dp"])
    chosen = fast if fused else local
    return jax.shard_map(
        chosen,
        mesh=mesh,
        in_specs=(
            P("dp", "seq", None),
            P(),
            P(),
            P("dp", "seq", None),
            P("dp", "seq", None),
            P("dp", "seq", None),
            P("dp", "seq", None),
        ),
        out_specs=(
            P("dp", "seq", None),
            P("dp", "seq", None),
            P("dp", "seq", None),
            P("dp", None),
            P("dp", None),
        ),
        check_vma=False,
    )
```

```python
import functools
import math

import jax
import jax.numpy as jnp
from jax import lax
from jax.experimental import pallas as pl
from jax.experimental.pallas import tpu as pltpu
from jax.sharding import PartitionSpec as P

HEAD_SIZE = 128
LOCAL_HEADS = 1


def entering(part, axis, combine, identity, reverse):
    count = lax.axis_size(axis)
    place = lax.axis_index(axis)
    ahead = count - 1 - place if reverse else place
    gathered = lax.all_gather(part, axis)
    state = jnp.zeros_like(part) + jnp.asarray(identity, part.dtype)

    def one(turn, state):
        source = count - 1 - turn if reverse else turn
        return combine(state, lax.dynamic_index_in_dim(gathered, source, 0, False))

    return lax.fori_loop(0, ahead, one, state)


def add_states(earlier, later):
    return earlier + later


def rounded_values(array):
    return array.astype(jnp.bfloat16)


def local(inputs, adapter_down_weight, adapter_up_weight, query, key, value, output_gradient):
    rows = query.shape[1]
    width = query.shape[2]
    seq_count = lax.axis_size("seq")
    dp_count = lax.axis_size("dp")
    length = rows * seq_count
    factor = 1.0 / math.sqrt(HEAD_SIZE * length)
    queries = query.reshape(rows, LOCAL_HEADS, HEAD_SIZE)
    keys = key.reshape(rows, LOCAL_HEADS, HEAD_SIZE)
    values = value.reshape(rows, LOCAL_HEADS, HEAD_SIZE)
    grads_out = output_gradient.reshape(rows, LOCAL_HEADS, HEAD_SIZE)
    kv_state = jnp.einsum("thi,thj->hij", keys, values, preferred_element_type=jnp.float32)
    qg_state = jnp.einsum("thi,thj->hij", queries, grads_out, preferred_element_type=jnp.float32)
    zeros = jnp.zeros_like(kv_state)
    prefix = entering(kv_state, "seq", add_states, zeros, False)
    suffix = entering(qg_state, "seq", add_states, zeros, True)
    prefix = rounded_values(prefix)
    suffix = rounded_values(suffix)
    rows_idx = lax.broadcasted_iota(jnp.int32, (rows, rows), 0)
    cols_idx = lax.broadcasted_iota(jnp.int32, (rows, rows), 1)
    causal = rows_idx >= cols_idx
    grad_scores = rounded_values(
        jnp.where(
            causal,
            jnp.einsum("thj,shj->hts", grads_out, values, preferred_element_type=jnp.float32),
            0.0,
        )
    )
    scores = rounded_values(
        jnp.where(
            causal,
            jnp.einsum("thi,shi->hts", queries, keys, preferred_element_type=jnp.float32),
            0.0,
        )
    )
    query_grad = jnp.einsum(
        "hts,shi->thi", grad_scores, keys, preferred_element_type=jnp.float32
    ) + jnp.einsum("thj,hij->thi", grads_out, prefix, preferred_element_type=jnp.float32)
    key_grad = jnp.einsum(
        "hts,thi->shi", grad_scores, queries, preferred_element_type=jnp.float32
    ) + jnp.einsum("shj,hij->shi", values, suffix, preferred_element_type=jnp.float32)
    value_grad = jnp.einsum(
        "hts,thj->shj", scores, grads_out, preferred_element_type=jnp.float32
    ) + jnp.einsum("shi,hij->shj", keys, suffix, preferred_element_type=jnp.float32)
    query_grad = rounded_values(factor * query_grad).reshape(rows, width)
    key_grad = rounded_values(factor * key_grad).reshape(rows, width)
    value_grad = rounded_values(factor * value_grad).reshape(rows, width)
    flattened = inputs.reshape(rows, inputs.shape[2])
    gradient_list = jnp.concatenate([query_grad, key_grad, value_grad], axis=1)
    low_rank_state = rounded_values(
        jnp.dot(flattened, adapter_down_weight, preferred_element_type=jnp.float32)
    )
    low_rank_gradient = rounded_values(
        jnp.dot(gradient_list, adapter_up_weight, preferred_element_type=jnp.float32)
    )
    inverse = 1.0 / math.sqrt(length * dp_count)
    contract = (((0,), (0,)), ((), ()))
    down_part = lax.psum_scatter(
        lax.dot_general(flattened, low_rank_gradient, contract, preferred_element_type=jnp.float32)
        * inverse,
        "dp",
        scatter_dimension=0,
        tiled=True,
    )
    up_term = (
        lax.dot_general(gradient_list, low_rank_state, contract, preferred_element_type=jnp.float32)
        * inverse
    )
    up_part = lax.psum_scatter(up_term, "dp", scatter_dimension=0, tiled=True)
    down_grad, up_grad = lax.psum((down_part, up_part), "seq")
    return (
        query_grad.reshape(1, rows, width),
        key_grad.reshape(1, rows, width),
        value_grad.reshape(1, rows, width),
        down_grad,
        up_grad,
    )


MESH = pl.DeviceIdType.MESH
CORES = 2
LINE = 4
KINDS = 9
Y, X, ZI, ZM, ZF, ZO, B, F, ZL = range(KINDS)
ROLES = ("outer", "inner")
CUTS = (
    (6, 5, 2), (9, 3, 0), (6, 0, 0), (7, 1, 2), (2, 1, 0), (3, 6, 0), (5, 0, 0), (9, 1, 0),
    (5, 0, 0), (8, 4, 0), (7, 4, 0), (7, 1, 2), (3, 6, 1), (5, 0, 0), (6, 3, 0), (3, 0, 0),
    (5, 6, 3), (2, 0, 0), (8, 0, 0), (0, 0, 2), (3, 1, 0), (6, 1, 2), (5, 4, 3), (8, 1, 0),
)
RATE, HOP, MORE, EARLY = 92.0, 1.75, 0.75, 4.3
DEEP = (2.0, 0.7, 2.0)
COST = {"y_send": 0.17, "x_send": 0.18, "x_first": 0.32, "z_first": 0.32, "z_join": 0.34, "p_send": 0.25}


def cut(shard, ushard):
    unit = shard // sum(parts for parts, _, _ in CUTS)
    places, off = {}, 0
    for i in sorted(range(len(CUTS)), key=lambda i: CUTS[i][1] != 2):
        places[i] = off
        off += CUTS[i][0] * unit
    return [
        (places[i], parts * unit, color, mode) if parts else (shard, ushard, color, mode)
        for i, (parts, color, mode) in enumerate(CUTS)
    ]


def fetched(pieces):
    return sum(n for _, n, color, _ in pieces if color == 2)


def working(color):
    return {3: ("inner",), 5: ("inner",), 4: ("outer",), 6: ("outer",)}.get(color, ROLES)


def direct(color, mode):
    return mode == 3 and color < 3


def landing(pieces):
    slots = {}
    for i, (_, _, color, mode) in enumerate(pieces):
        for kind in (Y, X, ZI, ZM):
            slots[kind, i] = len(slots)
        if color >= 3:
            slots[ZL, i] = len(slots)
        if mode in (0, 2):
            slots[ZO, i] = slots[ZI, i]
        if mode == 1:
            slots[B, i] = len(slots)
        if mode == 2:
            slots[B, i] = slots[ZM, i]
        if direct(color, mode):
            slots[ZF, i] = len(slots)
    return slots


def plan(pieces):
    free, links, arrive = {}, {}, {}
    out = {role: [] for role in ROLES}
    todo = {role: [] for role in ROLES}
    starts = {role: {"y_send": [], "x_first": [], "z_first": []} for role in ROLES}
    early = any(color == 2 for _, _, color, _ in pieces)
    for i, (_, _, color, mode) in enumerate(pieces):
        first_x = color in (1, 5, 6)
        landed = Y if first_x else X
        for role in working(color):
            if color == 2:
                arrive[role, "P", i] = EARLY
                todo[role].append(("p_send", i, ("P",)))
                continue
            if color >= 3:
                todo[role].append(("z_join", i, (ZL,)))
                starts["outer" if role == "inner" else "inner"]["z_first"].append(i)
            else:
                starts[role]["x_first" if first_x else "y_send"].append(i)
            todo[role].append(("y_second", i, (X,)) if first_x else ("x_send", i, (Y,)))
        if "outer" in working(color):
            todo["outer"].append(("z_in", i, (landed,)))
        needs = (landed,) * ("inner" in working(color)) + (ZI,) * ("outer" in working(color))
        if direct(color, mode):
            todo["inner"] += [("z_own", i, (landed,)), ("z_out", i, (ZI, ZM, ZF))]
        else:
            todo["inner"] += [("z_mid", i, needs), ("z_out", i, (ZM,))]
        if mode in (0, 2):
            todo["outer"].append(("relay", i, (ZO,)))
        if mode in (1, 2):
            todo["inner" if mode == 1 else "outer"].append(("forward", i, (B,)))
    if early:
        for role in ROLES:
            links[role, Y] = 128 / RATE
            arrive[role, "L", 0] = EARLY - 1.1
            arrive[role, "G", 0] = EARLY - 0.1
            todo[role] += [("p_low", 0, ("L",)), ("p_get", 0, ("G",))]

    def move(role, link, rows, now, to, kind, i, then=None):
        begin = max(now, links.get((role, link), 0.0))
        done = begin + rows / RATE
        links[role, link] = done
        if then:
            begin = max(begin + MORE, links.get(then, 0.0))
            done = max(begin + rows / RATE, done + MORE)
            links[then] = done
        arrive[to, kind, i] = max(done + HOP, arrive.get((to, kind, i), 0.0))

    def carry(role, op, i, now):
        _, n, color, mode = pieces[i]
        h = n // 2
        first_x = color in (1, 5, 6)
        if op == "z_first":
            move(role, ZI if role == "outer" else ZO, 2 * n, now, "inner" if role == "outer" else "outer", ZL, i)
        elif op == "y_send" or (op == "z_join" and not first_x):
            move(role, Y, n, now, role, Y, i)
        elif op in ("x_send", "p_send"):
            move(role, X, h, now, role, X, i)
        elif op == "x_first" or op == "z_join":
            move(role, X, n, now, role, X, i)
        elif op == "y_second":
            move(role, Y, h, now, role, Y, i)
        elif op == "z_in":
            move(role, ZI, h, now, "inner", ZI, i)
            if direct(color, mode):
                move(role, ZI, h, now, "inner", ZF, i, ("inner", ZM))
        elif op in ("z_mid", "z_own"):
            move(role, ZM, h, now, role, ZM, i)
        elif op == "z_out":
            if mode == 3:
                move(role, X, h, now, "outer", F, i, (role, ZO))
            if mode != 2:
                move(role, X, h, now, role, B, i)
            move(role, ZO, h, now, "outer", ZO, i)
        elif op == "relay":
            move(role, X, h, now, role, B, i)
        elif op == "forward":
            to = "outer" if role == "inner" else "inner"
            move(role, ZO if role == "inner" else ZI, h, now, to, F, i)

    while True:
        options = []
        for role in ROLES:
            clock = free.get(role, 0.0)
            for op, i, kinds in todo[role]:
                if all((role, kind, i) in arrive for kind in kinds):
                    ready = max(arrive[role, kind, i] for kind in kinds)
                    options.append((max(clock, ready), ready, role, op, i, kinds))
            side = ZI if role == "outer" else ZO
            for op, link, deep in (("y_send", Y, DEEP[0]), ("x_first", X, DEEP[1]), ("z_first", side, DEEP[2])):
                if starts[role][op]:
                    ready = links.get((role, link), 0.0) - deep
                    options.append((max(clock, ready), ready, role, op, starts[role][op][0], None))
        if not options:
            return out
        now, _, role, op, i, kinds = min(options, key=lambda option: option[:2])
        if kinds is None:
            starts[role][op].pop(0)
        else:
            todo[role].remove((op, i, kinds))
        out[role].append((now, op, i))
        now += COST.get(op, 0.03)
        free[role] = now
        carry(role, op, i, now)
        out["end"] = max(arrive.values())
        out["links"] = links


def fits(seq_count, dp_count):
    return dp_count == 2 * CORES and seq_count == 2 * LINE


def dot(a, b, da, db):
    return lax.dot_general(a, b, (((da,), (db,)), ((), ())), preferred_element_type=jnp.float32)


def fused_kernel(
    depth, factor, inverse,
    x_hbm, w_hbm, u_hbm, q_hbm, k_hbm, v_hbm, g_hbm,
    qo_ref, ko_ref, vo_ref, down_ref, up_ref,
    x_ref, w_ref, u_ref, four_ref, xs_ref, xr_ref, xt_ref,
    st_ref, pair_ref, kvr_ref, qgr_ref, ox_ref, sxs_ref, sxr_ref,
    ls_ref, lr_ref, ups_ref, upr_ref, fg_ref,
    ys_ref, yr_ref, acc_ref, xrs_ref, zs_ref, zr_ref, zm_ref, zf_ref, zl_ref,
    ps_ref, pr_ref, pt_ref, lo_ref, them_ref, pre_s, pre_r,
    load_sem, core_s, core_r, scan_s, scan_r, sx_s, sx_r,
    send_s, hop_r,
):
    seq = lax.axis_index("seq")
    dp = lax.axis_index("dp")
    z, x = seq // 2, seq % 2
    y, c = dp // CORES, dp % CORES
    mate = {"seq": seq, "dp": y * CORES + (1 - c)}
    across = {"seq": seq, "dp": (1 - y) * CORES + c}
    apart = {"seq": seq, "dp": (1 - y) * CORES + (1 - c)}
    beside = {"seq": z * 2 + (1 - x), "dp": dp}

    near = jnp.where(z % 3 == 0, z + 1 - 2 * (z // 3), 3 * (z // 2))
    diagonal = {"seq": near * 2 + (1 - x), "dp": dp}

    def along(other):
        return {"seq": other * 2 + x, "dp": dp}

    for i, part in enumerate((q_hbm, k_hbm, v_hbm, g_hbm)):
        pltpu.make_async_copy(part, four_ref.at[i], load_sem.at[2]).start()
    load_u = pltpu.make_async_copy(u_hbm, u_ref, load_sem.at[3])
    load_x = pltpu.make_async_copy(x_hbm, x_ref, load_sem.at[0])
    load_w = pltpu.make_async_copy(w_hbm, w_ref, load_sem.at[1])
    load_u.start()
    load_x.start()
    load_w.start()

    barrier = pltpu.get_barrier_semaphore()
    friends = [mate, across, apart, beside, diagonal] + [along(lax.rem(z + d, depth)) for d in range(1, depth)]
    for friend in friends:
        pl.semaphore_signal(barrier, inc=1, device_id=friend, device_id_type=MESH)

    rows, width = qo_ref.shape
    shard = down_ref.shape[0]
    ushard = up_ref.shape[0]
    pieces = cut(shard, ushard)
    early = fetched(pieces)
    pltpu.make_async_copy(four_ref, four_ref, load_sem.at[2]).wait()
    q, k, v, g = four_ref[0], four_ref[1], four_ref[2], four_ref[3]
    st_ref[0] = dot(k, v, 0, 0)
    st_ref[1] = dot(q, g, 0, 0)
    pl.semaphore_wait(barrier, len(friends))

    def remote(src, dst, ssem, rsem, where):
        return pltpu.make_async_remote_copy(
            src_ref=src, dst_ref=dst, send_sem=ssem, recv_sem=rsem, device_id=where, device_id_type=MESH
        )

    lead = width // 2
    first, second = slice(0, lead), slice(lead, width)
    other = remote(st_ref.at[:, second, :], ox_ref, sx_s.at[1], sx_r.at[1], beside)
    other.start()

    def scan(source, part, at):
        ups, downs = [], []
        for d in range(1, depth):
            slot = at * (depth - 1) + d - 1
            back = at * (depth - 1) + depth - d - 1
            ups.append(remote(source.at[0, part, :], kvr_ref.at[d - 1, part, :], scan_s.at[0], scan_r.at[slot], along(lax.rem(z + d, depth))))
            downs.append(remote(source.at[1, part, :], qgr_ref.at[d - 1, part, :], scan_s.at[0], scan_r.at[back], along(lax.rem(z - d + depth, depth))))
        for d in range(1, depth):
            pl.when(z + d < depth)(ups[d - 1].start)
            pl.when(z >= d)(downs[d - 1].start)
        return ups, downs

    def collect(ups, downs, part):
        sxs_ref[:, part, :] = jnp.zeros((2, lead, width), jnp.float32)
        for d in range(1, depth):
            @pl.when(z >= d)
            def _(d=d):
                ups[d - 1].wait_recv()
                sxs_ref[0, part, :] += kvr_ref[d - 1, part, :]

            @pl.when(z + d < depth)
            def _(d=d):
                downs[d - 1].wait_recv()
                sxs_ref[1, part, :] += qgr_ref[d - 1, part, :]

    scan_a = scan(st_ref, first, 0)

    load_x.wait()
    core_copies, extra = [], []
    if early:
        for at, where, core in ((0, across, c), (1, apart, 1 - c)):
            cols = pl.ds(pl.multiple_of(((1 - y) * CORES + core) * shard, 128), early)
            ps_ref[at] = x_ref[:, cols].astype(jnp.float32)
            copy = remote(ps_ref.at[at], pr_ref.at[at], pre_s.at[at], pre_r.at[at], where)
            copy.start()
            extra.append(copy)
    for part in range(2):
        cols = pl.ds(pl.multiple_of((part * CORES + 1 - c) * shard, 128), shard)
        xs_ref[part] = x_ref[:, cols].astype(jnp.float32)
        copy = remote(xs_ref.at[part], xr_ref.at[part], core_s.at[part], core_r.at[part], mate)
        copy.start()
        core_copies.append(copy)

    other.wait_recv()
    pair_ref[:, second, :] = st_ref[:, second, :] + ox_ref[...]
    scan_b = scan(pair_ref, second, 1)

    r_idx = lax.broadcasted_iota(jnp.int32, (rows, rows), 0)
    c_idx = lax.broadcasted_iota(jnp.int32, (rows, rows), 1)
    causal = r_idx >= c_idx
    gs = jnp.where(causal, dot(g, v, 1, 1), 0.0).astype(jnp.bfloat16)
    sc = jnp.where(causal, dot(q, k, 1, 1), 0.0).astype(jnp.bfloat16)
    q_in = dot(gs, k, 1, 0)
    k_in = dot(gs, q, 0, 0)
    v_in = dot(sc, g, 0, 0)

    for part in range(2):
        cols = pl.ds(pl.multiple_of((part * CORES + c) * shard, 128), shard)
        xt_ref[part, :, 0:rows] = x_ref[:, cols].T

    load_w.wait()
    low = jnp.dot(x_ref[...], w_ref[...], preferred_element_type=jnp.float32).astype(jnp.bfloat16)

    collect(*scan_a, first)
    lead_sum = sxs_ref[:, first, :]

    @pl.when(x == 0)
    def _():
        sxs_ref[0, first, :] += st_ref[0, first, :]

    @pl.when(x == 1)
    def _():
        sxs_ref[1, first, :] += st_ref[1, first, :]

    swap = remote(sxs_ref.at[:, first, :], sxr_ref, sx_s.at[0], sx_r.at[0], beside)
    swap.start()

    for part in range(2):
        core_copies[part].wait_recv()
        xt_ref[part, :, rows:] = xr_ref[part].astype(jnp.bfloat16).T

    collect(*scan_b, second)

    @pl.when(x == 1)
    def _():
        sxs_ref[0, second, :] += ox_ref[0]

    @pl.when(x == 0)
    def _():
        sxs_ref[1, second, :] += ox_ref[1]

    swap.wait_recv()
    states = jnp.concatenate([lead_sum + sxr_ref[...], sxs_ref[:, second, :]], axis=1).astype(jnp.bfloat16)
    prefix, suffix = states[0], states[1]
    q_grad = (factor * (q_in + dot(g, prefix, 1, 1))).astype(jnp.bfloat16)
    k_grad = (factor * (k_in + dot(v, suffix, 1, 1))).astype(jnp.bfloat16)
    v_grad = (factor * (v_in + dot(k, suffix, 1, 0))).astype(jnp.bfloat16)
    fg = jnp.concatenate([q_grad, k_grad, v_grad], axis=1)
    load_u.wait()
    low_grad = dot(fg, u_ref[...], 1, 0).astype(jnp.bfloat16)
    ls_ref[...] = low_grad.astype(jnp.float32)
    low_copy = remote(ls_ref, lr_ref, core_s.at[2], core_r.at[2], mate)
    low_copy.start()
    if early:
        low_across = remote(ls_ref, lo_ref.at[0], pre_s.at[2], pre_r.at[2], across)
        low_across.start()
        low_apart = remote(lo_ref.at[0], lo_ref.at[1], pre_s.at[3], pre_r.at[3], mate)
        extra.extend([low_across, low_apart])
    qo_ref[...] = q_grad
    ko_ref[...] = k_grad
    vo_ref[...] = v_grad

    low_copy.wait_recv()
    both = jnp.concatenate([low_grad, lr_ref[...].astype(jnp.bfloat16)], axis=0)

    outer = (z == 0) | (z == depth - 1)
    inner = jnp.logical_not(outer)
    mid = jnp.where(z < depth // 2, depth // 2 - 1, depth // 2)
    end = jnp.where(z < depth // 2, 0, depth - 1)
    inward, outward, opposite = along(mid), along(end), along(depth - 1 - z)
    further = along(depth - 1 - mid)
    corner = {"seq": end * 2 + (1 - x), "dp": dp}
    slots = landing(pieces)
    sent = {}

    def send(role, kind, i, src, dst, where):
        sent[kind] = sent.get(kind, 0) + src.shape[0]
        at = slots.get((kind, i), len(slots))
        remote(src, dst, send_s.at[kind], hop_r.at[at], where).start()

    def arrived(kind, i, like):
        remote(like, like, send_s.at[kind], hop_r.at[slots[kind, i]], mate).wait_recv()

    def partial(i, part):
        off, n = pieces[i][:2]
        if off < shard:
            return jnp.dot(xt_ref[part, off : off + n, :], both, preferred_element_type=jnp.float32)
        mine = pl.ds(pl.multiple_of((part * CORES + c) * ushard, 8), ushard)
        return fg_ref[mine, :] + upr_ref[part]

    def half(i, which):
        off, n = pieces[i][:2]
        return pl.ds(pl.multiple_of(off + which * (n // 2), 8), n // 2)

    def short(i):
        off, n = pieces[i][:2]
        return slice(off // 2, off // 2 + n // 2)

    def place(i, which):
        off, n = pieces[i][:2]
        ref, base = (down_ref, off) if off < shard else (up_ref, 0)
        return ref.at[pl.ds(pl.multiple_of(base + which * (n // 2), 8), n // 2), :]

    def perform(role, op, i):
        off, n, color, mode = pieces[i]
        h = n // 2
        first_x = color in (1, 5, 6)
        workers = working(color)
        whole, low_half, high_half = slice(off, off + n), slice(off, off + h), slice(off + h, off + n)
        small = short(i)
        landed = Y if first_x else X
        if op == "y_send":
            if off >= shard:
                up_copy.wait_recv()
            ys_ref[whole, :] = partial(i, 1 - y)
            send(role, Y, i, ys_ref.at[whole, :], yr_ref.at[whole, :], across)
        elif op == "z_first":
            where = inward if role == "outer" else outward
            ys_ref[whole, :] = partial(i, 1 - y)
            send(role, ZL, i, ys_ref.at[whole, :], zl_ref.at[0, whole, :], where)
            acc_ref[whole, :] = partial(i, y)
            send(role, ZL, i, acc_ref.at[whole, :], zl_ref.at[1, whole, :], where)
        elif op == "z_join":
            arrived(ZL, i, zl_ref.at[:, whole, :])
            ys_ref[whole, :] = partial(i, 1 - y) + zl_ref[0, whole, :]
            if first_x:
                send(role, X, i, ys_ref.at[half(i, 1 - x), :], yr_ref.at[high_half, :], beside)
                acc_ref[whole, :] = partial(i, y) + zl_ref[1, whole, :]
                send(role, X, i, acc_ref.at[half(i, 1 - x), :], yr_ref.at[low_half, :], beside)
            else:
                send(role, Y, i, ys_ref.at[whole, :], yr_ref.at[whole, :], across)
        elif op == "p_low":
            low_across.wait_recv()
            low_apart.start()
        elif op == "p_get":
            low_apart.wait_recv()
            for at in range(2):
                extra[at].wait_recv()
                pt_ref[:, at * rows : (at + 1) * rows] = pr_ref[at].astype(jnp.bfloat16).T
                them_ref[at * rows : (at + 1) * rows, :] = lo_ref[at].astype(jnp.bfloat16)
        elif op == "p_send":
            acc_ref[whole, :] = partial(i, y) + jnp.dot(
                pt_ref[whole, :], them_ref[...], preferred_element_type=jnp.float32
            )
            send(role, X, i, acc_ref.at[half(i, 1 - x), :], xrs_ref.at[small, :], beside)
        elif op == "x_send":
            own = partial(i, y)
            if color >= 3:
                own = own + zl_ref[1, whole, :]
            arrived(Y, i, yr_ref.at[whole, :])
            acc_ref[whole, :] = own + yr_ref[whole, :]
            send(role, X, i, acc_ref.at[half(i, 1 - x), :], xrs_ref.at[small, :], beside)
        elif op == "x_first":
            ys_ref[whole, :] = partial(i, 1 - y)
            send(role, X, i, ys_ref.at[half(i, 1 - x), :], yr_ref.at[high_half, :], beside)
            acc_ref[whole, :] = partial(i, y)
            send(role, X, i, acc_ref.at[half(i, 1 - x), :], yr_ref.at[low_half, :], beside)
        elif op == "y_second":
            arrived(X, i, yr_ref.at[whole, :])
            ys_ref[half(i, x), :] += yr_ref[high_half, :]
            send(role, Y, i, ys_ref.at[half(i, x), :], xrs_ref.at[small, :], across)
            acc_ref[half(i, x), :] += yr_ref[low_half, :]
        elif op == "z_in":
            arrived(landed, i, xrs_ref.at[small, :])
            zs_ref[small, :] = acc_ref[half(i, x), :] + xrs_ref[small, :]
            send(role, ZI, i, zs_ref.at[small, :], zr_ref.at[small, :], inward)
            if direct(color, mode):
                send(role, ZF, i, zs_ref.at[small, :], zf_ref.at[small, :], further)
        elif op == "z_own":
            arrived(landed, i, xrs_ref.at[small, :])
            zs_ref[small, :] = acc_ref[half(i, x), :] + xrs_ref[small, :]
            send(role, ZM, i, zs_ref.at[small, :], zm_ref.at[small, :], opposite)
        elif op == "z_mid":
            if "inner" in workers:
                arrived(landed, i, xrs_ref.at[small, :])
                own = acc_ref[half(i, x), :] + xrs_ref[small, :]
            if "outer" in workers:
                arrived(ZI, i, zr_ref.at[small, :])
                own = own + zr_ref[small, :] if "inner" in workers else zr_ref[small, :]
            zs_ref[small, :] = own
            send(role, ZM, i, zs_ref.at[small, :], zm_ref.at[small, :], opposite)
        elif op == "z_out":
            own = zs_ref[small, :]
            if direct(color, mode):
                arrived(ZI, i, zr_ref.at[small, :])
                own = own + zr_ref[small, :]
            arrived(ZM, i, zm_ref.at[small, :])
            own = own + zm_ref[small, :]
            if direct(color, mode):
                arrived(ZF, i, zf_ref.at[small, :])
                own = own + zf_ref[small, :]
            spot = place(i, x)
            spot[...] = own * inverse
            if mode == 3:
                send(role, F, i, spot, spot, corner)
            if mode in (0, 1, 3):
                send(role, B, i, spot, spot, beside)
            send(role, ZO, i, spot, spot, outward)
        elif op == "relay":
            spot = place(i, x)
            arrived(ZO, i, spot)
            send(role, B, i, spot, spot, beside)
        elif op == "forward":
            spot = place(i, 1 - x)
            arrived(B, i, spot)
            send(role, F, i, spot, spot, outward if role == "inner" else inward)

    up_all = dot(fg, low, 0, 0)
    fg_ref[...] = up_all
    for part in range(2):
        rng = pl.ds(pl.multiple_of((part * CORES + 1 - c) * ushard, 8), ushard)
        ups_ref[part] = fg_ref[rng, :]
    up_copy = remote(ups_ref, upr_ref, core_s.at[3], core_r.at[3], mate)
    up_copy.start()

    for role, here in (("outer", outer), ("inner", inner)):
        @pl.when(here)
        def _(role=role):
            sent.clear()
            for _, op, i in plan(pieces)[role]:
                perform(role, op, i)
            late = sum(n // 2 for _, n, _, mode in pieces if mode in (1, 3) and role == "outer") + sum(
                n // 2 for _, n, _, mode in pieces if (role, mode) not in (("outer", 2), ("inner", 1)))
            like = ys_ref.at[0:late, :]
            remote(like, like, send_s.at[0], hop_r.at[len(slots)], mate).wait_recv()
            for kind, rows in list(sent.items()):
                like = zl_ref.at[:, 0 : rows // 2, :] if kind == ZL else ys_ref.at[0:rows, :]
                remote(like, like, send_s.at[kind], hop_r.at[len(slots)], mate).wait_send()

    remote(kvr_ref, kvr_ref, scan_s.at[0], scan_r.at[0], mate).wait_send()
    for copy in core_copies + [other, swap, low_copy, up_copy] + extra:
        copy.wait_send()


def write_out(*refs):
    copies = [pltpu.make_async_copy(refs[i], refs[5 + i], refs[10].at[i]) for i in range(5)]
    for copy in copies:
        copy.start()
    for copy in copies:
        copy.wait()


def fast(inputs, adapter_down_weight, adapter_up_weight, query, key, value, output_gradient):
    rows, width = query.shape[1:]
    model = inputs.shape[2]
    rank = adapter_down_weight.shape[1]
    features = adapter_up_weight.shape[0]
    seq_count = lax.axis_size("seq")
    dp_count = lax.axis_size("dp")
    length = rows * seq_count
    factor = 1.0 / math.sqrt(HEAD_SIZE * length)
    inverse = 1.0 / math.sqrt(length * dp_count)
    depth = seq_count // 2
    shard, ushard = model // dp_count, features // dp_count
    total = shard + ushard
    pieces = cut(shard, ushard)
    early = max(fetched(pieces), rows)
    f32, bf16 = jnp.float32, jnp.bfloat16
    dma = pltpu.SemaphoreType.DMA
    vmem = pl.BlockSpec(memory_space=pltpu.VMEM)
    hbm = pl.BlockSpec(memory_space=pl.ANY)
    shapes = [jax.ShapeDtypeStruct((rows, width), bf16)] * 3 + [
        jax.ShapeDtypeStruct((shard, rank), f32),
        jax.ShapeDtypeStruct((ushard, rank), f32),
    ]
    out = pl.pallas_call(
        functools.partial(fused_kernel, depth, factor, inverse),
        out_shape=[pltpu.VMEM(part.shape, part.dtype) for part in shapes],
        in_specs=[hbm] * 7,
        out_specs=[vmem] * 5,
        scratch_shapes=[
            pltpu.VMEM((rows, model), bf16),
            pltpu.VMEM((model, rank), bf16),
            pltpu.VMEM((features, rank), bf16),
            pltpu.VMEM((4, rows, width), bf16),
            pltpu.VMEM((2, rows, shard), f32),
            pltpu.VMEM((2, rows, shard), f32),
            pltpu.VMEM((2, shard, 2 * rows), bf16),
            pltpu.VMEM((2, width, width), f32),
            pltpu.VMEM((2, width, width), f32),
            pltpu.VMEM((depth - 1, width, width), f32),
            pltpu.VMEM((depth - 1, width, width), f32),
            pltpu.VMEM((2, width // 2, width), f32),
            pltpu.VMEM((2, width, width), f32),
            pltpu.VMEM((2, width // 2, width), f32),
            pltpu.VMEM((rows, rank), f32),
            pltpu.VMEM((rows, rank), f32),
            pltpu.VMEM((2, ushard, rank), f32),
            pltpu.VMEM((2, ushard, rank), f32),
            pltpu.VMEM((features, rank), f32),
            pltpu.VMEM((total, rank), f32),
            pltpu.VMEM((total, rank), f32),
            pltpu.VMEM((total, rank), f32),
            pltpu.VMEM((total // 2, rank), f32),
            pltpu.VMEM((total // 2, rank), f32),
            pltpu.VMEM((total // 2, rank), f32),
            pltpu.VMEM((total // 2, rank), f32),
            pltpu.VMEM((total // 2, rank), f32),
            pltpu.VMEM((2, total, rank), f32),
            pltpu.VMEM((2, rows, early), f32),
            pltpu.VMEM((2, rows, early), f32),
            pltpu.VMEM((early, 2 * rows), bf16),
            pltpu.VMEM((2, rows, rank), f32),
            pltpu.VMEM((2 * rows, rank), bf16),
            dma((4,)), dma((4,)),
            dma((4,)), dma((4,)), dma((4,)),
            dma((1,)), dma((2 * depth - 2,)),
            dma((2,)), dma((2,)),
            dma((KINDS,)), dma((len(landing(pieces)) + 1,)),
        ],
        compiler_params=pltpu.CompilerParams(
            collective_id=0, has_side_effects=True
        ),
    )(
        inputs.reshape(rows, model), adapter_down_weight, adapter_up_weight,
        query.reshape(rows, width), key.reshape(rows, width),
        value.reshape(rows, width), output_gradient.reshape(rows, width),
    )
    out = pl.pallas_call(
        write_out,
        out_shape=shapes,
        in_specs=[vmem] * 5,
        out_specs=[hbm] * 5,
        scratch_shapes=[dma((5,))],
    )(*[pltpu.with_memory_space_constraint(part, pltpu.VMEM) for part in out])
    return tuple(part.reshape(1, rows, width) for part in out[:3]) + tuple(out[3:])


def solution(mesh):
    fused = fits(mesh.shape["seq"], mesh.shape["dp"])
    chosen = fast if fused else local
    return jax.shard_map(
        chosen,
        mesh=mesh,
        in_specs=(
            P("dp", "seq", None),
            P(),
            P(),
            P("dp", "seq", None),
            P("dp", "seq", None),
            P("dp", "seq", None),
            P("dp", "seq", None),
        ),
        out_specs=(
            P("dp", "seq", None),
            P("dp", "seq", None),
            P("dp", "seq", None),
            P("dp", None),
            P("dp", None),
        ),
        check_vma=False,
    )
```

```python
import functools
import math

import jax
import jax.numpy as jnp
from jax import lax
from jax.experimental import pallas as pl
from jax.experimental.pallas import tpu as pltpu
from jax.sharding import PartitionSpec as P

HEAD_SIZE = 128
LOCAL_HEADS = 1


def entering(part, axis, combine, identity, reverse):
    count = lax.axis_size(axis)
    place = lax.axis_index(axis)
    ahead = count - 1 - place if reverse else place
    gathered = lax.all_gather(part, axis)
    state = jnp.zeros_like(part) + jnp.asarray(identity, part.dtype)

    def one(turn, state):
        source = count - 1 - turn if reverse else turn
        return combine(state, lax.dynamic_index_in_dim(gathered, source, 0, False))

    return lax.fori_loop(0, ahead, one, state)


def add_states(earlier, later):
    return earlier + later


def rounded_values(array):
    return array.astype(jnp.bfloat16)


def local(inputs, adapter_down_weight, adapter_up_weight, query, key, value, output_gradient):
    rows = query.shape[1]
    width = query.shape[2]
    seq_count = lax.axis_size("seq")
    dp_count = lax.axis_size("dp")
    length = rows * seq_count
    factor = 1.0 / math.sqrt(HEAD_SIZE * length)
    queries = query.reshape(rows, LOCAL_HEADS, HEAD_SIZE)
    keys = key.reshape(rows, LOCAL_HEADS, HEAD_SIZE)
    values = value.reshape(rows, LOCAL_HEADS, HEAD_SIZE)
    grads_out = output_gradient.reshape(rows, LOCAL_HEADS, HEAD_SIZE)
    kv_state = jnp.einsum("thi,thj->hij", keys, values, preferred_element_type=jnp.float32)
    qg_state = jnp.einsum("thi,thj->hij", queries, grads_out, preferred_element_type=jnp.float32)
    zeros = jnp.zeros_like(kv_state)
    prefix = entering(kv_state, "seq", add_states, zeros, False)
    suffix = entering(qg_state, "seq", add_states, zeros, True)
    prefix = rounded_values(prefix)
    suffix = rounded_values(suffix)
    rows_idx = lax.broadcasted_iota(jnp.int32, (rows, rows), 0)
    cols_idx = lax.broadcasted_iota(jnp.int32, (rows, rows), 1)
    causal = rows_idx >= cols_idx
    grad_scores = rounded_values(
        jnp.where(
            causal,
            jnp.einsum("thj,shj->hts", grads_out, values, preferred_element_type=jnp.float32),
            0.0,
        )
    )
    scores = rounded_values(
        jnp.where(
            causal,
            jnp.einsum("thi,shi->hts", queries, keys, preferred_element_type=jnp.float32),
            0.0,
        )
    )
    query_grad = jnp.einsum(
        "hts,shi->thi", grad_scores, keys, preferred_element_type=jnp.float32
    ) + jnp.einsum("thj,hij->thi", grads_out, prefix, preferred_element_type=jnp.float32)
    key_grad = jnp.einsum(
        "hts,thi->shi", grad_scores, queries, preferred_element_type=jnp.float32
    ) + jnp.einsum("shj,hij->shi", values, suffix, preferred_element_type=jnp.float32)
    value_grad = jnp.einsum(
        "hts,thj->shj", scores, grads_out, preferred_element_type=jnp.float32
    ) + jnp.einsum("shi,hij->shj", keys, suffix, preferred_element_type=jnp.float32)
    query_grad = rounded_values(factor * query_grad).reshape(rows, width)
    key_grad = rounded_values(factor * key_grad).reshape(rows, width)
    value_grad = rounded_values(factor * value_grad).reshape(rows, width)
    flattened = inputs.reshape(rows, inputs.shape[2])
    gradient_list = jnp.concatenate([query_grad, key_grad, value_grad], axis=1)
    low_rank_state = rounded_values(
        jnp.dot(flattened, adapter_down_weight, preferred_element_type=jnp.float32)
    )
    low_rank_gradient = rounded_values(
        jnp.dot(gradient_list, adapter_up_weight, preferred_element_type=jnp.float32)
    )
    inverse = 1.0 / math.sqrt(length * dp_count)
    contract = (((0,), (0,)), ((), ()))
    down_part = lax.psum_scatter(
        lax.dot_general(flattened, low_rank_gradient, contract, preferred_element_type=jnp.float32)
        * inverse,
        "dp",
        scatter_dimension=0,
        tiled=True,
    )
    up_term = (
        lax.dot_general(gradient_list, low_rank_state, contract, preferred_element_type=jnp.float32)
        * inverse
    )
    up_part = lax.psum_scatter(up_term, "dp", scatter_dimension=0, tiled=True)
    down_grad, up_grad = lax.psum((down_part, up_part), "seq")
    return (
        query_grad.reshape(1, rows, width),
        key_grad.reshape(1, rows, width),
        value_grad.reshape(1, rows, width),
        down_grad,
        up_grad,
    )


MESH = pl.DeviceIdType.MESH
CORES = 2
LINE = 4
KINDS = 10
Y, X, ZI, ZM, ZF, ZO, B, F, ZL, D = range(KINDS)
OPS = (
    "y_send", "x_send", "x_first", "y_second", "z_first", "z_join", "z_in", "z_own", "z_mid",
    "z_out", "relay", "forward", "p_low", "p_get", "p_send", "far", "near",
)
UNITS = 128
CUTS = (
    (
        (3, 3, 0, 0), (7, 5, 2, 0), (5, 4, 1, 0), (4, 0, 3, 0), (2, 0, 2, 0), (3, 0, 2, 0),
        (7, 6, 0, 0), (0, 0, 0, 0), (3, 2, 0, 0), (3, 2, 0, 0), (3, 1, 0, 0), (7, 0, 0, 0),
        (5, 6, 0, 0), (3, 1, 3, 0), (2, 0, 1, 0), (11, 0, 0, 0), (3, 4, 0, 0), (6, 3, 0, 0),
        (3, 0, 0, 0), (12, 2, 0, 0),
    ),
    (
        (10, 6, 0, 1), (14, 6, 1, 0), (6, 4, 1, 0), (2, 2, 2, 0), (3, 6, 1, 0), (9, 2, 2, 0),
        (10, 1, 0, 0), (16, 0, 0, 1), (2, 3, 3, 0), (5, 2, 0, 0), (5, 0, 0, 0), (5, 1, 0, 1),
        (4, 6, 0, 0), (5, 6, 0, 0), (9, 3, 2, 0), (9, 4, 3, 0), (3, 0, 0, 0), (0, 0, 0, 0),
        (3, 2, 2, 0), (2, 5, 0, 0), (2, 0, 2, 0), (15, 1, 2, 0), (4, 2, 2, 0), (5, 5, 2, 1),
        (16, 0, 0, 0),
    ),
)
ORDERS = (
    (
        512, 266, 513, 269, 3, 4, 5, 7, 11, 529, 14, 15, 394, 1536, 397, 642, 1664, 1800, 1801, 1811,
        131, 132, 133, 135, 18, 139, 646, 142, 776, 777, 652, 143, 787, 778, 771, 781, 772, 773, 656, 775,
        130, 779, 146, 390, 782, 396, 144, 783, 770, 786, 774, 780, 784, 1288, 1289, 1280, 1299, 1290, 1281, 1284,
        1285, 1297, 1287, 1291, 1409, 1412, 1413, 1295, 1298, 1286, 1292, 1296,
    ),
    (
        520, 526, 531, 535, 262, 267, 277, 7, 1536, 1664, 1795, 1797, 1801, 1810, 1814, 390, 395, 405, 771, 640,
        773, 135, 777, 10, 786, 790, 16, 774, 17, 779, 20, 24, 789, 641, 384, 138, 144, 642, 145, 148,
        644, 775, 652, 152, 653, 768, 385, 778, 784, 130, 785, 788, 655, 1283, 388, 396, 1285, 792, 1289, 1298,
        769, 397, 1302, 770, 1411, 143, 772, 780, 1286, 1413, 1291, 1426, 1299, 781, 1430, 783, 1301, 1931, 1294, 1303,
        1287, 1280, 1290, 1429, 1296, 1297, 1422, 1300, 1431, 1927, 1304, 1920, 1428, 1292, 1293,
    ),
    (
        514, 266, 269, 3, 4, 518, 5, 7, 11, 14, 15, 524, 394, 1536, 397, 640, 1664, 1800, 1801, 1811,
        131, 132, 133, 135, 528, 641, 18, 139, 142, 657, 143, 909, 899, 128, 146, 385, 1032, 1033, 145, 1024,
        1043, 1034, 1025, 1160, 1028, 1161, 1155, 1029, 1041, 1031, 1165, 1035, 1038, 1152, 1171, 1162, 1153, 1039, 1156, 1026,
        1157, 1042, 1169, 1030, 1159, 1036, 1040, 1163, 1166, 1167, 1154, 1170, 1158, 1422, 1164, 1168, 1410,
    ),
    (
        512, 513, 262, 267, 277, 7, 1536, 648, 1664, 1795, 1797, 1801, 1810, 1814, 390, 395, 514, 405, 516, 654,
        524, 659, 135, 136, 525, 663, 1027, 527, 10, 16, 403, 17, 1029, 1033, 1042, 1046, 20, 24, 1155, 142,
        1032, 1030, 138, 1035, 407, 144, 1043, 145, 1157, 148, 1045, 1161, 1170, 1038, 1174, 1160, 1158, 152, 1047, 1163,
        1031, 1171, 1024, 1173, 1034, 1040, 1166, 1041, 1175, 1044, 1931, 1048, 1159, 1025, 1152, 1026, 1028, 1162, 1036, 1168,
        1169, 1037, 1172, 1927, 1039, 1920, 1176, 1153, 1154, 1156, 1164, 1165, 1167, 1409, 1410, 1412, 1943,
    ),
)


def lanes(n):
    return -(-n // 128) * 128


def lent(shard):
    return shard // UNITS * sum(parts for parts, _, _, moved in CUTS[1] if moved)


def fetched(shard, core):
    return lanes(shard // UNITS * sum(parts for parts, color, _, _ in CUTS[core] if color == 2))


def cut(shard, ushard, core):
    table, unit, room = CUTS[core], shard // UNITS, lanes(lent(shard))
    places, off = {}, 0
    for i in sorted(range(len(table)), key=lambda i: (table[i][3], table[i][1] != 2)):
        if table[i][3] and off < shard + room - lent(shard):
            off = shard + room - lent(shard)
        places[i] = off
        off += table[i][0] * unit
    return [
        (places[i], parts * unit, color, mode, moved) if parts else (shard + room, ushard, color, mode, moved)
        for i, (parts, color, mode, moved) in enumerate(table)
    ]


def working(color):
    return {3: ("inner",), 5: ("inner",), 4: ("outer",), 6: ("outer",)}.get(color, ("outer", "inner"))


def direct(color, mode):
    return mode == 3 and color < 3


def landing(pieces):
    slots = {}
    for i, (_, _, color, mode, moved) in enumerate(pieces):
        for kind in (Y, X, ZI, ZM):
            slots[kind, i] = len(slots)
        if color >= 3:
            slots[ZL, i] = len(slots)
        if mode in (0, 2):
            slots[ZO, i] = slots[ZI, i]
        if mode == 1:
            slots[B, i] = len(slots)
        if mode == 2:
            slots[B, i] = slots[ZM, i]
        if direct(color, mode):
            slots[ZF, i] = len(slots)
        if moved:
            for kind, modes in ((ZO, (1, 3)), (B, (0, 3)), (F, (1, 2, 3))):
                if mode in modes:
                    slots[kind, i] = len(slots)
    return slots


def fits(seq_count, dp_count):
    return dp_count == 2 * CORES and seq_count == 2 * LINE


def dot(a, b, da, db):
    return lax.dot_general(a, b, (((da,), (db,)), ((), ())), preferred_element_type=jnp.float32)


def fused_kernel(
    depth, factor, inverse,
    x_hbm, w_hbm, u_hbm, q_hbm, k_hbm, v_hbm, g_hbm,
    qo_ref, ko_ref, vo_ref, down_ref, up_ref,
    x_ref, w_ref, u_ref, four_ref, xs_ref, xr_ref, xt_ref,
    st_ref, pair_ref, kvr_ref, qgr_ref, ox_ref, sxs_ref, sxr_ref, lead_ref,
    ls_ref, lr_ref, ups_ref, upr_ref, fg_ref,
    ys_ref, yr_ref, acc_ref, xrs_ref, zs_ref, zr_ref, zm_ref, zf_ref, zl_ref,
    ps_ref, pr_ref, pt_ref, lo_ref, them_ref, xes_ref, xer_ref, lent_ref, pre_s, pre_r,
    load_sem, core_s, core_r, scan_s, scan_r, sx_s, sx_r,
    send_s, hop_r,
):
    seq = lax.axis_index("seq")
    dp = lax.axis_index("dp")
    z, x = seq // 2, seq % 2
    y, c = dp // CORES, dp % CORES
    mate = {"seq": seq, "dp": y * CORES + (1 - c)}
    across = {"seq": seq, "dp": (1 - y) * CORES + c}
    apart = {"seq": seq, "dp": (1 - y) * CORES + (1 - c)}
    beside = {"seq": z * 2 + (1 - x), "dp": dp}

    near = jnp.where(z % 3 == 0, z + 1 - 2 * (z // 3), 3 * (z // 2))
    diagonal = {"seq": near * 2 + (1 - x), "dp": dp}

    def along(other):
        return {"seq": other * 2 + x, "dp": dp}

    for i, part in enumerate((q_hbm, k_hbm, v_hbm, g_hbm)):
        pltpu.make_async_copy(part, four_ref.at[i], load_sem.at[2]).start()
    load_u = pltpu.make_async_copy(u_hbm, u_ref, load_sem.at[3])
    load_x = pltpu.make_async_copy(x_hbm, x_ref, load_sem.at[0])
    load_w = pltpu.make_async_copy(w_hbm, w_ref, load_sem.at[1])
    load_u.start()
    load_x.start()
    load_w.start()

    barrier = pltpu.get_barrier_semaphore()
    friends = [mate, across, apart, beside, diagonal] + [along(lax.rem(z + d, depth)) for d in range(1, depth)]
    for friend in friends:
        pl.semaphore_signal(barrier, inc=1, device_id=friend, device_id_type=MESH)

    rows, width = qo_ref.shape
    shard = down_ref.shape[0]
    ushard = up_ref.shape[0]
    early = [fetched(shard, core) for core in range(CORES)]
    moved_rows = lent(shard)
    room = lanes(moved_rows)
    base = shard + room
    pltpu.make_async_copy(four_ref, four_ref, load_sem.at[2]).wait()
    q, k, v, g = four_ref[0], four_ref[1], four_ref[2], four_ref[3]
    st_ref[0] = dot(k, v, 0, 0)
    st_ref[1] = dot(q, g, 0, 0)
    pl.semaphore_wait(barrier, len(friends))

    def remote(src, dst, ssem, rsem, where):
        return pltpu.make_async_remote_copy(
            src_ref=src, dst_ref=dst, send_sem=ssem, recv_sem=rsem, device_id=where, device_id_type=MESH
        )

    lead = width // 2
    first, second = slice(0, lead), slice(lead, width)
    other = remote(st_ref.at[:, second, :], ox_ref, sx_s.at[1], sx_r.at[1], beside)
    other.start()

    def scan(source, part, at):
        ups, downs = [], []
        for d in range(1, depth):
            slot = at * (depth - 1) + d - 1
            back = at * (depth - 1) + depth - d - 1
            ups.append(remote(source.at[0, part, :], kvr_ref.at[d - 1, part, :], scan_s.at[0], scan_r.at[slot], along(lax.rem(z + d, depth))))
            downs.append(remote(source.at[1, part, :], qgr_ref.at[d - 1, part, :], scan_s.at[0], scan_r.at[back], along(lax.rem(z - d + depth, depth))))
        for d in range(1, depth):
            pl.when(z + d < depth)(ups[d - 1].start)
            pl.when(z >= d)(downs[d - 1].start)
        return ups, downs

    def collect(scans, part, which):
        sxs_ref[which, part, :] = jnp.zeros((lead, width), jnp.float32)
        for d in range(1, depth):
            @pl.when(z + d < depth if which else z >= d)
            def _(d=d):
                scans[which][d - 1].wait_recv()
                sxs_ref[which, part, :] += (kvr_ref, qgr_ref)[which][d - 1, part, :]

    scan_a = scan(st_ref, first, 0)

    load_x.wait()
    core_copies, extra = [], []
    for core in range(CORES):
        if early[core]:
            cols = pl.ds(pl.multiple_of(((1 - y) * CORES + core) * shard, 128), early[core])
            mine = ps_ref.at[core, :, 0 : early[core]]
            mine[...] = x_ref[:, cols].astype(jnp.float32)
            where = {"seq": seq, "dp": (1 - y) * CORES + core}
            copy = remote(mine, pr_ref.at[c, :, 0 : early[core]], pre_s.at[core], pre_r.at[c], where)
            copy.start()
            extra.append(copy)
    if room:
        for part in range(2):
            xes_ref[part] = x_ref[:, (part * CORES + 1) * shard - room : (part * CORES + 1) * shard].astype(jnp.float32)
        lend = remote(xes_ref, xer_ref, pre_s.at[4], pre_r.at[4], mate)
        pl.when(c == 0)(lend.start)
    for part in range(2):
        cols = pl.ds(pl.multiple_of((part * CORES + 1 - c) * shard, 128), shard)
        xs_ref[part] = x_ref[:, cols].astype(jnp.float32)
        copy = remote(xs_ref.at[part], xr_ref.at[part], core_s.at[part], core_r.at[part], mate)
        copy.start()
        core_copies.append(copy)

    other.wait_recv()
    pair_ref[:, second, :] = st_ref[:, second, :] + ox_ref[...]
    scan_b = scan(pair_ref, second, 1)

    r_idx = lax.broadcasted_iota(jnp.int32, (rows, rows), 0)
    c_idx = lax.broadcasted_iota(jnp.int32, (rows, rows), 1)
    causal = r_idx >= c_idx
    gs = jnp.where(causal, dot(g, v, 1, 1), 0.0).astype(jnp.bfloat16)
    sc = jnp.where(causal, dot(q, k, 1, 1), 0.0).astype(jnp.bfloat16)
    q_in = dot(gs, k, 1, 0)
    k_in = dot(gs, q, 0, 0)
    v_in = dot(sc, g, 0, 0)

    for part in range(2):
        cols = pl.ds(pl.multiple_of((part * CORES + c) * shard, 128), shard)
        xt_ref[part, 0:shard, 0:rows] = x_ref[:, cols].T

    load_w.wait()
    low = jnp.dot(x_ref[...], w_ref[...], preferred_element_type=jnp.float32).astype(jnp.bfloat16)

    swaps = [
        remote(sxs_ref.at[which, first, :], sxr_ref.at[which], sx_s.at[2 * which], sx_r.at[2 * which], beside)
        for which in range(2)
    ]

    def settle(which):
        collect(scan_a, first, which)
        lead_ref[which] = sxs_ref[which, first, :]

        @pl.when(x == which)
        def _():
            sxs_ref[which, first, :] += st_ref[which, first, :]

        swaps[which].start()

    for here, turns in ((z < depth // 2, (0, 1)), (z >= depth // 2, (1, 0))):
        @pl.when(here)
        def _(turns=turns):
            for which in turns:
                settle(which)

    for part in range(2):
        core_copies[part].wait_recv()
        xt_ref[part, 0:shard, rows:] = xr_ref[part].astype(jnp.bfloat16).T

    if room:
        @pl.when(c == 1)
        def _():
            lend.wait_recv()
            for part in range(2):
                xt_ref[part, shard:base, 0:rows] = x_ref[:, (part * CORES + 1) * shard - room : (part * CORES + 1) * shard].T
                xt_ref[part, shard:base, rows:] = xer_ref[part].astype(jnp.bfloat16).T

    for which in range(2):
        collect(scan_b, second, which)

    @pl.when(x == 1)
    def _():
        sxs_ref[0, second, :] += ox_ref[0]

    @pl.when(x == 0)
    def _():
        sxs_ref[1, second, :] += ox_ref[1]

    for swap in swaps:
        swap.wait_recv()
    states = jnp.concatenate([lead_ref[...] + sxr_ref[...], sxs_ref[:, second, :]], axis=1).astype(jnp.bfloat16)
    prefix, suffix = states[0], states[1]
    q_grad = (factor * (q_in + dot(g, prefix, 1, 1))).astype(jnp.bfloat16)
    k_grad = (factor * (k_in + dot(v, suffix, 1, 1))).astype(jnp.bfloat16)
    v_grad = (factor * (v_in + dot(k, suffix, 1, 0))).astype(jnp.bfloat16)
    fg = jnp.concatenate([q_grad, k_grad, v_grad], axis=1)
    load_u.wait()
    low_grad = dot(fg, u_ref[...], 1, 0).astype(jnp.bfloat16)
    ls_ref[...] = low_grad.astype(jnp.float32)
    low_copy = remote(ls_ref, lr_ref, core_s.at[2], core_r.at[2], mate)
    low_copy.start()
    if sum(early):
        low_across = remote(ls_ref, lo_ref.at[c], pre_s.at[2], pre_r.at[2], across)
        low_across.start()
        low_apart = remote(lo_ref.at[c], lo_ref.at[c], pre_s.at[3], pre_r.at[3], mate)
        extra.append(low_across)
    qo_ref[...] = q_grad
    ko_ref[...] = k_grad
    vo_ref[...] = v_grad

    low_copy.wait_recv()
    both = jnp.concatenate([low_grad, lr_ref[...].astype(jnp.bfloat16)], axis=0)

    outer = (z == 0) | (z == depth - 1)
    inner = jnp.logical_not(outer)
    mid = jnp.where(z < depth // 2, depth // 2 - 1, depth // 2)
    end = jnp.where(z < depth // 2, 0, depth - 1)
    inward, outward, opposite = along(mid), along(end), along(depth - 1 - z)
    further = along(depth - 1 - mid)
    corner = {"seq": end * 2 + (1 - x), "dp": dp}
    cuts = [cut(shard, ushard, core) for core in range(CORES)]
    landings = [landing(pieces) for pieces in cuts]
    last = max(len(slots) for slots in landings)
    sent = {}
    pieces, slots = [], {}

    def send(role, kind, i, src, dst, where):
        sent[kind] = sent.get(kind, 0) + src.shape[0]
        at = slots.get((kind, i), last)
        remote(src, dst, send_s.at[kind], hop_r.at[at], where).start()

    def arrived(kind, i, like):
        remote(like, like, send_s.at[kind], hop_r.at[slots[kind, i]], mate).wait_recv()

    def partial(i, part):
        off, n = pieces[i][:2]
        if off < base:
            return jnp.dot(xt_ref[part, off : off + n, :], both, preferred_element_type=jnp.float32)
        mine = pl.ds(pl.multiple_of((part * CORES + c) * ushard, 8), ushard)
        return fg_ref[mine, :] + upr_ref[part]

    def half(i, which):
        off, n = pieces[i][:2]
        return pl.ds(pl.multiple_of(off + which * (n // 2), 8), n // 2)

    def short(i):
        off, n = pieces[i][:2]
        return slice(off // 2, off // 2 + n // 2)

    def place(i, which):
        off, n = pieces[i][:2]
        ref, start = (up_ref, 0) if off >= base else (lent_ref, off - shard) if off >= shard else (down_ref, off)
        return ref.at[pl.ds(pl.multiple_of(start + which * (n // 2), 8), n // 2), :]

    def deliver(role, i, which):
        off, n, _, _, moved = pieces[i]
        if moved:
            h = n // 2
            home = down_ref.at[pl.ds(pl.multiple_of(off - room + which * h, 8), h), :]
            sent[D] = sent.get(D, 0) + h
            remote(place(i, which), home, send_s.at[D], hop_r.at[last + 1], mate).start()

    def perform(role, core, op, i):
        off, n, color, mode, moved = pieces[i]
        h = n // 2
        first_x = color in (1, 5, 6)
        workers = working(color)
        whole, low_half, high_half = slice(off, off + n), slice(off, off + h), slice(off + h, off + n)
        small = short(i)
        landed = Y if first_x else X
        if op == "y_send":
            if off >= base:
                up_copy.wait_recv()
            ys_ref[whole, :] = partial(i, 1 - y)
            send(role, Y, i, ys_ref.at[whole, :], yr_ref.at[whole, :], across)
        elif op == "z_first":
            where = inward if role == "outer" else outward
            ys_ref[whole, :] = partial(i, 1 - y)
            send(role, ZL, i, ys_ref.at[whole, :], zl_ref.at[0, whole, :], where)
            acc_ref[whole, :] = partial(i, y)
            send(role, ZL, i, acc_ref.at[whole, :], zl_ref.at[1, whole, :], where)
        elif op == "z_join":
            arrived(ZL, i, zl_ref.at[:, whole, :])
            ys_ref[whole, :] = partial(i, 1 - y) + zl_ref[0, whole, :]
            if first_x:
                send(role, X, i, ys_ref.at[half(i, 1 - x), :], yr_ref.at[high_half, :], beside)
                acc_ref[whole, :] = partial(i, y) + zl_ref[1, whole, :]
                send(role, X, i, acc_ref.at[half(i, 1 - x), :], yr_ref.at[low_half, :], beside)
            else:
                send(role, Y, i, ys_ref.at[whole, :], yr_ref.at[whole, :], across)
        elif op == "p_low":
            low_across.wait_recv()
            if early[1 - core]:
                low_apart.start()
        elif op == "p_get":
            remote(ls_ref, ls_ref, pre_s.at[3], pre_r.at[3], mate).wait_recv()
            for at in range(2):
                theirs = pr_ref.at[at, :, 0 : early[core]]
                remote(theirs, theirs, pre_s.at[at], pre_r.at[at], mate).wait_recv()
                pt_ref[0 : early[core], at * rows : (at + 1) * rows] = theirs[...].astype(jnp.bfloat16).T
                them_ref[at * rows : (at + 1) * rows, :] = lo_ref[at].astype(jnp.bfloat16)
        elif op == "p_send":
            acc_ref[whole, :] = partial(i, y) + jnp.dot(
                pt_ref[whole, :], them_ref[...], preferred_element_type=jnp.float32
            )
            send(role, X, i, acc_ref.at[half(i, 1 - x), :], xrs_ref.at[small, :], beside)
        elif op == "x_send":
            own = partial(i, y)
            if color >= 3:
                own = own + zl_ref[1, whole, :]
            arrived(Y, i, yr_ref.at[whole, :])
            acc_ref[whole, :] = own + yr_ref[whole, :]
            send(role, X, i, acc_ref.at[half(i, 1 - x), :], xrs_ref.at[small, :], beside)
        elif op == "x_first":
            ys_ref[whole, :] = partial(i, 1 - y)
            send(role, X, i, ys_ref.at[half(i, 1 - x), :], yr_ref.at[high_half, :], beside)
            acc_ref[whole, :] = partial(i, y)
            send(role, X, i, acc_ref.at[half(i, 1 - x), :], yr_ref.at[low_half, :], beside)
        elif op == "y_second":
            arrived(X, i, yr_ref.at[whole, :])
            ys_ref[half(i, x), :] += yr_ref[high_half, :]
            send(role, Y, i, ys_ref.at[half(i, x), :], xrs_ref.at[small, :], across)
            acc_ref[half(i, x), :] += yr_ref[low_half, :]
        elif op == "z_in":
            arrived(landed, i, xrs_ref.at[small, :])
            zs_ref[small, :] = acc_ref[half(i, x), :] + xrs_ref[small, :]
            send(role, ZI, i, zs_ref.at[small, :], zr_ref.at[small, :], inward)
            if direct(color, mode):
                send(role, ZF, i, zs_ref.at[small, :], zf_ref.at[small, :], further)
        elif op == "z_own":
            arrived(landed, i, xrs_ref.at[small, :])
            zs_ref[small, :] = acc_ref[half(i, x), :] + xrs_ref[small, :]
            send(role, ZM, i, zs_ref.at[small, :], zm_ref.at[small, :], opposite)
        elif op == "z_mid":
            if "inner" in workers:
                arrived(landed, i, xrs_ref.at[small, :])
                own = acc_ref[half(i, x), :] + xrs_ref[small, :]
            if "outer" in workers:
                arrived(ZI, i, zr_ref.at[small, :])
                own = own + zr_ref[small, :] if "inner" in workers else zr_ref[small, :]
            zs_ref[small, :] = own
            send(role, ZM, i, zs_ref.at[small, :], zm_ref.at[small, :], opposite)
        elif op == "z_out":
            own = zs_ref[small, :]
            if direct(color, mode):
                arrived(ZI, i, zr_ref.at[small, :])
                own = own + zr_ref[small, :]
            arrived(ZM, i, zm_ref.at[small, :])
            own = own + zm_ref[small, :]
            if direct(color, mode):
                arrived(ZF, i, zf_ref.at[small, :])
                own = own + zf_ref[small, :]
            spot = place(i, x)
            spot[...] = own * inverse
            if mode == 3:
                send(role, F, i, spot, spot, corner)
            if mode in (0, 1, 3):
                send(role, B, i, spot, spot, beside)
            send(role, ZO, i, spot, spot, outward)
            deliver(role, i, x)
        elif op == "relay":
            spot = place(i, x)
            arrived(ZO, i, spot)
            send(role, B, i, spot, spot, beside)
            deliver(role, i, x)
        elif op == "forward":
            spot = place(i, 1 - x)
            arrived(B, i, spot)
            send(role, F, i, spot, spot, outward if role == "inner" else inward)
            deliver(role, i, 1 - x)
        elif op == "near":
            arrived(ZO, i, place(i, x))
            deliver(role, i, x)
        elif op == "far":
            arrived(B if mode == 0 or (mode == 3 and role == "inner") else F, i, place(i, 1 - x))
            deliver(role, i, 1 - x)

    up_all = dot(fg, low, 0, 0)
    fg_ref[...] = up_all
    for part in range(2):
        rng = pl.ds(pl.multiple_of((part * CORES + 1 - c) * ushard, 8), ushard)
        ups_ref[part] = fg_ref[rng, :]
    up_copy = remote(ups_ref, upr_ref, core_s.at[3], core_r.at[3], mate)
    up_copy.start()

    for role, here in (("outer", outer), ("inner", inner)):
        for core in range(CORES):
            @pl.when(here & (c == core))
            def _(role=role, core=core):
                sent.clear()
                slots.clear()
                slots.update(landings[core])
                pieces[:] = cuts[core]
                for code in ORDERS[2 * (role == "inner") + core]:
                    perform(role, core, OPS[code // UNITS], code % UNITS)
                late = 0
                for _, n, _, mode, moved in pieces:
                    if not moved:
                        late += n // 2 * (mode in (1, 3) and role == "outer")
                        late += n // 2 * ((role, mode) not in (("outer", 2), ("inner", 1)))
                for rows_in, at in ((late, last), ((1 - core) * moved_rows, last + 1)):
                    if rows_in:
                        like = ys_ref.at[0:rows_in, :]
                        remote(like, like, send_s.at[0], hop_r.at[at], mate).wait_recv()
                for kind, rows_out in list(sent.items()):
                    like = zl_ref.at[:, 0 : rows_out // 2, :] if kind == ZL else ys_ref.at[0:rows_out, :]
                    remote(like, like, send_s.at[kind], hop_r.at[last], mate).wait_send()
                if early[1 - core]:
                    low_apart.wait_send()
                if room and core == 0:
                    lend.wait_send()

    remote(kvr_ref, kvr_ref, scan_s.at[0], scan_r.at[0], mate).wait_send()
    for copy in core_copies + swaps + [other, low_copy, up_copy] + extra:
        copy.wait_send()


def write_out(*refs):
    copies = [pltpu.make_async_copy(refs[i], refs[5 + i], refs[10].at[i]) for i in range(5)]
    for copy in copies:
        copy.start()
    for copy in copies:
        copy.wait()


def fast(inputs, adapter_down_weight, adapter_up_weight, query, key, value, output_gradient):
    rows, width = query.shape[1:]
    model = inputs.shape[2]
    rank = adapter_down_weight.shape[1]
    features = adapter_up_weight.shape[0]
    seq_count = lax.axis_size("seq")
    dp_count = lax.axis_size("dp")
    length = rows * seq_count
    factor = 1.0 / math.sqrt(HEAD_SIZE * length)
    inverse = 1.0 / math.sqrt(length * dp_count)
    depth = seq_count // 2
    shard, ushard = model // dp_count, features // dp_count
    room = lanes(lent(shard))
    total = shard + room + ushard
    slots = max(len(landing(cut(shard, ushard, core))) for core in range(CORES))
    early = max([fetched(shard, core) for core in range(CORES)] + [128])
    spare = max(room, 128)
    f32, bf16 = jnp.float32, jnp.bfloat16
    dma = pltpu.SemaphoreType.DMA
    vmem = pl.BlockSpec(memory_space=pltpu.VMEM)
    hbm = pl.BlockSpec(memory_space=pl.ANY)
    shapes = [jax.ShapeDtypeStruct((rows, width), bf16)] * 3 + [
        jax.ShapeDtypeStruct((shard, rank), f32),
        jax.ShapeDtypeStruct((ushard, rank), f32),
    ]
    out = pl.pallas_call(
        functools.partial(fused_kernel, depth, factor, inverse),
        out_shape=[pltpu.VMEM(part.shape, part.dtype) for part in shapes],
        in_specs=[hbm] * 7,
        out_specs=[vmem] * 5,
        scratch_shapes=[
            pltpu.VMEM((rows, model), bf16),
            pltpu.VMEM((model, rank), bf16),
            pltpu.VMEM((features, rank), bf16),
            pltpu.VMEM((4, rows, width), bf16),
            pltpu.VMEM((2, rows, shard), f32),
            pltpu.VMEM((2, rows, shard), f32),
            pltpu.VMEM((2, shard + room, 2 * rows), bf16),
            pltpu.VMEM((2, width, width), f32),
            pltpu.VMEM((2, width, width), f32),
            pltpu.VMEM((depth - 1, width, width), f32),
            pltpu.VMEM((depth - 1, width, width), f32),
            pltpu.VMEM((2, width // 2, width), f32),
            pltpu.VMEM((2, width, width), f32),
            pltpu.VMEM((2, width // 2, width), f32),
            pltpu.VMEM((2, width // 2, width), f32),
            pltpu.VMEM((rows, rank), f32),
            pltpu.VMEM((rows, rank), f32),
            pltpu.VMEM((2, ushard, rank), f32),
            pltpu.VMEM((2, ushard, rank), f32),
            pltpu.VMEM((features, rank), f32),
            pltpu.VMEM((total, rank), f32),
            pltpu.VMEM((total, rank), f32),
            pltpu.VMEM((total, rank), f32),
            pltpu.VMEM((total // 2, rank), f32),
            pltpu.VMEM((total // 2, rank), f32),
            pltpu.VMEM((total // 2, rank), f32),
            pltpu.VMEM((total // 2, rank), f32),
            pltpu.VMEM((total // 2, rank), f32),
            pltpu.VMEM((2, total, rank), f32),
            pltpu.VMEM((2, rows, early), f32),
            pltpu.VMEM((2, rows, early), f32),
            pltpu.VMEM((early, 2 * rows), bf16),
            pltpu.VMEM((2, rows, rank), f32),
            pltpu.VMEM((2 * rows, rank), bf16),
            pltpu.VMEM((2, rows, spare), f32),
            pltpu.VMEM((2, rows, spare), f32),
            pltpu.VMEM((spare, rank), f32),
            dma((5,)), dma((5,)),
            dma((4,)), dma((4,)), dma((4,)),
            dma((1,)), dma((2 * depth - 2,)),
            dma((3,)), dma((3,)),
            dma((KINDS,)), dma((slots + 2,)),
        ],
        compiler_params=pltpu.CompilerParams(
            collective_id=0, has_side_effects=True
        ),
    )(
        inputs.reshape(rows, model), adapter_down_weight, adapter_up_weight,
        query.reshape(rows, width), key.reshape(rows, width),
        value.reshape(rows, width), output_gradient.reshape(rows, width),
    )
    out = pl.pallas_call(
        write_out,
        out_shape=shapes,
        in_specs=[vmem] * 5,
        out_specs=[hbm] * 5,
        scratch_shapes=[dma((5,))],
    )(*[pltpu.with_memory_space_constraint(part, pltpu.VMEM) for part in out])
    return tuple(part.reshape(1, rows, width) for part in out[:3]) + tuple(out[3:])


def solution(mesh):
    fused = fits(mesh.shape["seq"], mesh.shape["dp"])
    chosen = fast if fused else local
    return jax.shard_map(
        chosen,
        mesh=mesh,
        in_specs=(
            P("dp", "seq", None),
            P(),
            P(),
            P("dp", "seq", None),
            P("dp", "seq", None),
            P("dp", "seq", None),
            P("dp", "seq", None),
        ),
        out_specs=(
            P("dp", "seq", None),
            P("dp", "seq", None),
            P("dp", "seq", None),
            P("dp", None),
            P("dp", None),
        ),
        check_vma=False,
    )
```

```python
import functools
import math

import jax
import jax.numpy as jnp
from jax import lax
from jax.experimental import pallas as pl
from jax.experimental.pallas import tpu as pltpu
from jax.sharding import PartitionSpec as P

HEAD_SIZE = 128
LOCAL_HEADS = 1


def entering(part, axis, combine, identity, reverse):
    count = lax.axis_size(axis)
    place = lax.axis_index(axis)
    ahead = count - 1 - place if reverse else place
    gathered = lax.all_gather(part, axis)
    state = jnp.zeros_like(part) + jnp.asarray(identity, part.dtype)

    def one(turn, state):
        source = count - 1 - turn if reverse else turn
        return combine(state, lax.dynamic_index_in_dim(gathered, source, 0, False))

    return lax.fori_loop(0, ahead, one, state)


def add_states(earlier, later):
    return earlier + later


def rounded_values(array):
    return array.astype(jnp.bfloat16)


def local(inputs, adapter_down_weight, adapter_up_weight, query, key, value, output_gradient):
    rows = query.shape[1]
    width = query.shape[2]
    seq_count = lax.axis_size("seq")
    dp_count = lax.axis_size("dp")
    length = rows * seq_count
    factor = 1.0 / math.sqrt(HEAD_SIZE * length)
    queries = query.reshape(rows, LOCAL_HEADS, HEAD_SIZE)
    keys = key.reshape(rows, LOCAL_HEADS, HEAD_SIZE)
    values = value.reshape(rows, LOCAL_HEADS, HEAD_SIZE)
    grads_out = output_gradient.reshape(rows, LOCAL_HEADS, HEAD_SIZE)
    kv_state = jnp.einsum("thi,thj->hij", keys, values, preferred_element_type=jnp.float32)
    qg_state = jnp.einsum("thi,thj->hij", queries, grads_out, preferred_element_type=jnp.float32)
    zeros = jnp.zeros_like(kv_state)
    prefix = entering(kv_state, "seq", add_states, zeros, False)
    suffix = entering(qg_state, "seq", add_states, zeros, True)
    prefix = rounded_values(prefix)
    suffix = rounded_values(suffix)
    rows_idx = lax.broadcasted_iota(jnp.int32, (rows, rows), 0)
    cols_idx = lax.broadcasted_iota(jnp.int32, (rows, rows), 1)
    causal = rows_idx >= cols_idx
    grad_scores = rounded_values(
        jnp.where(
            causal,
            jnp.einsum("thj,shj->hts", grads_out, values, preferred_element_type=jnp.float32),
            0.0,
        )
    )
    scores = rounded_values(
        jnp.where(
            causal,
            jnp.einsum("thi,shi->hts", queries, keys, preferred_element_type=jnp.float32),
            0.0,
        )
    )
    query_grad = jnp.einsum(
        "hts,shi->thi", grad_scores, keys, preferred_element_type=jnp.float32
    ) + jnp.einsum("thj,hij->thi", grads_out, prefix, preferred_element_type=jnp.float32)
    key_grad = jnp.einsum(
        "hts,thi->shi", grad_scores, queries, preferred_element_type=jnp.float32
    ) + jnp.einsum("shj,hij->shi", values, suffix, preferred_element_type=jnp.float32)
    value_grad = jnp.einsum(
        "hts,thj->shj", scores, grads_out, preferred_element_type=jnp.float32
    ) + jnp.einsum("shi,hij->shj", keys, suffix, preferred_element_type=jnp.float32)
    query_grad = rounded_values(factor * query_grad).reshape(rows, width)
    key_grad = rounded_values(factor * key_grad).reshape(rows, width)
    value_grad = rounded_values(factor * value_grad).reshape(rows, width)
    flattened = inputs.reshape(rows, inputs.shape[2])
    gradient_list = jnp.concatenate([query_grad, key_grad, value_grad], axis=1)
    low_rank_state = rounded_values(
        jnp.dot(flattened, adapter_down_weight, preferred_element_type=jnp.float32)
    )
    low_rank_gradient = rounded_values(
        jnp.dot(gradient_list, adapter_up_weight, preferred_element_type=jnp.float32)
    )
    inverse = 1.0 / math.sqrt(length * dp_count)
    contract = (((0,), (0,)), ((), ()))
    down_part = lax.psum_scatter(
        lax.dot_general(flattened, low_rank_gradient, contract, preferred_element_type=jnp.float32)
        * inverse,
        "dp",
        scatter_dimension=0,
        tiled=True,
    )
    up_term = (
        lax.dot_general(gradient_list, low_rank_state, contract, preferred_element_type=jnp.float32)
        * inverse
    )
    up_part = lax.psum_scatter(up_term, "dp", scatter_dimension=0, tiled=True)
    down_grad, up_grad = lax.psum((down_part, up_part), "seq")
    return (
        query_grad.reshape(1, rows, width),
        key_grad.reshape(1, rows, width),
        value_grad.reshape(1, rows, width),
        down_grad,
        up_grad,
    )


MESH = pl.DeviceIdType.MESH
CORES = 2
LINE = 4
KINDS = 10
Y, X, ZI, ZM, ZF, ZO, B, F, ZL, D = range(KINDS)
OPS = (
    "y_send", "x_send", "x_first", "y_second", "z_first", "z_join", "z_in", "z_own", "z_mid",
    "z_out", "relay", "forward", "p_low", "p_get", "p_send", "far", "near",
)
UNITS = 128
CUTS = (
    (
        (3, 3, 0, 0), (7, 5, 2, 0), (5, 4, 1, 0), (4, 0, 3, 0), (2, 0, 2, 0), (3, 0, 2, 0),
        (7, 6, 0, 0), (0, 0, 0, 0), (3, 2, 0, 0), (3, 2, 0, 0), (3, 1, 0, 0), (7, 0, 0, 0),
        (5, 6, 0, 0), (3, 1, 3, 0), (2, 0, 1, 0), (11, 0, 0, 0), (3, 4, 0, 0), (6, 3, 0, 0),
        (3, 0, 0, 0), (12, 2, 0, 0),
    ),
    (
        (10, 6, 0, 1), (14, 6, 1, 0), (6, 4, 1, 0), (2, 2, 2, 0), (3, 6, 1, 0), (9, 2, 2, 0),
        (10, 1, 0, 0), (16, 0, 0, 1), (2, 3, 3, 0), (5, 2, 0, 0), (5, 0, 0, 0), (5, 1, 0, 1),
        (4, 6, 0, 0), (5, 6, 0, 0), (9, 3, 2, 0), (9, 4, 3, 0), (3, 0, 0, 0), (0, 0, 0, 0),
        (3, 2, 2, 0), (2, 5, 0, 0), (2, 0, 2, 0), (15, 1, 2, 0), (4, 2, 2, 0), (5, 5, 2, 1),
        (16, 0, 0, 0),
    ),
)
ORDERS = (
    (
        512, 266, 513, 269, 3, 4, 5, 7, 11, 529, 14, 15, 394, 1536, 397, 642, 1664, 1800, 1801, 1811,
        131, 132, 133, 135, 18, 139, 646, 142, 776, 777, 652, 143, 787, 778, 771, 781, 772, 773, 656, 775,
        130, 779, 146, 390, 782, 396, 144, 783, 770, 786, 774, 780, 784, 1288, 1289, 1280, 1299, 1290, 1281, 1284,
        1285, 1297, 1287, 1291, 1409, 1412, 1413, 1295, 1298, 1286, 1292, 1296,
    ),
    (
        520, 526, 531, 535, 262, 267, 277, 7, 1536, 1664, 1795, 1797, 1801, 1810, 1814, 390, 395, 405, 771, 640,
        773, 135, 777, 10, 786, 790, 16, 774, 17, 779, 20, 24, 789, 641, 384, 138, 144, 642, 145, 148,
        644, 775, 652, 152, 653, 768, 385, 778, 784, 130, 785, 788, 655, 1283, 388, 396, 1285, 792, 1289, 1298,
        769, 397, 1302, 770, 1411, 143, 772, 780, 1286, 1413, 1291, 1426, 1299, 781, 1430, 783, 1301, 1931, 1294, 1303,
        1287, 1280, 1290, 1429, 1296, 1297, 1422, 1300, 1431, 1927, 1304, 1920, 1428, 1292, 1293,
    ),
    (
        514, 266, 269, 3, 4, 518, 5, 7, 11, 14, 15, 524, 394, 1536, 397, 640, 1664, 1800, 1801, 1811,
        131, 132, 133, 135, 528, 641, 18, 139, 142, 657, 143, 909, 899, 128, 146, 385, 1032, 1033, 145, 1024,
        1043, 1034, 1025, 1160, 1028, 1161, 1155, 1029, 1041, 1031, 1165, 1035, 1038, 1152, 1171, 1162, 1153, 1039, 1156, 1026,
        1157, 1042, 1169, 1030, 1159, 1036, 1040, 1163, 1166, 1167, 1154, 1170, 1158, 1422, 1164, 1168, 1410,
    ),
    (
        512, 513, 262, 267, 277, 7, 1536, 648, 1664, 1795, 1797, 1801, 1810, 1814, 390, 395, 514, 405, 516, 654,
        524, 659, 135, 136, 525, 663, 1027, 527, 10, 16, 403, 17, 1029, 1033, 1042, 1046, 20, 24, 1155, 142,
        1032, 1030, 138, 1035, 407, 144, 1043, 145, 1157, 148, 1045, 1161, 1170, 1038, 1174, 1160, 1158, 152, 1047, 1163,
        1031, 1171, 1024, 1173, 1034, 1040, 1166, 1041, 1175, 1044, 1931, 1048, 1159, 1025, 1152, 1026, 1028, 1162, 1036, 1168,
        1169, 1037, 1172, 1927, 1039, 1920, 1176, 1153, 1154, 1156, 1164, 1165, 1167, 1409, 1410, 1412, 1943,
    ),
)


def lanes(n):
    return -(-n // 128) * 128


def lent(shard):
    return shard // UNITS * sum(parts for parts, _, _, moved in CUTS[1] if moved)


def fetched(shard, core):
    return lanes(shard // UNITS * sum(parts for parts, color, _, _ in CUTS[core] if color == 2))


def cut(shard, ushard, core):
    table, unit, room = CUTS[core], shard // UNITS, lanes(lent(shard))
    places, off = {}, 0
    for i in sorted(range(len(table)), key=lambda i: (table[i][3], table[i][1] != 2)):
        if table[i][3] and off < shard + room - lent(shard):
            off = shard + room - lent(shard)
        places[i] = off
        off += table[i][0] * unit
    return [
        (places[i], parts * unit, color, mode, moved) if parts else (shard + room, ushard, color, mode, moved)
        for i, (parts, color, mode, moved) in enumerate(table)
    ]


def working(color):
    return {3: ("inner",), 5: ("inner",), 4: ("outer",), 6: ("outer",)}.get(color, ("outer", "inner"))


def direct(color, mode):
    return mode == 3 and color < 3


def waits(role, color, mode, moved):
    work = role in working(color)
    kinds = [Y] * (work and color != 2) + [X] * work + [ZL] * (work and color >= 3)
    if role == "inner":
        kinds += [ZM] + [ZI] * ("outer" in working(color)) + [ZF] * direct(color, mode)
        kinds += [B] * (mode == 1 or (moved and mode in (0, 3))) + [F] * (moved and mode == 2)
    else:
        kinds += [ZO] * (mode in (0, 2) or moved)
        kinds += [B] * (mode == 2 or (moved and mode == 0)) + [F] * (moved and mode in (1, 3))
    return kinds


def landing(pieces):
    slots = {}
    for role in ("outer", "inner"):
        spots = [
            (role, kind, i)
            for i, (_, _, color, mode, moved) in enumerate(pieces)
            for kind in waits(role, color, mode, moved)
        ]
        slots.update((spot, at) for at, spot in enumerate(spots))
    return slots


def reached(role, kind):
    if kind in (ZI, ZF):
        return "inner"
    if kind == ZO:
        return "outer"
    if kind in (F, ZL):
        return "outer" if role == "inner" else "inner"
    return role


def fits(seq_count, dp_count):
    return dp_count == 2 * CORES and seq_count == 2 * LINE


def dot(a, b, da, db):
    return lax.dot_general(a, b, (((da,), (db,)), ((), ())), preferred_element_type=jnp.float32)


def fused_kernel(
    depth, factor, inverse,
    x_hbm, w_hbm, u_hbm, q_hbm, k_hbm, v_hbm, g_hbm,
    qo_ref, ko_ref, vo_ref, down_ref, up_ref,
    x_ref, w_ref, u_ref, four_ref, xs_ref, xr_ref, xt_ref,
    st_ref, pair_ref, kvr_ref, qgr_ref, ox_ref, sxs_ref, sxr_ref, lead_ref,
    ls_ref, lr_ref, ups_ref, upr_ref, fg_ref,
    ys_ref, yr_ref, acc_ref, xrs_ref, zs_ref, zr_ref, zm_ref, zf_ref, zl_ref,
    ps_ref, pr_ref, pt_ref, lo_ref, them_ref, xes_ref, xer_ref, lent_ref, pre_s, pre_r,
    load_sem, core_s, core_r, scan_s, scan_r, sx_s, sx_r,
    send_s, hop_r,
):
    seq = lax.axis_index("seq")
    dp = lax.axis_index("dp")
    z, x = seq // 2, seq % 2
    y, c = dp // CORES, dp % CORES
    mate = {"seq": seq, "dp": y * CORES + (1 - c)}
    across = {"seq": seq, "dp": (1 - y) * CORES + c}
    apart = {"seq": seq, "dp": (1 - y) * CORES + (1 - c)}
    beside = {"seq": z * 2 + (1 - x), "dp": dp}

    near = jnp.where(z % 3 == 0, z + 1 - 2 * (z // 3), 3 * (z // 2))
    diagonal = {"seq": near * 2 + (1 - x), "dp": dp}

    def along(other):
        return {"seq": other * 2 + x, "dp": dp}

    for i, part in enumerate((q_hbm, k_hbm, v_hbm, g_hbm)):
        pltpu.make_async_copy(part, four_ref.at[i], load_sem.at[2]).start()
    load_u = pltpu.make_async_copy(u_hbm, u_ref, load_sem.at[3])
    load_x = pltpu.make_async_copy(x_hbm, x_ref, load_sem.at[0])
    load_w = pltpu.make_async_copy(w_hbm, w_ref, load_sem.at[1])
    load_u.start()
    load_x.start()
    load_w.start()

    barrier = pltpu.get_barrier_semaphore()
    friends = [mate, across, apart, beside, diagonal] + [along(lax.rem(z + d, depth)) for d in range(1, depth)]
    for friend in friends:
        pl.semaphore_signal(barrier, inc=1, device_id=friend, device_id_type=MESH)

    rows, width = qo_ref.shape
    shard = down_ref.shape[0]
    ushard = up_ref.shape[0]
    early = [fetched(shard, core) for core in range(CORES)]
    moved_rows = lent(shard)
    room = lanes(moved_rows)
    base = shard + room
    pltpu.make_async_copy(four_ref, four_ref, load_sem.at[2]).wait()
    q, k, v, g = four_ref[0], four_ref[1], four_ref[2], four_ref[3]
    st_ref[0] = dot(k, v, 0, 0)
    st_ref[1] = dot(q, g, 0, 0)
    pl.semaphore_wait(barrier, len(friends))

    def remote(src, dst, ssem, rsem, where):
        return pltpu.make_async_remote_copy(
            src_ref=src, dst_ref=dst, send_sem=ssem, recv_sem=rsem, device_id=where, device_id_type=MESH
        )

    lead = width // 2
    first, second = slice(0, lead), slice(lead, width)
    other = remote(st_ref.at[:, second, :], ox_ref, sx_s.at[1], sx_r.at[1], beside)

    def scan(source, part, at):
        ups, downs = [], []
        for d in range(1, depth):
            slot = at * (depth - 1) + d - 1
            back = at * (depth - 1) + depth - d - 1
            ups.append(remote(source.at[0, part, :], kvr_ref.at[d - 1, part, :], scan_s.at[0], scan_r.at[slot], along(lax.rem(z + d, depth))))
            downs.append(remote(source.at[1, part, :], qgr_ref.at[d - 1, part, :], scan_s.at[0], scan_r.at[back], along(lax.rem(z - d + depth, depth))))
        return ups, downs

    def launch(scans):
        for d in reversed(range(1, depth)):
            pl.when(z + d < depth)(scans[0][d - 1].start)
            pl.when(z >= d)(scans[1][d - 1].start)

    def collect(scans, part, which):
        sxs_ref[which, part, :] = jnp.zeros((lead, width), jnp.float32)
        for d in range(1, depth):
            @pl.when(z + d < depth if which else z >= d)
            def _(d=d):
                scans[which][d - 1].wait_recv()
                sxs_ref[which, part, :] += (kvr_ref, qgr_ref)[which][d - 1, part, :]

    scan_a = scan(st_ref, first, 0)

    def begin():
        other.start()
        launch(scan_a)

    pl.when(c == 0)(begin)
    load_x.wait()
    core_copies, extra = [], []
    for core in range(CORES):
        if early[core]:
            cols = pl.ds(pl.multiple_of(((1 - y) * CORES + core) * shard, 128), early[core])
            mine = ps_ref.at[core, :, 0 : early[core]]
            mine[...] = x_ref[:, cols].astype(jnp.float32)
            where = {"seq": seq, "dp": (1 - y) * CORES + core}
            copy = remote(mine, pr_ref.at[c, :, 0 : early[core]], pre_s.at[core], pre_r.at[c], where)
            copy.start()
            extra.append(copy)
    if room:
        for part in range(2):
            xes_ref[part] = x_ref[:, (part * CORES + 1) * shard - room : (part * CORES + 1) * shard].astype(jnp.float32)
        lend = remote(xes_ref, xer_ref, pre_s.at[4], pre_r.at[4], mate)
        pl.when(c == 0)(lend.start)
    for part in range(2):
        cols = pl.ds(pl.multiple_of((part * CORES + 1 - c) * shard, 128), shard)
        xs_ref[part] = x_ref[:, cols].astype(jnp.float32)
        copy = remote(xs_ref.at[part], xr_ref.at[part], core_s.at[part], core_r.at[part], mate)
        copy.start()
        core_copies.append(copy)

    r_idx = lax.broadcasted_iota(jnp.int32, (rows, rows), 0)
    c_idx = lax.broadcasted_iota(jnp.int32, (rows, rows), 1)
    causal = r_idx >= c_idx
    gs = jnp.where(causal, dot(g, v, 1, 1), 0.0).astype(jnp.bfloat16)
    sc = jnp.where(causal, dot(q, k, 1, 1), 0.0).astype(jnp.bfloat16)
    q_in = dot(gs, k, 1, 0)
    k_in = dot(gs, q, 0, 0)
    v_in = dot(sc, g, 0, 0)

    for part in range(2):
        cols = pl.ds(pl.multiple_of((part * CORES + c) * shard, 128), shard)
        xt_ref[part, 0:shard, 0:rows] = x_ref[:, cols].T

    pl.when(c == 1)(begin)
    load_w.wait()
    low = jnp.dot(x_ref[...], w_ref[...], preferred_element_type=jnp.float32).astype(jnp.bfloat16)

    other.wait_recv()
    pair_ref[:, second, :] = st_ref[:, second, :] + ox_ref[...]
    scan_b = scan(pair_ref, second, 1)
    launch(scan_b)

    swaps = [
        remote(sxs_ref.at[which, first, :], sxr_ref.at[which], sx_s.at[2 * which], sx_r.at[2 * which], beside)
        for which in range(2)
    ]

    def settle(which):
        collect(scan_a, first, which)
        lead_ref[which] = sxs_ref[which, first, :]

        @pl.when(x == which)
        def _():
            sxs_ref[which, first, :] += st_ref[which, first, :]

        swaps[which].start()

    for here, turns in ((z < depth // 2, (0, 1)), (z >= depth // 2, (1, 0))):
        @pl.when(here)
        def _(turns=turns):
            for which in turns:
                settle(which)

    for part in range(2):
        core_copies[part].wait_recv()
        xt_ref[part, 0:shard, rows:] = xr_ref[part].astype(jnp.bfloat16).T

    if room:
        @pl.when(c == 1)
        def _():
            lend.wait_recv()
            for part in range(2):
                xt_ref[part, shard:base, 0:rows] = x_ref[:, (part * CORES + 1) * shard - room : (part * CORES + 1) * shard].T
                xt_ref[part, shard:base, rows:] = xer_ref[part].astype(jnp.bfloat16).T

    for which in range(2):
        collect(scan_b, second, which)

    @pl.when(x == 1)
    def _():
        sxs_ref[0, second, :] += ox_ref[0]

    @pl.when(x == 0)
    def _():
        sxs_ref[1, second, :] += ox_ref[1]

    for swap in swaps:
        swap.wait_recv()
    states = jnp.concatenate([lead_ref[...] + sxr_ref[...], sxs_ref[:, second, :]], axis=1).astype(jnp.bfloat16)
    prefix, suffix = states[0], states[1]
    q_grad = (factor * (q_in + dot(g, prefix, 1, 1))).astype(jnp.bfloat16)
    k_grad = (factor * (k_in + dot(v, suffix, 1, 1))).astype(jnp.bfloat16)
    v_grad = (factor * (v_in + dot(k, suffix, 1, 0))).astype(jnp.bfloat16)
    fg = jnp.concatenate([q_grad, k_grad, v_grad], axis=1)
    load_u.wait()
    low_grad = dot(fg, u_ref[...], 1, 0).astype(jnp.bfloat16)
    ls_ref[...] = low_grad.astype(jnp.float32)
    low_copy = remote(ls_ref, lr_ref, core_s.at[2], core_r.at[2], mate)
    low_copy.start()
    if sum(early):
        low_across = remote(ls_ref, lo_ref.at[c], pre_s.at[2], pre_r.at[2], across)
        low_across.start()
        low_apart = remote(lo_ref.at[c], lo_ref.at[c], pre_s.at[3], pre_r.at[3], mate)
        extra.append(low_across)
    qo_ref[...] = q_grad
    ko_ref[...] = k_grad
    vo_ref[...] = v_grad

    low_copy.wait_recv()
    both = jnp.concatenate([low_grad, lr_ref[...].astype(jnp.bfloat16)], axis=0)

    outer = (z == 0) | (z == depth - 1)
    inner = jnp.logical_not(outer)
    mid = jnp.where(z < depth // 2, depth // 2 - 1, depth // 2)
    end = jnp.where(z < depth // 2, 0, depth - 1)
    inward, outward, opposite = along(mid), along(end), along(depth - 1 - z)
    further = along(depth - 1 - mid)
    corner = {"seq": end * 2 + (1 - x), "dp": dp}
    cuts = [cut(shard, ushard, core) for core in range(CORES)]
    landings = [landing(pieces) for pieces in cuts]
    last = 1 + max(at for slots in landings for at in slots.values())
    sent = {}
    pieces, slots = [], {}

    def send(role, kind, i, src, dst, where):
        sent[kind] = sent.get(kind, 0) + src.shape[0]
        at = slots.get((reached(role, kind), kind, i), last)
        remote(src, dst, send_s.at[kind], hop_r.at[at], where).start()

    def arrived(role, kind, i, like):
        remote(like, like, send_s.at[kind], hop_r.at[slots[role, kind, i]], mate).wait_recv()

    def partial(i, part):
        off, n = pieces[i][:2]
        if off < base:
            return jnp.dot(xt_ref[part, off : off + n, :], both, preferred_element_type=jnp.float32)
        mine = pl.ds(pl.multiple_of((part * CORES + c) * ushard, 8), ushard)
        return fg_ref[mine, :] + upr_ref[part]

    def half(i, which):
        off, n = pieces[i][:2]
        return pl.ds(pl.multiple_of(off + which * (n // 2), 8), n // 2)

    def short(i):
        off, n = pieces[i][:2]
        return slice(off // 2, off // 2 + n // 2)

    def place(i, which):
        off, n = pieces[i][:2]
        ref, start = (up_ref, 0) if off >= base else (lent_ref, off - shard) if off >= shard else (down_ref, off)
        return ref.at[pl.ds(pl.multiple_of(start + which * (n // 2), 8), n // 2), :]

    def deliver(role, i, which):
        off, n, _, _, moved = pieces[i]
        if moved:
            h = n // 2
            home = down_ref.at[pl.ds(pl.multiple_of(off - room + which * h, 8), h), :]
            sent[D] = sent.get(D, 0) + h
            remote(place(i, which), home, send_s.at[D], hop_r.at[last + 1], mate).start()

    def perform(role, core, op, i):
        off, n, color, mode, moved = pieces[i]
        h = n // 2
        first_x = color in (1, 5, 6)
        workers = working(color)
        whole, low_half, high_half = slice(off, off + n), slice(off, off + h), slice(off + h, off + n)
        small = short(i)
        landed = Y if first_x else X
        if op == "y_send":
            if off >= base:
                up_copy.wait_recv()
            ys_ref[whole, :] = partial(i, 1 - y)
            send(role, Y, i, ys_ref.at[whole, :], yr_ref.at[whole, :], across)
        elif op == "z_first":
            where = inward if role == "outer" else outward
            ys_ref[whole, :] = partial(i, 1 - y)
            send(role, ZL, i, ys_ref.at[whole, :], zl_ref.at[0, whole, :], where)
            acc_ref[whole, :] = partial(i, y)
            send(role, ZL, i, acc_ref.at[whole, :], zl_ref.at[1, whole, :], where)
        elif op == "z_join":
            arrived(role, ZL, i, zl_ref.at[:, whole, :])
            ys_ref[whole, :] = partial(i, 1 - y) + zl_ref[0, whole, :]
            if first_x:
                send(role, X, i, ys_ref.at[half(i, 1 - x), :], yr_ref.at[high_half, :], beside)
                acc_ref[whole, :] = partial(i, y) + zl_ref[1, whole, :]
                send(role, X, i, acc_ref.at[half(i, 1 - x), :], yr_ref.at[low_half, :], beside)
            else:
                send(role, Y, i, ys_ref.at[whole, :], yr_ref.at[whole, :], across)
        elif op == "p_low":
            low_across.wait_recv()
            if early[1 - core]:
                low_apart.start()
        elif op == "p_get":
            remote(ls_ref, ls_ref, pre_s.at[3], pre_r.at[3], mate).wait_recv()
            for at in range(2):
                theirs = pr_ref.at[at, :, 0 : early[core]]
                remote(theirs, theirs, pre_s.at[at], pre_r.at[at], mate).wait_recv()
                pt_ref[0 : early[core], at * rows : (at + 1) * rows] = theirs[...].astype(jnp.bfloat16).T
                them_ref[at * rows : (at + 1) * rows, :] = lo_ref[at].astype(jnp.bfloat16)
        elif op == "p_send":
            acc_ref[whole, :] = partial(i, y) + jnp.dot(
                pt_ref[whole, :], them_ref[...], preferred_element_type=jnp.float32
            )
            send(role, X, i, acc_ref.at[half(i, 1 - x), :], xrs_ref.at[small, :], beside)
        elif op == "x_send":
            own = partial(i, y)
            if color >= 3:
                own = own + zl_ref[1, whole, :]
            arrived(role, Y, i, yr_ref.at[whole, :])
            acc_ref[whole, :] = own + yr_ref[whole, :]
            send(role, X, i, acc_ref.at[half(i, 1 - x), :], xrs_ref.at[small, :], beside)
        elif op == "x_first":
            ys_ref[whole, :] = partial(i, 1 - y)
            send(role, X, i, ys_ref.at[half(i, 1 - x), :], yr_ref.at[high_half, :], beside)
            acc_ref[whole, :] = partial(i, y)
            send(role, X, i, acc_ref.at[half(i, 1 - x), :], yr_ref.at[low_half, :], beside)
        elif op == "y_second":
            arrived(role, X, i, yr_ref.at[whole, :])
            ys_ref[half(i, x), :] += yr_ref[high_half, :]
            send(role, Y, i, ys_ref.at[half(i, x), :], xrs_ref.at[small, :], across)
            acc_ref[half(i, x), :] += yr_ref[low_half, :]
        elif op == "z_in":
            arrived(role, landed, i, xrs_ref.at[small, :])
            zs_ref[small, :] = acc_ref[half(i, x), :] + xrs_ref[small, :]
            send(role, ZI, i, zs_ref.at[small, :], zr_ref.at[small, :], inward)
            if direct(color, mode):
                send(role, ZF, i, zs_ref.at[small, :], zf_ref.at[small, :], further)
        elif op == "z_own":
            arrived(role, landed, i, xrs_ref.at[small, :])
            zs_ref[small, :] = acc_ref[half(i, x), :] + xrs_ref[small, :]
            send(role, ZM, i, zs_ref.at[small, :], zm_ref.at[small, :], opposite)
        elif op == "z_mid":
            if "inner" in workers:
                arrived(role, landed, i, xrs_ref.at[small, :])
                own = acc_ref[half(i, x), :] + xrs_ref[small, :]
            if "outer" in workers:
                arrived(role, ZI, i, zr_ref.at[small, :])
                own = own + zr_ref[small, :] if "inner" in workers else zr_ref[small, :]
            zs_ref[small, :] = own
            send(role, ZM, i, zs_ref.at[small, :], zm_ref.at[small, :], opposite)
        elif op == "z_out":
            own = zs_ref[small, :]
            if direct(color, mode):
                arrived(role, ZI, i, zr_ref.at[small, :])
                own = own + zr_ref[small, :]
            arrived(role, ZM, i, zm_ref.at[small, :])
            own = own + zm_ref[small, :]
            if direct(color, mode):
                arrived(role, ZF, i, zf_ref.at[small, :])
                own = own + zf_ref[small, :]
            spot = place(i, x)
            spot[...] = own * inverse
            if mode == 3:
                send(role, F, i, spot, spot, corner)
            if mode in (0, 1, 3):
                send(role, B, i, spot, spot, beside)
            send(role, ZO, i, spot, spot, outward)
            deliver(role, i, x)
        elif op == "relay":
            spot = place(i, x)
            arrived(role, ZO, i, spot)
            send(role, B, i, spot, spot, beside)
            deliver(role, i, x)
        elif op == "forward":
            spot = place(i, 1 - x)
            arrived(role, B, i, spot)
            send(role, F, i, spot, spot, outward if role == "inner" else inward)
            deliver(role, i, 1 - x)
        elif op == "near":
            arrived(role, ZO, i, place(i, x))
            deliver(role, i, x)
        elif op == "far":
            arrived(role, B if mode == 0 or (mode == 3 and role == "inner") else F, i, place(i, 1 - x))
            deliver(role, i, 1 - x)

    up_all = dot(fg, low, 0, 0)
    fg_ref[...] = up_all
    for part in range(2):
        rng = pl.ds(pl.multiple_of((part * CORES + 1 - c) * ushard, 8), ushard)
        ups_ref[part] = fg_ref[rng, :]
    up_copy = remote(ups_ref, upr_ref, core_s.at[3], core_r.at[3], mate)
    up_copy.start()

    for role, here in (("outer", outer), ("inner", inner)):
        for core in range(CORES):
            @pl.when(here & (c == core))
            def _(role=role, core=core):
                sent.clear()
                slots.clear()
                slots.update(landings[core])
                pieces[:] = cuts[core]
                for code in ORDERS[2 * (role == "inner") + core]:
                    perform(role, core, OPS[code // UNITS], code % UNITS)
                late = 0
                for _, n, _, mode, moved in pieces:
                    if not moved:
                        late += n // 2 * (mode in (1, 3) and role == "outer")
                        late += n // 2 * ((role, mode) not in (("outer", 2), ("inner", 1)))
                for rows_in, at in ((late, last), ((1 - core) * moved_rows, last + 1)):
                    if rows_in:
                        like = ys_ref.at[0:rows_in, :]
                        remote(like, like, send_s.at[0], hop_r.at[at], mate).wait_recv()
                for kind, rows_out in list(sent.items()):
                    like = zl_ref.at[:, 0 : rows_out // 2, :] if kind == ZL else ys_ref.at[0:rows_out, :]
                    remote(like, like, send_s.at[kind], hop_r.at[last], mate).wait_send()
                if early[1 - core]:
                    low_apart.wait_send()
                if room and core == 0:
                    lend.wait_send()

    remote(kvr_ref, kvr_ref, scan_s.at[0], scan_r.at[0], mate).wait_send()
    for copy in core_copies + swaps + [other, low_copy, up_copy] + extra:
        copy.wait_send()


def write_out(*refs):
    copies = [pltpu.make_async_copy(refs[i], refs[5 + i], refs[10].at[i]) for i in range(5)]
    for copy in copies:
        copy.start()
    for copy in copies:
        copy.wait()


def fast(inputs, adapter_down_weight, adapter_up_weight, query, key, value, output_gradient):
    rows, width = query.shape[1:]
    model = inputs.shape[2]
    rank = adapter_down_weight.shape[1]
    features = adapter_up_weight.shape[0]
    seq_count = lax.axis_size("seq")
    dp_count = lax.axis_size("dp")
    length = rows * seq_count
    factor = 1.0 / math.sqrt(HEAD_SIZE * length)
    inverse = 1.0 / math.sqrt(length * dp_count)
    depth = seq_count // 2
    shard, ushard = model // dp_count, features // dp_count
    room = lanes(lent(shard))
    total = shard + room + ushard
    slots = 1 + max(max(landing(cut(shard, ushard, core)).values()) for core in range(CORES))
    early = max([fetched(shard, core) for core in range(CORES)] + [128])
    spare = max(room, 128)
    f32, bf16 = jnp.float32, jnp.bfloat16
    dma = pltpu.SemaphoreType.DMA
    vmem = pl.BlockSpec(memory_space=pltpu.VMEM)
    hbm = pl.BlockSpec(memory_space=pl.ANY)
    shapes = [jax.ShapeDtypeStruct((rows, width), bf16)] * 3 + [
        jax.ShapeDtypeStruct((shard, rank), f32),
        jax.ShapeDtypeStruct((ushard, rank), f32),
    ]
    out = pl.pallas_call(
        functools.partial(fused_kernel, depth, factor, inverse),
        out_shape=[pltpu.VMEM(part.shape, part.dtype) for part in shapes],
        in_specs=[hbm] * 7,
        out_specs=[vmem] * 5,
        scratch_shapes=[
            pltpu.VMEM((rows, model), bf16),
            pltpu.VMEM((model, rank), bf16),
            pltpu.VMEM((features, rank), bf16),
            pltpu.VMEM((4, rows, width), bf16),
            pltpu.VMEM((2, rows, shard), f32),
            pltpu.VMEM((2, rows, shard), f32),
            pltpu.VMEM((2, shard + room, 2 * rows), bf16),
            pltpu.VMEM((2, width, width), f32),
            pltpu.VMEM((2, width, width), f32),
            pltpu.VMEM((depth - 1, width, width), f32),
            pltpu.VMEM((depth - 1, width, width), f32),
            pltpu.VMEM((2, width // 2, width), f32),
            pltpu.VMEM((2, width, width), f32),
            pltpu.VMEM((2, width // 2, width), f32),
            pltpu.VMEM((2, width // 2, width), f32),
            pltpu.VMEM((rows, rank), f32),
            pltpu.VMEM((rows, rank), f32),
            pltpu.VMEM((2, ushard, rank), f32),
            pltpu.VMEM((2, ushard, rank), f32),
            pltpu.VMEM((features, rank), f32),
            pltpu.VMEM((total, rank), f32),
            pltpu.VMEM((total, rank), f32),
            pltpu.VMEM((total, rank), f32),
            pltpu.VMEM((total // 2, rank), f32),
            pltpu.VMEM((total // 2, rank), f32),
            pltpu.VMEM((total // 2, rank), f32),
            pltpu.VMEM((total // 2, rank), f32),
            pltpu.VMEM((total // 2, rank), f32),
            pltpu.VMEM((2, total, rank), f32),
            pltpu.VMEM((2, rows, early), f32),
            pltpu.VMEM((2, rows, early), f32),
            pltpu.VMEM((early, 2 * rows), bf16),
            pltpu.VMEM((2, rows, rank), f32),
            pltpu.VMEM((2 * rows, rank), bf16),
            pltpu.VMEM((2, rows, spare), f32),
            pltpu.VMEM((2, rows, spare), f32),
            pltpu.VMEM((spare, rank), f32),
            dma((5,)), dma((5,)),
            dma((4,)), dma((4,)), dma((4,)),
            dma((1,)), dma((2 * depth - 2,)),
            dma((3,)), dma((3,)),
            dma((KINDS,)), dma((slots + 2,)),
        ],
        compiler_params=pltpu.CompilerParams(
            collective_id=0, has_side_effects=True
        ),
    )(
        inputs.reshape(rows, model), adapter_down_weight, adapter_up_weight,
        query.reshape(rows, width), key.reshape(rows, width),
        value.reshape(rows, width), output_gradient.reshape(rows, width),
    )
    out = pl.pallas_call(
        write_out,
        out_shape=shapes,
        in_specs=[vmem] * 5,
        out_specs=[hbm] * 5,
        scratch_shapes=[dma((5,))],
    )(*[pltpu.with_memory_space_constraint(part, pltpu.VMEM) for part in out])
    return tuple(part.reshape(1, rows, width) for part in out[:3]) + tuple(out[3:])


def solution(mesh):
    fused = fits(mesh.shape["seq"], mesh.shape["dp"])
    chosen = fast if fused else local
    return jax.shard_map(
        chosen,
        mesh=mesh,
        in_specs=(
            P("dp", "seq", None),
            P(),
            P(),
            P("dp", "seq", None),
            P("dp", "seq", None),
            P("dp", "seq", None),
            P("dp", "seq", None),
        ),
        out_specs=(
            P("dp", "seq", None),
            P("dp", "seq", None),
            P("dp", "seq", None),
            P("dp", None),
            P("dp", None),
        ),
        check_vma=False,
    )
```

```python
import functools
import math

import jax
import jax.numpy as jnp
from jax import lax
from jax.experimental import pallas as pl
from jax.experimental.pallas import tpu as pltpu
from jax.sharding import PartitionSpec as P

HEAD_SIZE = 128
LOCAL_HEADS = 1


def entering(part, axis, combine, identity, reverse):
    count = lax.axis_size(axis)
    place = lax.axis_index(axis)
    ahead = count - 1 - place if reverse else place
    gathered = lax.all_gather(part, axis)
    state = jnp.zeros_like(part) + jnp.asarray(identity, part.dtype)

    def one(turn, state):
        source = count - 1 - turn if reverse else turn
        return combine(state, lax.dynamic_index_in_dim(gathered, source, 0, False))

    return lax.fori_loop(0, ahead, one, state)


def add_states(earlier, later):
    return earlier + later


def rounded_values(array):
    return array.astype(jnp.bfloat16)


def local(inputs, adapter_down_weight, adapter_up_weight, query, key, value, output_gradient):
    rows = query.shape[1]
    width = query.shape[2]
    seq_count = lax.axis_size("seq")
    dp_count = lax.axis_size("dp")
    length = rows * seq_count
    factor = 1.0 / math.sqrt(HEAD_SIZE * length)
    queries = query.reshape(rows, LOCAL_HEADS, HEAD_SIZE)
    keys = key.reshape(rows, LOCAL_HEADS, HEAD_SIZE)
    values = value.reshape(rows, LOCAL_HEADS, HEAD_SIZE)
    grads_out = output_gradient.reshape(rows, LOCAL_HEADS, HEAD_SIZE)
    kv_state = jnp.einsum("thi,thj->hij", keys, values, preferred_element_type=jnp.float32)
    qg_state = jnp.einsum("thi,thj->hij", queries, grads_out, preferred_element_type=jnp.float32)
    zeros = jnp.zeros_like(kv_state)
    prefix = entering(kv_state, "seq", add_states, zeros, False)
    suffix = entering(qg_state, "seq", add_states, zeros, True)
    prefix = rounded_values(prefix)
    suffix = rounded_values(suffix)
    rows_idx = lax.broadcasted_iota(jnp.int32, (rows, rows), 0)
    cols_idx = lax.broadcasted_iota(jnp.int32, (rows, rows), 1)
    causal = rows_idx >= cols_idx
    grad_scores = rounded_values(
        jnp.where(
            causal,
            jnp.einsum("thj,shj->hts", grads_out, values, preferred_element_type=jnp.float32),
            0.0,
        )
    )
    scores = rounded_values(
        jnp.where(
            causal,
            jnp.einsum("thi,shi->hts", queries, keys, preferred_element_type=jnp.float32),
            0.0,
        )
    )
    query_grad = jnp.einsum(
        "hts,shi->thi", grad_scores, keys, preferred_element_type=jnp.float32
    ) + jnp.einsum("thj,hij->thi", grads_out, prefix, preferred_element_type=jnp.float32)
    key_grad = jnp.einsum(
        "hts,thi->shi", grad_scores, queries, preferred_element_type=jnp.float32
    ) + jnp.einsum("shj,hij->shi", values, suffix, preferred_element_type=jnp.float32)
    value_grad = jnp.einsum(
        "hts,thj->shj", scores, grads_out, preferred_element_type=jnp.float32
    ) + jnp.einsum("shi,hij->shj", keys, suffix, preferred_element_type=jnp.float32)
    query_grad = rounded_values(factor * query_grad).reshape(rows, width)
    key_grad = rounded_values(factor * key_grad).reshape(rows, width)
    value_grad = rounded_values(factor * value_grad).reshape(rows, width)
    flattened = inputs.reshape(rows, inputs.shape[2])
    gradient_list = jnp.concatenate([query_grad, key_grad, value_grad], axis=1)
    low_rank_state = rounded_values(
        jnp.dot(flattened, adapter_down_weight, preferred_element_type=jnp.float32)
    )
    low_rank_gradient = rounded_values(
        jnp.dot(gradient_list, adapter_up_weight, preferred_element_type=jnp.float32)
    )
    inverse = 1.0 / math.sqrt(length * dp_count)
    contract = (((0,), (0,)), ((), ()))
    down_part = lax.psum_scatter(
        lax.dot_general(flattened, low_rank_gradient, contract, preferred_element_type=jnp.float32)
        * inverse,
        "dp",
        scatter_dimension=0,
        tiled=True,
    )
    up_term = (
        lax.dot_general(gradient_list, low_rank_state, contract, preferred_element_type=jnp.float32)
        * inverse
    )
    up_part = lax.psum_scatter(up_term, "dp", scatter_dimension=0, tiled=True)
    down_grad, up_grad = lax.psum((down_part, up_part), "seq")
    return (
        query_grad.reshape(1, rows, width),
        key_grad.reshape(1, rows, width),
        value_grad.reshape(1, rows, width),
        down_grad,
        up_grad,
    )


MESH = pl.DeviceIdType.MESH
CORES = 2
LINE = 4
KINDS = 10
Y, X, ZI, ZM, ZF, ZO, B, F, ZL, D = range(KINDS)
OPS = (
    "y_send", "x_send", "x_first", "y_second", "z_first", "z_join", "z_in", "z_own", "z_mid",
    "z_out", "relay", "forward", "p_low", "p_get", "p_send", "far", "near",
)
UNITS = 128
CUTS = (
    (
        (3, 3, 0, 0), (7, 5, 2, 0), (5, 4, 1, 0), (4, 0, 3, 0), (2, 0, 2, 0), (3, 0, 2, 0),
        (7, 6, 0, 0), (0, 0, 0, 0), (3, 2, 0, 0), (3, 2, 0, 0), (3, 1, 0, 0), (7, 0, 0, 0),
        (5, 6, 0, 0), (3, 1, 3, 0), (2, 0, 1, 0), (11, 0, 0, 0), (3, 4, 0, 0), (6, 3, 0, 0),
        (3, 0, 0, 0), (12, 2, 0, 0),
    ),
    (
        (10, 6, 0, 1), (14, 6, 1, 0), (6, 4, 1, 0), (2, 2, 2, 0), (3, 6, 1, 0), (9, 2, 2, 0),
        (10, 1, 0, 0), (16, 0, 0, 1), (2, 3, 3, 0), (5, 2, 0, 0), (5, 0, 0, 0), (5, 1, 0, 1),
        (4, 6, 0, 0), (5, 6, 0, 0), (9, 3, 2, 0), (9, 4, 3, 0), (3, 0, 0, 0), (0, 0, 0, 0),
        (3, 2, 2, 0), (2, 5, 0, 0), (2, 0, 2, 0), (15, 1, 2, 0), (4, 2, 2, 0), (5, 5, 2, 1),
        (16, 0, 0, 0),
    ),
)
ORDERS = (
    (
        512, 266, 513, 269, 3, 4, 5, 7, 11, 529, 14, 15, 1536, 394, 397, 642, 1664, 1800, 1801, 1811,
        131, 132, 133, 135, 18, 139, 646, 142, 776, 777, 652, 143, 778, 787, 771, 781, 772, 773, 656, 775,
        130, 779, 146, 390, 782, 396, 144, 783, 770, 786, 774, 780, 784, 1288, 1289, 1290, 1280, 1299, 1281, 1284,
        1285, 1287, 1297, 1291, 1409, 1412, 1413, 1295, 1298, 1286, 1292, 1296,
    ),
    (
        520, 526, 531, 535, 262, 267, 277, 7, 1536, 1664, 1795, 1797, 1801, 1810, 1814, 390, 395, 405, 771, 640,
        773, 10, 135, 777, 786, 16, 790, 17, 774, 779, 20, 24, 641, 789, 384, 138, 144, 642, 145, 148,
        644, 775, 652, 653, 152, 768, 385, 778, 784, 130, 785, 788, 655, 1283, 388, 1285, 396, 1289, 1298, 397,
        1302, 769, 792, 770, 1411, 1286, 143, 1413, 772, 780, 1291, 1426, 1299, 781, 1430, 1294, 783, 1931, 1301, 1303,
        1422, 1287, 1280, 1290, 1296, 1297, 1300, 1429, 1431, 1927, 1920, 1304, 1428, 1292, 1293,
    ),
    (
        514, 266, 269, 3, 4, 518, 5, 7, 11, 14, 15, 524, 1536, 394, 397, 640, 1664, 1800, 1801, 1811,
        131, 132, 133, 528, 18, 135, 641, 139, 142, 657, 143, 909, 899, 128, 146, 385, 1032, 1033, 145, 1034,
        1024, 1043, 1025, 1028, 1029, 1160, 1155, 1161, 1031, 1165, 1041, 1035, 1038, 1162, 1152, 1171, 1153, 1156, 1039, 1157,
        1026, 1042, 1159, 1169, 1030, 1036, 1040, 1163, 1166, 1167, 1154, 1170, 1158, 1164, 1422, 1168, 1410,
    ),
    (
        512, 513, 262, 267, 277, 7, 1536, 648, 1664, 1795, 1797, 1801, 1810, 1814, 390, 395, 514, 405, 516, 654,
        524, 659, 135, 525, 136, 663, 1027, 527, 10, 16, 403, 1029, 17, 20, 1033, 1042, 24, 1046, 1032, 1155,
        142, 1030, 138, 1035, 407, 144, 1043, 1157, 145, 1161, 148, 1170, 1038, 1174, 1160, 1045, 1158, 1163, 152, 1171,
        1047, 1031, 1166, 1024, 1034, 1040, 1931, 1173, 1041, 1044, 1175, 1025, 1159, 1152, 1162, 1048, 1168, 1026, 1169, 1028,
        1172, 1036, 1037, 1927, 1153, 1920, 1039, 1176, 1154, 1156, 1164, 1165, 1167, 1409, 1410, 1412, 1943,
    ),
)


def lanes(n):
    return -(-n // 128) * 128


def lent(shard):
    return shard // UNITS * sum(parts for parts, _, _, moved in CUTS[1] if moved)


def fetched(shard, core):
    return lanes(shard // UNITS * sum(parts for parts, color, _, _ in CUTS[core] if color == 2))


def cut(shard, ushard, core):
    table, unit, room = CUTS[core], shard // UNITS, lanes(lent(shard))
    places, off = {}, 0
    for i in sorted(range(len(table)), key=lambda i: (table[i][3], table[i][1] != 2)):
        if table[i][3] and off < shard + room - lent(shard):
            off = shard + room - lent(shard)
        places[i] = off
        off += table[i][0] * unit
    return [
        (places[i], parts * unit, color, mode, moved) if parts else (shard + room, ushard, color, mode, moved)
        for i, (parts, color, mode, moved) in enumerate(table)
    ]


def working(color):
    return {3: ("inner",), 5: ("inner",), 4: ("outer",), 6: ("outer",)}.get(color, ("outer", "inner"))


def direct(color, mode):
    return mode == 3 and color < 3


def waits(role, color, mode, moved):
    work = role in working(color)
    kinds = [Y] * (work and color != 2) + [X] * work + [ZL] * (work and color >= 3)
    if role == "inner":
        kinds += [ZM] + [ZI] * ("outer" in working(color)) + [ZF] * direct(color, mode)
        kinds += [B] * (mode == 1 or (moved and mode in (0, 3))) + [F] * (moved and mode == 2)
    else:
        kinds += [ZO] * (mode in (0, 2) or moved)
        kinds += [B] * (mode == 2 or (moved and mode == 0)) + [F] * (moved and mode in (1, 3))
    return kinds


def landing(pieces):
    slots = {}
    for role in ("outer", "inner"):
        spots = [
            (role, kind, i)
            for i, (_, _, color, mode, moved) in enumerate(pieces)
            for kind in waits(role, color, mode, moved)
        ]
        slots.update((spot, at) for at, spot in enumerate(spots))
    return slots


def reached(role, kind):
    if kind in (ZI, ZF):
        return "inner"
    if kind == ZO:
        return "outer"
    if kind in (F, ZL):
        return "outer" if role == "inner" else "inner"
    return role


def fits(seq_count, dp_count):
    return dp_count == 2 * CORES and seq_count == 2 * LINE


def dot(a, b, da, db):
    return lax.dot_general(a, b, (((da,), (db,)), ((), ())), preferred_element_type=jnp.float32)


def fused_kernel(
    depth, factor, inverse,
    x_hbm, w_hbm, u_hbm, q_hbm, k_hbm, v_hbm, g_hbm,
    qo_ref, ko_ref, vo_ref, down_ref, up_ref,
    x_ref, w_ref, u_ref, four_ref, xs_ref, xr_ref, xt_ref,
    st_ref, pair_ref, kvr_ref, qgr_ref, ox_ref, sxs_ref, sxr_ref, lead_ref,
    ls_ref, lr_ref, ups_ref, upr_ref, fg_ref,
    ys_ref, yr_ref, acc_ref, xrs_ref, zs_ref, zr_ref, zm_ref, zf_ref, zl_ref,
    ps_ref, pr_ref, pt_ref, lo_ref, them_ref, xes_ref, xer_ref, lent_ref, pre_s, pre_r,
    load_sem, core_s, core_r, scan_s, scan_r, sx_s, sx_r,
    send_s, hop_r,
):
    seq = lax.axis_index("seq")
    dp = lax.axis_index("dp")
    z, x = seq // 2, seq % 2
    y, c = dp // CORES, dp % CORES
    mate = {"seq": seq, "dp": y * CORES + (1 - c)}
    across = {"seq": seq, "dp": (1 - y) * CORES + c}
    apart = {"seq": seq, "dp": (1 - y) * CORES + (1 - c)}
    beside = {"seq": z * 2 + (1 - x), "dp": dp}

    near = jnp.where(z % 3 == 0, z + 1 - 2 * (z // 3), 3 * (z // 2))
    diagonal = {"seq": near * 2 + (1 - x), "dp": dp}

    def along(other):
        return {"seq": other * 2 + x, "dp": dp}

    for i, part in enumerate((q_hbm, k_hbm, v_hbm, g_hbm)):
        pltpu.make_async_copy(part, four_ref.at[i], load_sem.at[2]).start()
    load_u = pltpu.make_async_copy(u_hbm, u_ref, load_sem.at[3])
    load_x = pltpu.make_async_copy(x_hbm, x_ref, load_sem.at[0])
    load_w = pltpu.make_async_copy(w_hbm, w_ref, load_sem.at[1])
    load_u.start()
    load_x.start()
    load_w.start()

    barrier = pltpu.get_barrier_semaphore()
    friends = [mate, across, apart, beside, diagonal] + [along(lax.rem(z + d, depth)) for d in range(1, depth)]
    for friend in friends:
        pl.semaphore_signal(barrier, inc=1, device_id=friend, device_id_type=MESH)

    rows, width = qo_ref.shape
    shard = down_ref.shape[0]
    ushard = up_ref.shape[0]
    early = [fetched(shard, core) for core in range(CORES)]
    moved_rows = lent(shard)
    room = lanes(moved_rows)
    base = shard + room
    pltpu.make_async_copy(four_ref, four_ref, load_sem.at[2]).wait()
    q, k, v, g = four_ref[0], four_ref[1], four_ref[2], four_ref[3]
    st_ref[0] = dot(k, v, 0, 0)
    st_ref[1] = dot(q, g, 0, 0)
    pl.semaphore_wait(barrier, len(friends))

    def remote(src, dst, ssem, rsem, where):
        return pltpu.make_async_remote_copy(
            src_ref=src, dst_ref=dst, send_sem=ssem, recv_sem=rsem, device_id=where, device_id_type=MESH
        )

    lead = width // 2
    first, second = slice(0, lead), slice(lead, width)
    other = remote(st_ref.at[:, second, :], ox_ref, sx_s.at[1], sx_r.at[1], beside)

    def scan(source, part, at):
        ups, downs = [], []
        for d in range(1, depth):
            slot = at * (depth - 1) + d - 1
            back = at * (depth - 1) + depth - d - 1
            ups.append(remote(source.at[0, part, :], kvr_ref.at[d - 1, part, :], scan_s.at[0], scan_r.at[slot], along(lax.rem(z + d, depth))))
            downs.append(remote(source.at[1, part, :], qgr_ref.at[d - 1, part, :], scan_s.at[0], scan_r.at[back], along(lax.rem(z - d + depth, depth))))
        return ups, downs

    def launch(scans):
        for d in reversed(range(1, depth)):
            pl.when(z + d < depth)(scans[0][d - 1].start)
            pl.when(z >= d)(scans[1][d - 1].start)

    def collect(scans, part, which):
        sxs_ref[which, part, :] = jnp.zeros((lead, width), jnp.float32)
        for d in range(1, depth):
            @pl.when(z + d < depth if which else z >= d)
            def _(d=d):
                scans[which][d - 1].wait_recv()
                sxs_ref[which, part, :] += (kvr_ref, qgr_ref)[which][d - 1, part, :]

    scan_a = scan(st_ref, first, 0)

    def begin():
        other.start()
        launch(scan_a)

    pl.when(c == 0)(begin)
    load_x.wait()
    core_copies, extra = [], []
    for core in range(CORES):
        if early[core]:
            cols = pl.ds(pl.multiple_of(((1 - y) * CORES + core) * shard, 128), early[core])
            mine = ps_ref.at[core, :, 0 : early[core]]
            mine[...] = x_ref[:, cols].astype(jnp.float32)
            where = {"seq": seq, "dp": (1 - y) * CORES + core}
            copy = remote(mine, pr_ref.at[c, :, 0 : early[core]], pre_s.at[core], pre_r.at[c], where)
            copy.start()
            extra.append(copy)
    if room:
        for part in range(2):
            xes_ref[part] = x_ref[:, (part * CORES + 1) * shard - room : (part * CORES + 1) * shard].astype(jnp.float32)
        lend = remote(xes_ref, xer_ref, pre_s.at[4], pre_r.at[4], mate)
        pl.when(c == 0)(lend.start)
    for part in range(2):
        cols = pl.ds(pl.multiple_of((part * CORES + 1 - c) * shard, 128), shard)
        xs_ref[part] = x_ref[:, cols].astype(jnp.float32)
        copy = remote(xs_ref.at[part], xr_ref.at[part], core_s.at[part], core_r.at[part], mate)
        copy.start()
        core_copies.append(copy)

    r_idx = lax.broadcasted_iota(jnp.int32, (rows, rows), 0)
    c_idx = lax.broadcasted_iota(jnp.int32, (rows, rows), 1)
    causal = r_idx >= c_idx
    gs = jnp.where(causal, dot(g, v, 1, 1), 0.0).astype(jnp.bfloat16)
    sc = jnp.where(causal, dot(q, k, 1, 1), 0.0).astype(jnp.bfloat16)
    q_in = dot(gs, k, 1, 0)
    k_in = dot(gs, q, 0, 0)
    v_in = dot(sc, g, 0, 0)

    for part in range(2):
        cols = pl.ds(pl.multiple_of((part * CORES + c) * shard, 128), shard)
        xt_ref[part, 0:shard, 0:rows] = x_ref[:, cols].T

    pl.when(c == 1)(begin)
    load_w.wait()
    low = jnp.dot(x_ref[...], w_ref[...], preferred_element_type=jnp.float32).astype(jnp.bfloat16)

    other.wait_recv()
    pair_ref[:, second, :] = st_ref[:, second, :] + ox_ref[...]
    scan_b = scan(pair_ref, second, 1)
    launch(scan_b)

    swaps = [
        remote(sxs_ref.at[which, first, :], sxr_ref.at[which], sx_s.at[2 * which], sx_r.at[2 * which], beside)
        for which in range(2)
    ]

    def settle(which):
        collect(scan_a, first, which)
        lead_ref[which] = sxs_ref[which, first, :]

        @pl.when(x == which)
        def _():
            sxs_ref[which, first, :] += st_ref[which, first, :]

        swaps[which].start()

    for here, turns in ((z < depth // 2, (0, 1)), (z >= depth // 2, (1, 0))):
        @pl.when(here)
        def _(turns=turns):
            for which in turns:
                settle(which)

    for part in range(2):
        core_copies[part].wait_recv()
        xt_ref[part, 0:shard, rows:] = xr_ref[part].astype(jnp.bfloat16).T

    if room:
        @pl.when(c == 1)
        def _():
            lend.wait_recv()
            for part in range(2):
                xt_ref[part, shard:base, 0:rows] = x_ref[:, (part * CORES + 1) * shard - room : (part * CORES + 1) * shard].T
                xt_ref[part, shard:base, rows:] = xer_ref[part].astype(jnp.bfloat16).T

    for which in range(2):
        collect(scan_b, second, which)

    @pl.when(x == 1)
    def _():
        sxs_ref[0, second, :] += ox_ref[0]

    @pl.when(x == 0)
    def _():
        sxs_ref[1, second, :] += ox_ref[1]

    for swap in swaps:
        swap.wait_recv()
    states = jnp.concatenate([lead_ref[...] + sxr_ref[...], sxs_ref[:, second, :]], axis=1).astype(jnp.bfloat16)
    prefix, suffix = states[0], states[1]
    q_grad = (factor * (q_in + dot(g, prefix, 1, 1))).astype(jnp.bfloat16)
    k_grad = (factor * (k_in + dot(v, suffix, 1, 1))).astype(jnp.bfloat16)
    v_grad = (factor * (v_in + dot(k, suffix, 1, 0))).astype(jnp.bfloat16)
    fg = jnp.concatenate([q_grad, k_grad, v_grad], axis=1)
    load_u.wait()
    low_grad = dot(fg, u_ref[...], 1, 0).astype(jnp.bfloat16)
    ls_ref[...] = low_grad.astype(jnp.float32)
    low_copy = remote(ls_ref, lr_ref, core_s.at[2], core_r.at[2], mate)
    low_copy.start()
    if sum(early):
        low_across = remote(ls_ref, lo_ref.at[c], pre_s.at[2], pre_r.at[2], across)
        low_across.start()
        low_apart = remote(lo_ref.at[c], lo_ref.at[c], pre_s.at[3], pre_r.at[3], mate)
        extra.append(low_across)
    qo_ref[...] = q_grad
    ko_ref[...] = k_grad
    vo_ref[...] = v_grad

    low_copy.wait_recv()
    both = jnp.concatenate([low_grad, lr_ref[...].astype(jnp.bfloat16)], axis=0)

    outer = (z == 0) | (z == depth - 1)
    inner = jnp.logical_not(outer)
    mid = jnp.where(z < depth // 2, depth // 2 - 1, depth // 2)
    end = jnp.where(z < depth // 2, 0, depth - 1)
    inward, outward, opposite = along(mid), along(end), along(depth - 1 - z)
    further = along(depth - 1 - mid)
    corner = {"seq": end * 2 + (1 - x), "dp": dp}
    cuts = [cut(shard, ushard, core) for core in range(CORES)]
    landings = [landing(pieces) for pieces in cuts]
    last = 1 + max(at for slots in landings for at in slots.values())
    sent = {}
    pieces, slots = [], {}

    def send(role, kind, i, src, dst, where):
        sent[kind] = sent.get(kind, 0) + src.shape[0]
        at = slots.get((reached(role, kind), kind, i), last)
        remote(src, dst, send_s.at[kind], hop_r.at[at], where).start()

    def arrived(role, kind, i, like):
        remote(like, like, send_s.at[kind], hop_r.at[slots[role, kind, i]], mate).wait_recv()

    def partial(i, part):
        off, n = pieces[i][:2]
        if off < base:
            return jnp.dot(xt_ref[part, off : off + n, :], both, preferred_element_type=jnp.float32)
        mine = pl.ds(pl.multiple_of((part * CORES + c) * ushard, 8), ushard)
        return fg_ref[mine, :] + upr_ref[part]

    def half(i, which):
        off, n = pieces[i][:2]
        return pl.ds(pl.multiple_of(off + which * (n // 2), 8), n // 2)

    def short(i):
        off, n = pieces[i][:2]
        return slice(off // 2, off // 2 + n // 2)

    def place(i, which):
        off, n = pieces[i][:2]
        ref, start = (up_ref, 0) if off >= base else (lent_ref, off - shard) if off >= shard else (down_ref, off)
        return ref.at[pl.ds(pl.multiple_of(start + which * (n // 2), 8), n // 2), :]

    def deliver(role, i, which):
        off, n, _, _, moved = pieces[i]
        if moved:
            h = n // 2
            home = down_ref.at[pl.ds(pl.multiple_of(off - room + which * h, 8), h), :]
            sent[D] = sent.get(D, 0) + h
            remote(place(i, which), home, send_s.at[D], hop_r.at[last + 1], mate).start()

    def perform(role, core, op, i):
        off, n, color, mode, moved = pieces[i]
        h = n // 2
        first_x = color in (1, 5, 6)
        workers = working(color)
        whole, low_half, high_half = slice(off, off + n), slice(off, off + h), slice(off + h, off + n)
        small = short(i)
        landed = Y if first_x else X
        if op == "y_send":
            if off >= base:
                up_copy.wait_recv()
            ys_ref[whole, :] = partial(i, 1 - y)
            send(role, Y, i, ys_ref.at[whole, :], yr_ref.at[whole, :], across)
        elif op == "z_first":
            where = inward if role == "outer" else outward
            ys_ref[whole, :] = partial(i, 1 - y)
            send(role, ZL, i, ys_ref.at[whole, :], zl_ref.at[0, whole, :], where)
            acc_ref[whole, :] = partial(i, y)
            send(role, ZL, i, acc_ref.at[whole, :], zl_ref.at[1, whole, :], where)
        elif op == "z_join":
            arrived(role, ZL, i, zl_ref.at[:, whole, :])
            ys_ref[whole, :] = partial(i, 1 - y) + zl_ref[0, whole, :]
            if first_x:
                send(role, X, i, ys_ref.at[half(i, 1 - x), :], yr_ref.at[high_half, :], beside)
                acc_ref[whole, :] = partial(i, y) + zl_ref[1, whole, :]
                send(role, X, i, acc_ref.at[half(i, 1 - x), :], yr_ref.at[low_half, :], beside)
            else:
                send(role, Y, i, ys_ref.at[whole, :], yr_ref.at[whole, :], across)
        elif op == "p_low":
            low_across.wait_recv()
            if early[1 - core]:
                low_apart.start()
        elif op == "p_get":
            remote(ls_ref, ls_ref, pre_s.at[3], pre_r.at[3], mate).wait_recv()
            for at in range(2):
                theirs = pr_ref.at[at, :, 0 : early[core]]
                remote(theirs, theirs, pre_s.at[at], pre_r.at[at], mate).wait_recv()
                pt_ref[0 : early[core], at * rows : (at + 1) * rows] = theirs[...].astype(jnp.bfloat16).T
                them_ref[at * rows : (at + 1) * rows, :] = lo_ref[at].astype(jnp.bfloat16)
        elif op == "p_send":
            acc_ref[whole, :] = partial(i, y) + jnp.dot(
                pt_ref[whole, :], them_ref[...], preferred_element_type=jnp.float32
            )
            send(role, X, i, acc_ref.at[half(i, 1 - x), :], xrs_ref.at[small, :], beside)
        elif op == "x_send":
            own = partial(i, y)
            if color >= 3:
                own = own + zl_ref[1, whole, :]
            arrived(role, Y, i, yr_ref.at[whole, :])
            acc_ref[whole, :] = own + yr_ref[whole, :]
            send(role, X, i, acc_ref.at[half(i, 1 - x), :], xrs_ref.at[small, :], beside)
        elif op == "x_first":
            ys_ref[whole, :] = partial(i, 1 - y)
            send(role, X, i, ys_ref.at[half(i, 1 - x), :], yr_ref.at[high_half, :], beside)
            acc_ref[whole, :] = partial(i, y)
            send(role, X, i, acc_ref.at[half(i, 1 - x), :], yr_ref.at[low_half, :], beside)
        elif op == "y_second":
            arrived(role, X, i, yr_ref.at[whole, :])
            ys_ref[half(i, x), :] += yr_ref[high_half, :]
            send(role, Y, i, ys_ref.at[half(i, x), :], xrs_ref.at[small, :], across)
            acc_ref[half(i, x), :] += yr_ref[low_half, :]
        elif op == "z_in":
            arrived(role, landed, i, xrs_ref.at[small, :])
            zs_ref[small, :] = acc_ref[half(i, x), :] + xrs_ref[small, :]
            send(role, ZI, i, zs_ref.at[small, :], zr_ref.at[small, :], inward)
            if direct(color, mode):
                send(role, ZF, i, zs_ref.at[small, :], zf_ref.at[small, :], further)
        elif op == "z_own":
            arrived(role, landed, i, xrs_ref.at[small, :])
            zs_ref[small, :] = acc_ref[half(i, x), :] + xrs_ref[small, :]
            send(role, ZM, i, zs_ref.at[small, :], zm_ref.at[small, :], opposite)
        elif op == "z_mid":
            if "inner" in workers:
                arrived(role, landed, i, xrs_ref.at[small, :])
                own = acc_ref[half(i, x), :] + xrs_ref[small, :]
            if "outer" in workers:
                arrived(role, ZI, i, zr_ref.at[small, :])
                own = own + zr_ref[small, :] if "inner" in workers else zr_ref[small, :]
            zs_ref[small, :] = own
            send(role, ZM, i, zs_ref.at[small, :], zm_ref.at[small, :], opposite)
        elif op == "z_out":
            own = zs_ref[small, :]
            if direct(color, mode):
                arrived(role, ZI, i, zr_ref.at[small, :])
                own = own + zr_ref[small, :]
            arrived(role, ZM, i, zm_ref.at[small, :])
            own = own + zm_ref[small, :]
            if direct(color, mode):
                arrived(role, ZF, i, zf_ref.at[small, :])
                own = own + zf_ref[small, :]
            spot = place(i, x)
            spot[...] = own * inverse
            if mode == 3:
                send(role, F, i, spot, spot, corner)
            if mode in (0, 1, 3):
                send(role, B, i, spot, spot, beside)
            send(role, ZO, i, spot, spot, outward)
            deliver(role, i, x)
        elif op == "relay":
            spot = place(i, x)
            arrived(role, ZO, i, spot)
            send(role, B, i, spot, spot, beside)
            deliver(role, i, x)
        elif op == "forward":
            spot = place(i, 1 - x)
            arrived(role, B, i, spot)
            send(role, F, i, spot, spot, outward if role == "inner" else inward)
            deliver(role, i, 1 - x)
        elif op == "near":
            arrived(role, ZO, i, place(i, x))
            deliver(role, i, x)
        elif op == "far":
            arrived(role, B if mode == 0 or (mode == 3 and role == "inner") else F, i, place(i, 1 - x))
            deliver(role, i, 1 - x)

    up_all = dot(fg, low, 0, 0)
    fg_ref[...] = up_all
    for part in range(2):
        rng = pl.ds(pl.multiple_of((part * CORES + 1 - c) * ushard, 8), ushard)
        ups_ref[part] = fg_ref[rng, :]
    up_copy = remote(ups_ref, upr_ref, core_s.at[3], core_r.at[3], mate)
    up_copy.start()

    for role, here in (("outer", outer), ("inner", inner)):
        for core in range(CORES):
            @pl.when(here & (c == core))
            def _(role=role, core=core):
                sent.clear()
                slots.clear()
                slots.update(landings[core])
                pieces[:] = cuts[core]
                for code in ORDERS[2 * (role == "inner") + core]:
                    perform(role, core, OPS[code // UNITS], code % UNITS)
                late = 0
                for _, n, _, mode, moved in pieces:
                    if not moved:
                        late += n // 2 * (mode in (1, 3) and role == "outer")
                        late += n // 2 * ((role, mode) not in (("outer", 2), ("inner", 1)))
                for rows_in, at in ((late, last), ((1 - core) * moved_rows, last + 1)):
                    if rows_in:
                        like = ys_ref.at[0:rows_in, :]
                        remote(like, like, send_s.at[0], hop_r.at[at], mate).wait_recv()
                for kind, rows_out in list(sent.items()):
                    like = zl_ref.at[:, 0 : rows_out // 2, :] if kind == ZL else ys_ref.at[0:rows_out, :]
                    remote(like, like, send_s.at[kind], hop_r.at[last], mate).wait_send()
                if early[1 - core]:
                    low_apart.wait_send()
                if room and core == 0:
                    lend.wait_send()

    remote(kvr_ref, kvr_ref, scan_s.at[0], scan_r.at[0], mate).wait_send()
    for copy in core_copies + swaps + [other, low_copy, up_copy] + extra:
        copy.wait_send()


def write_out(*refs):
    copies = [pltpu.make_async_copy(refs[i], refs[5 + i], refs[10].at[i]) for i in range(5)]
    for copy in copies:
        copy.start()
    for copy in copies:
        copy.wait()


def fast(inputs, adapter_down_weight, adapter_up_weight, query, key, value, output_gradient):
    rows, width = query.shape[1:]
    model = inputs.shape[2]
    rank = adapter_down_weight.shape[1]
    features = adapter_up_weight.shape[0]
    seq_count = lax.axis_size("seq")
    dp_count = lax.axis_size("dp")
    length = rows * seq_count
    factor = 1.0 / math.sqrt(HEAD_SIZE * length)
    inverse = 1.0 / math.sqrt(length * dp_count)
    depth = seq_count // 2
    shard, ushard = model // dp_count, features // dp_count
    room = lanes(lent(shard))
    total = shard + room + ushard
    slots = 1 + max(max(landing(cut(shard, ushard, core)).values()) for core in range(CORES))
    early = max([fetched(shard, core) for core in range(CORES)] + [128])
    spare = max(room, 128)
    f32, bf16 = jnp.float32, jnp.bfloat16
    dma = pltpu.SemaphoreType.DMA
    vmem = pl.BlockSpec(memory_space=pltpu.VMEM)
    hbm = pl.BlockSpec(memory_space=pl.ANY)
    shapes = [jax.ShapeDtypeStruct((rows, width), bf16)] * 3 + [
        jax.ShapeDtypeStruct((shard, rank), f32),
        jax.ShapeDtypeStruct((ushard, rank), f32),
    ]
    out = pl.pallas_call(
        functools.partial(fused_kernel, depth, factor, inverse),
        out_shape=[pltpu.VMEM(part.shape, part.dtype) for part in shapes],
        in_specs=[hbm] * 7,
        out_specs=[vmem] * 5,
        scratch_shapes=[
            pltpu.VMEM((rows, model), bf16),
            pltpu.VMEM((model, rank), bf16),
            pltpu.VMEM((features, rank), bf16),
            pltpu.VMEM((4, rows, width), bf16),
            pltpu.VMEM((2, rows, shard), f32),
            pltpu.VMEM((2, rows, shard), f32),
            pltpu.VMEM((2, shard + room, 2 * rows), bf16),
            pltpu.VMEM((2, width, width), f32),
            pltpu.VMEM((2, width, width), f32),
            pltpu.VMEM((depth - 1, width, width), f32),
            pltpu.VMEM((depth - 1, width, width), f32),
            pltpu.VMEM((2, width // 2, width), f32),
            pltpu.VMEM((2, width, width), f32),
            pltpu.VMEM((2, width // 2, width), f32),
            pltpu.VMEM((2, width // 2, width), f32),
            pltpu.VMEM((rows, rank), f32),
            pltpu.VMEM((rows, rank), f32),
            pltpu.VMEM((2, ushard, rank), f32),
            pltpu.VMEM((2, ushard, rank), f32),
            pltpu.VMEM((features, rank), f32),
            pltpu.VMEM((total, rank), f32),
            pltpu.VMEM((total, rank), f32),
            pltpu.VMEM((total, rank), f32),
            pltpu.VMEM((total // 2, rank), f32),
            pltpu.VMEM((total // 2, rank), f32),
            pltpu.VMEM((total // 2, rank), f32),
            pltpu.VMEM((total // 2, rank), f32),
            pltpu.VMEM((total // 2, rank), f32),
            pltpu.VMEM((2, total, rank), f32),
            pltpu.VMEM((2, rows, early), f32),
            pltpu.VMEM((2, rows, early), f32),
            pltpu.VMEM((early, 2 * rows), bf16),
            pltpu.VMEM((2, rows, rank), f32),
            pltpu.VMEM((2 * rows, rank), bf16),
            pltpu.VMEM((2, rows, spare), f32),
            pltpu.VMEM((2, rows, spare), f32),
            pltpu.VMEM((spare, rank), f32),
            dma((5,)), dma((5,)),
            dma((4,)), dma((4,)), dma((4,)),
            dma((1,)), dma((2 * depth - 2,)),
            dma((3,)), dma((3,)),
            dma((KINDS,)), dma((slots + 2,)),
        ],
        compiler_params=pltpu.CompilerParams(
            collective_id=0, has_side_effects=True
        ),
    )(
        inputs.reshape(rows, model), adapter_down_weight, adapter_up_weight,
        query.reshape(rows, width), key.reshape(rows, width),
        value.reshape(rows, width), output_gradient.reshape(rows, width),
    )
    out = pl.pallas_call(
        write_out,
        out_shape=shapes,
        in_specs=[vmem] * 5,
        out_specs=[hbm] * 5,
        scratch_shapes=[dma((5,))],
    )(*[pltpu.with_memory_space_constraint(part, pltpu.VMEM) for part in out])
    return tuple(part.reshape(1, rows, width) for part in out[:3]) + tuple(out[3:])


def solution(mesh):
    fused = fits(mesh.shape["seq"], mesh.shape["dp"])
    chosen = fast if fused else local
    return jax.shard_map(
        chosen,
        mesh=mesh,
        in_specs=(
            P("dp", "seq", None),
            P(),
            P(),
            P("dp", "seq", None),
            P("dp", "seq", None),
            P("dp", "seq", None),
            P("dp", "seq", None),
        ),
        out_specs=(
            P("dp", "seq", None),
            P("dp", "seq", None),
            P("dp", "seq", None),
            P("dp", None),
            P("dp", None),
        ),
        check_vma=False,
    )
```
